512 devices in a mesh: rows: 32 (over y, x, core), cov: 16 (over z).
Axes of the slice: x: 4, y: 4, z: 16, core: 2. Of those that a mesh axis runs over, the one named last changes fastest.
Arguments:
- design: bfloat16 [256, 16384, 128], P('cov', 'rows'), may hold values from -6 to 6
- outcome: int32 [16384, 128], P('rows'), may hold values from 0 to 1
- block_fill: int32 [16384], P('rows'), may hold values from 1 to 128
- block_group: int32 [16384], P('rows'), may hold values from 0 to 8191, as said below
- fixed_coef: float32 [256], P('cov'), may hold values from -0.375 to 0.375
- slopes: float32 [256, 8192], P('cov', 'rows'), may hold values from -0.375 to 0.375
- precision: float32 [256, 256], P('cov'), as said below
Outputs:
- fixed_grad: float32 [256], P('cov')
- slope_grad: float32 [256, 8192], P('cov', 'rows')
The draws below stay inside these ranges and needn't reach their ends.
Inputs may be any that keep to these rules, and one draw needn't show every extreme that they name: block_group names every group and rises along the blocks of each index of rows; group g is owned by index g // 256 of rows; the blocks of rows index d belong to groups owned by d - 1, d or d + 1; every index but the first holds blocks of groups owned by the index below, and every index but the last blocks of groups owned by the index above. `precision`: symmetric.
All inputs are finite; a program needn't handle non-finite values.
Results may differ from the reference program's by a relative error of at most 0.0003.
Values sent between devices are 32-bit elements; how exact they have to be, the bound alone decides.
No kernel may reach another device: no remote copies, remote signals or barrier semaphores. Data moves between devices by JAX's collectives and lax.ppermute only.
A program may use at most 64 MiB of HBM per device.

```python
import jax
import jax.numpy as jnp
from jax import lax

P_SIZE = 256
BLK = 128
NB_DEV = 512
G_DEV = 256
NB = 16384
GROUPS = 8192
N_ROWS = 32


def draw_block_group(key, part):
    row_devices = NB // NB_DEV
    edge_most = NB_DEV // 4
    key_one, key_two, key_three, key_four, key_five = jax.random.split(key, 5)
    lower_count = jax.random.randint(key_one, (row_devices,), 1, edge_most + 1)
    upper_count = jax.random.randint(key_two, (row_devices,), 1, edge_most + 1)
    device_ids = jnp.arange(row_devices, dtype=jnp.int32)
    lower_count = jnp.where(device_ids > 0, lower_count, 0)
    upper_count = jnp.where(device_ids < row_devices - 1, upper_count, 0)
    block_ids = jnp.arange(NB, dtype=jnp.int32)
    owners = block_ids // NB_DEV
    local = block_ids % NB_DEV
    lower_here = lower_count[owners]
    upper_here = upper_count[owners]
    neighbour_pick = jax.random.randint(key_three, (NB,), 0, G_DEV)
    first_pick = jax.random.randint(key_four, (NB,), 0, G_DEV)
    second_pick = jax.random.randint(key_five, (NB,), 0, G_DEV)
    extras = first_pick * second_pick // G_DEV
    own_offset = local - lower_here
    own_label = jnp.where(own_offset < G_DEV, own_offset, extras) + owners * G_DEV
    lower_label = (owners - 1) * G_DEV + neighbour_pick
    upper_label = (owners + 1) * G_DEV + neighbour_pick
    labels = jnp.where(local < lower_here, lower_label, jnp.where(local >= NB_DEV - upper_here, upper_label, own_label))
    labels = jnp.sort(labels.reshape(row_devices, NB_DEV), axis=1).reshape(NB)
    return labels.astype(jnp.int32)


def draw_precision(key, part):
    key_one, key_two = jax.random.split(key)
    noise = 0.7 * jax.random.normal(key_one, (P_SIZE, P_SIZE), jnp.float32)
    symmetric = 0.5 * (noise + noise.T)
    diagonal = jnp.exp(jax.random.uniform(key_two, (P_SIZE,), jnp.float32, jnp.log(4.0), jnp.log(32.0)))
    identity = jnp.eye(P_SIZE, dtype=jnp.float32)
    return (symmetric * (1.0 - identity) + identity * diagonal[None, :]).astype(jnp.float32)


def plant(result, own_key, low, top_value):
    longest = result.shape.index(max(result.shape))
    spots = []
    for shift in (0, 1):
        where = [jax.random.randint(jax.random.fold_in(own_key, axis), (), 0, length) for axis, length in enumerate(result.shape)]
        where[longest] = (where[longest] + shift) % result.shape[longest]
        spots.append(tuple(where))
    return result.at[spots[0]].set(low).at[spots[1]].set(top_value)


def level_of(key, dims, cuts, least, largest):
    def one(dim, parts):
        heights = jax.random.uniform(jax.random.fold_in(jax.random.fold_in(key, 6), dim), (parts,), jnp.float32, least / len(cuts), largest / len(cuts))
        return jnp.repeat(jnp.exp(heights), dims[dim] // parts).reshape((-1,) + (1,) * (len(dims) - dim - 1))

    level = one(*cuts[0])
    for cut in cuts[1:]:
        level = level * one(*cut)
    return level


def bell_draw(key, dims, width, most, cuts=(), kind=jnp.bfloat16):
    result = jax.random.normal(key, dims, jnp.float32) * width
    if len(cuts) > 0:
        result = level_of(key, dims, cuts, -0.22, 0.18) * result
    return jnp.clip(result, min=-most, max=most).astype(kind)


def setup_inputs(seed: int = 0) -> dict:
    arg_keys = jax.random.split(jax.random.key(seed), 8)
    design = bell_draw(arg_keys[0], (P_SIZE, NB, BLK), 1.0, 6.0, ((0, 16), (1, 32)))
    outcome = plant(jax.random.randint(arg_keys[1], (NB, BLK), 0, 2), jax.random.fold_in(arg_keys[1], 1), 0, 1).astype(jnp.int32)
    block_fill = plant(jax.random.randint(arg_keys[2], (NB,), 1, BLK + 1), jax.random.fold_in(arg_keys[2], 1), 1, BLK).astype(jnp.int32)
    block_group = draw_block_group(jax.random.fold_in(arg_keys[7], 71), 0)
    fixed_coef = bell_draw(arg_keys[4], (P_SIZE,), P_SIZE ** -0.5, 0.375, ((0, 16),), jnp.float32)
    slopes = bell_draw(arg_keys[5], (P_SIZE, GROUPS), P_SIZE ** -0.5, 0.375, ((0, 16), (1, 32)), jnp.float32)
    precision = draw_precision(jax.random.fold_in(arg_keys[7], 71), 0)
    return dict(design=design, outcome=outcome, block_fill=block_fill, block_group=block_group, fixed_coef=fixed_coef, slopes=slopes, precision=precision)


def reference(design, outcome, block_fill, block_group, fixed_coef, slopes, precision):
    combined = fixed_coef[:, None] + jnp.take(slopes, block_group, axis=1)

    def per_device(shard_index):
        start = (shard_index * NB_DEV).astype(jnp.int32)
        values = lax.dynamic_slice_in_dim(design, start, NB_DEV, 1).astype(jnp.float32)
        weights = lax.dynamic_slice_in_dim(combined, start, NB_DEV, 1)
        logits = jnp.einsum('pnb,pn->nb', values, weights, precision=lax.Precision.HIGHEST)
        labels = lax.dynamic_slice_in_dim(outcome, start, NB_DEV, 0).astype(jnp.float32)
        filled = lax.dynamic_slice_in_dim(block_fill, start, NB_DEV, 0)
        valid_rows = lax.broadcasted_iota(jnp.int32, (NB_DEV, BLK), 1) < filled[:, None]
        residual = jnp.where(valid_rows, labels - jax.nn.sigmoid(logits), jnp.float32(0.0))
        return jnp.einsum('pnb,nb->pn', values, residual, precision=lax.Precision.HIGHEST)

    stacked = lax.map(per_device, jnp.arange(N_ROWS, dtype=jnp.int32))
    block_grads = jnp.moveaxis(stacked, 0, 1).reshape(P_SIZE, NB)
    fixed_grad = jnp.sum(block_grads, axis=1) - fixed_coef
    group_terms = jax.ops.segment_sum(block_grads.T, block_group, num_segments=GROUPS).T
    prior_term = jnp.dot(precision, slopes, precision=lax.Precision.HIGHEST)
    return fixed_grad, group_terms - prior_term
```

```python
import jax
import jax.numpy as jnp
from jax import lax
from jax.experimental import pallas as pl
from jax.experimental.pallas import tpu as pltpu
from jax.sharding import PartitionSpec as P

f32 = jnp.float32
bf16 = jnp.bfloat16
VMEM = pl.BlockSpec(memory_space=pltpu.VMEM)
SMEM = pl.BlockSpec(memory_space=pltpu.SMEM)
LANES = 128
ROOM = pltpu.CompilerParams(vmem_limit_bytes=16 << 20)


def from_behind(shard, axis, by):
    peers = lax.axis_size(axis)
    pairs = [(i, i + by) for i in range(peers) if 0 <= i + by < peers]
    return lax.ppermute(shard, axis, pairs)


def exchange(parts, axis):
    return lax.all_to_all(parts, axis, 0, 0, tiled=True)


def three_parts(x):
    a = x.astype(bf16)
    rest = x - a.astype(f32)
    b = rest.astype(bf16)
    c = (rest - b.astype(f32)).astype(bf16)
    return jnp.concatenate([a, b, c], axis=0)


def select_kernel(where_ref, group_ref, fill_ref, outcome_ref, hot_ref, label_ref, valid_ref, scratch_ref):
    window, blocks = hot_ref.shape
    rows = label_ref.shape[0]
    offset = where_ref[0]
    index = group_ref[...] - offset
    for piece in range(0, window, 256):
        ids = lax.broadcasted_iota(jnp.int32, (256, blocks), 0) + piece
        hot_ref[piece : piece + 256, :] = (ids == index).astype(f32).astype(bf16)
    start = pl.multiple_of(where_ref[1] * rows, rows)
    fill = fill_ref[pl.ds(where_ref[1] * rows // LANES, 1), :].astype(f32)
    scratch_ref[...] = jnp.broadcast_to(fill, (LANES, LANES)).T
    column = scratch_ref[pl.ds(pl.multiple_of(lax.rem(start, LANES), rows), rows), :]
    lane = lax.broadcasted_iota(jnp.int32, (rows, LANES), 1).astype(f32)
    valid_ref[...] = (lane < column).astype(f32)
    label_ref[...] = outcome_ref[pl.ds(start, rows), :].astype(f32)


def predict_kernel(lower_ref, own_ref, upper_ref, fixed_ref, hot_ref, design_ref, out_ref, coef_ref):
    size = own_ref.shape[0]
    blocks = out_ref.shape[0]
    parts = [three_parts(r[...]) for r in (lower_ref, own_ref, upper_ref)]
    window = jnp.concatenate(parts, axis=1)
    picked = jnp.dot(window, hot_ref[...], preferred_element_type=f32)
    coefs = picked[:size] + picked[size : 2 * size] + picked[2 * size :]
    padded = jnp.concatenate([coefs, jnp.zeros((LANES - size, blocks), f32)], axis=0)
    coef_ref[...] = padded.T[:, :size] + fixed_ref[...]
    step = 32

    def chunk(i, carry):
        start = pl.multiple_of(i * step, step)
        here = coef_ref[pl.ds(start, step), :]
        total = jnp.zeros((step, LANES), f32)
        for p in range(size):
            total = total + here[:, p : p + 1] * design_ref[p, pl.ds(start, step), :].astype(f32)
        out_ref[pl.ds(start, step), :] = total
        return carry

    lax.fori_loop(0, blocks // step, chunk, 0)


def residual_kernel(parts_ref, label_ref, valid_ref, out_ref):
    logits = jnp.sum(parts_ref[...], axis=0)
    residual = jnp.where(valid_ref[...] > 0.5, label_ref[...] - jax.nn.sigmoid(logits), 0.0)
    out_ref[...] = jnp.broadcast_to(residual[None], out_ref.shape)


def gradient_kernel(design_ref, residual_ref, hot_ref, lower_ref, own_ref, upper_ref, fixed_ref, grad_ref):
    size, blocks, _ = design_ref.shape
    groups = own_ref.shape[1]
    step = 32
    lane = lax.broadcasted_iota(jnp.int32, (step, LANES), 1)

    def chunk(i, carry):
        start = pl.multiple_of(i * step, step)
        residual = residual_ref[pl.ds(start, step), :]
        grads = jnp.zeros((step, LANES), f32)
        for p in range(size):
            product = design_ref[p, pl.ds(start, step), :].astype(f32) * residual
            grads = jnp.where(lane == p, jnp.sum(product, axis=1, keepdims=True), grads)
        grad_ref[pl.ds(start, step), :] = grads
        return carry

    lax.fori_loop(0, blocks // step, chunk, 0)
    grads = grad_ref[...]
    fixed_ref[...] = jnp.broadcast_to(jnp.sum(grads, axis=0, keepdims=True), fixed_ref.shape)
    parts = three_parts(grads.T[:size])
    sums = lax.dot_general(parts, hot_ref[...], (((1,), (1,)), ((), ())), preferred_element_type=f32)
    sums = sums[:size] + sums[size : 2 * size] + sums[2 * size :]
    lower_ref[...] = sums[:, :groups]
    own_ref[...] = sums[:, groups : 2 * groups]
    upper_ref[...] = sums[:, 2 * groups :]


def finish_kernel(fixed_ref, coef_ref, own_ref, down_ref, up_ref, prior_ref, fixed_out, slope_out):
    size = coef_ref.shape[1]
    fixed_out[...] = jnp.sum(fixed_ref[...], axis=0, keepdims=True)[:, :size] - coef_ref[...]
    slope_out[...] = own_ref[...] + down_ref[...] + up_ref[...] - prior_ref[...]


def shape(*dims, dtype=f32):
    return jax.ShapeDtypeStruct(dims, dtype)


def body(design, outcome, block_fill, block_group, fixed_coef, slopes, precision):
    size, group_count = slopes.shape
    blocks = block_group.shape[0]
    covs, rows = lax.axis_size("cov"), lax.axis_size("rows")
    share = blocks // covs

    from_lower = from_behind(slopes, "rows", 1)
    from_upper = from_behind(slopes, "rows", -1)

    gathered = exchange(jnp.broadcast_to(slopes[None], (covs, size, group_count)), "cov")
    prior_term = jnp.dot(
        precision, gathered.reshape(covs * size, group_count), precision=lax.Precision.HIGHEST
    )

    where = jnp.stack([(lax.axis_index("rows") - 1) * group_count, lax.axis_index("cov")])
    hot, label, valid = pl.pallas_call(
        select_kernel,
        out_shape=(
            shape(3 * group_count, blocks, dtype=bf16),
            shape(share, LANES),
            shape(share, LANES),
        ),
        in_specs=[SMEM, VMEM, VMEM, VMEM],
        out_specs=(VMEM, VMEM, VMEM),
        scratch_shapes=[pltpu.VMEM((LANES, LANES), f32)],
        compiler_params=ROOM,
        name="select",
    )(where, block_group.reshape(1, blocks), block_fill.reshape(blocks // LANES, LANES), outcome)

    fixed_row = fixed_coef.reshape(1, size)
    partial = pl.pallas_call(
        predict_kernel,
        out_shape=shape(blocks, LANES),
        in_specs=[VMEM] * 6,
        out_specs=VMEM,
        scratch_shapes=[pltpu.VMEM((blocks, size), f32)],
        compiler_params=ROOM,
        name="predict",
    )(from_lower, slopes, from_upper, fixed_row, hot, design)

    received = exchange(partial.reshape(covs, share, LANES), "cov")
    spread = pl.pallas_call(
        residual_kernel,
        out_shape=shape(covs, share, LANES),
        in_specs=[VMEM] * 3,
        out_specs=VMEM,
        compiler_params=ROOM,
        name="residual",
    )(received, label, valid)
    residual = exchange(spread, "cov").reshape(blocks, LANES)

    to_lower, own, to_upper, fixed_parts = pl.pallas_call(
        gradient_kernel,
        out_shape=(shape(size, group_count),) * 3 + (shape(rows, LANES),),
        in_specs=[VMEM] * 3,
        out_specs=(VMEM,) * 4,
        scratch_shapes=[pltpu.VMEM((blocks, LANES), f32)],
        compiler_params=ROOM,
        name="gradient",
    )(design, residual, hot)

    given_down = from_behind(to_lower, "rows", -1)
    given_up = from_behind(to_upper, "rows", 1)
    fixed_all = exchange(fixed_parts, "rows")
    fixed_grad, slope_grad = pl.pallas_call(
        finish_kernel,
        out_shape=(shape(1, size), shape(size, group_count)),
        in_specs=[VMEM] * 6,
        out_specs=(VMEM, VMEM),
        compiler_params=ROOM,
        name="finish",
    )(fixed_all, fixed_row, own, given_down, given_up, prior_term)
    return (fixed_grad.reshape(size), slope_grad)


def solution(mesh):
    return jax.shard_map(
        body,
        mesh=mesh,
        in_specs=(
            P("cov", "rows", None),
            P("rows", None),
            P("rows"),
            P("rows"),
            P("cov"),
            P("cov", "rows"),
            P("cov", None),
        ),
        out_specs=(P("cov"), P("cov", "rows")),
        check_vma=False,
    )
```

```python
import jax
import jax.numpy as jnp
from jax import lax
from jax.experimental import pallas as pl
from jax.experimental.pallas import tpu as pltpu
from jax.sharding import PartitionSpec as P

f32 = jnp.float32
bf16 = jnp.bfloat16
VMEM = pl.BlockSpec(memory_space=pltpu.VMEM)
SMEM = pl.BlockSpec(memory_space=pltpu.SMEM)
HBM = pl.BlockSpec(memory_space=pltpu.HBM)
LANES = 128
ROOM = pltpu.CompilerParams(vmem_limit_bytes=16 << 20)


def from_behind(shard, axis, by):
    peers = lax.axis_size(axis)
    pairs = [(i, i + by) for i in range(peers) if 0 <= i + by < peers]
    return lax.ppermute(shard, axis, pairs)


def exchange(parts, axis):
    return lax.all_to_all(parts, axis, 0, 0, tiled=True)


def cost(flops, size):
    return pl.CostEstimate(flops=flops, bytes_accessed=size, transcendentals=0)


def three_parts(x):
    a = x.astype(bf16)
    rest = x - a.astype(f32)
    b = rest.astype(bf16)
    c = (rest - b.astype(f32)).astype(bf16)
    return jnp.concatenate([a, b, c], axis=0)


def add_parts(x):
    size = x.shape[0] // 3
    return x[:size] + x[size : 2 * size] + x[2 * size :]


def select_kernel(
    where_ref, group_hbm, fill_hbm, outcome_hbm, fixed_hbm, slopes_hbm, design_hbm,
    hot_ref, label_ref, valid_ref, fixed_ref, slope_ref, coef_ref, design_ref,
    group_ref, fill_ref, outcome_ref, own_ref, column_ref, sems,
):
    window, blocks = hot_ref.shape
    rows = label_ref.shape[0]
    size, groups = own_ref.shape
    start = pl.multiple_of(where_ref[1] * rows, rows)
    copies = [
        pltpu.make_async_copy(group_hbm, group_ref, sems.at[0]),
        pltpu.make_async_copy(slopes_hbm, own_ref, sems.at[1]),
        pltpu.make_async_copy(fixed_hbm, fixed_ref, sems.at[2]),
        pltpu.make_async_copy(fill_hbm, fill_ref, sems.at[3]),
        pltpu.make_async_copy(outcome_hbm.at[pl.ds(start, rows)], outcome_ref, sems.at[4]),
        pltpu.make_async_copy(design_hbm, design_ref, sems.at[5]),
    ]
    for copy in copies:
        copy.start()
    for copy in copies[:5]:
        copy.wait()
    index = group_ref[...] - where_ref[0]
    for piece in range(0, window, groups):
        ids = lax.broadcasted_iota(jnp.int32, (groups, blocks), 0) + piece
        hot_ref[piece : piece + groups, :] = (ids == index).astype(f32).astype(bf16)
    own = own_ref[...]
    for half in range(groups // LANES):
        slope_ref[half * size : (half + 1) * size, :] = own[:, half * LANES : (half + 1) * LANES]
    coef_ref[...] = add_parts(
        jnp.dot(three_parts(own), hot_ref[groups : 2 * groups, :], preferred_element_type=f32)
    )
    fill = fill_ref[pl.ds(start // LANES, 1), :].astype(f32)
    column_ref[...] = jnp.broadcast_to(fill, (LANES, LANES)).T
    column = column_ref[pl.ds(pl.multiple_of(lax.rem(start, LANES), rows), rows), :]
    lane = lax.broadcasted_iota(jnp.int32, (rows, LANES), 1).astype(f32)
    valid_ref[...] = (lane < column).astype(f32)
    label_ref[...] = outcome_ref[...].astype(f32)
    copies[5].wait()


def predict_kernel(lower_ref, upper_ref, own_coef_ref, fixed_ref, hot_ref, design_ref, out_ref, coef_ref):
    size, groups = lower_ref.shape
    blocks = out_ref.shape[0]
    coefs = own_coef_ref[...]
    coefs += add_parts(
        jnp.dot(three_parts(lower_ref[...]), hot_ref[:groups, :], preferred_element_type=f32)
    )
    coefs += add_parts(
        jnp.dot(three_parts(upper_ref[...]), hot_ref[2 * groups :, :], preferred_element_type=f32)
    )
    padded = jnp.concatenate([coefs, jnp.zeros((LANES - size, blocks), f32)], axis=0)
    coef_ref[...] = padded.T[:, :size] + fixed_ref[...]
    step = 32

    def chunk(i, carry):
        start = pl.multiple_of(i * step, step)
        here = coef_ref[pl.ds(start, step), :]
        total = jnp.zeros((step, LANES), f32)
        for p in range(size):
            total = total + here[:, p : p + 1] * design_ref[p, pl.ds(start, step), :].astype(f32)
        out_ref[pl.ds(start, step), :] = total
        return carry

    lax.fori_loop(0, blocks // step, chunk, 0)


def residual_kernel(parts_ref, label_ref, valid_ref, slope_ref, out_ref):
    rows = label_ref.shape[0]
    logits = jnp.sum(parts_ref[...], axis=0)
    residual = jnp.where(valid_ref[...] > 0.5, label_ref[...] - jax.nn.sigmoid(logits), 0.0)
    peers = out_ref.shape[0]
    out_ref[:, :rows, :] = jnp.broadcast_to(residual[None], (peers,) + residual.shape)
    out_ref[:, rows:, :] = jnp.broadcast_to(slope_ref[...][None], (peers,) + slope_ref.shape)


def gradient_kernel(design_ref, back_ref, fixed_ref, grad_ref):
    size, blocks, _ = design_ref.shape
    step = blocks // back_ref.shape[0]
    lane = lax.broadcasted_iota(jnp.int32, (step, LANES), 1)

    def chunk(i, total):
        start = pl.multiple_of(i * step, step)
        residual = back_ref[i, :step, :]
        grads = jnp.zeros((step, LANES), f32)
        for p in range(size):
            product = design_ref[p, pl.ds(start, step), :].astype(f32) * residual
            grads = jnp.where(lane == p, jnp.sum(product, axis=1, keepdims=True), grads)
        grad_ref[pl.ds(start, step), :] = grads
        return total + grads

    total = lax.fori_loop(0, blocks // step, chunk, jnp.zeros((step, LANES), f32))
    fixed_ref[...] = jnp.broadcast_to(jnp.sum(total, axis=0, keepdims=True), fixed_ref.shape)


def group_kernel(grad_ref, hot_ref, back_ref, precision_ref, lower_ref, own_ref, upper_ref):
    size, groups = own_ref.shape
    rows = back_ref.shape[1] - size * (groups // LANES)
    parts = three_parts(grad_ref[...].T[:size])
    sums = add_parts(
        lax.dot_general(parts, hot_ref[...], (((1,), (1,)), ((), ())), preferred_element_type=f32)
    )
    lower_ref[...] = sums[:, :groups]
    upper_ref[...] = sums[:, 2 * groups :]
    slopes = [
        back_ref[:, rows + half * size : rows + (half + 1) * size, :].reshape(-1, LANES)
        for half in range(groups // LANES)
    ]
    prior = jnp.dot(
        precision_ref[...],
        jnp.concatenate(slopes, axis=1),
        precision=lax.Precision.HIGHEST,
        preferred_element_type=f32,
    )
    own_ref[...] = sums[:, groups : 2 * groups] - prior


def finish_kernel(fixed_all_ref, fixed_ref, own_ref, down_ref, up_ref, fixed_out, slope_out):
    size = fixed_ref.shape[1]
    fixed_out[...] = jnp.sum(fixed_all_ref[...], axis=0, keepdims=True)[:, :size] - fixed_ref[...]
    slope_out[...] = own_ref[...] + down_ref[...] + up_ref[...]


def shape(*dims, dtype=f32):
    return jax.ShapeDtypeStruct(dims, dtype)


def body(design, outcome, block_fill, block_group, fixed_coef, slopes, precision):
    size, group_count = slopes.shape
    blocks = block_group.shape[0]
    covs, rows = lax.axis_size("cov"), lax.axis_size("rows")
    share = blocks // covs
    slope_rows = size * group_count // LANES

    from_lower = from_behind(slopes, "rows", 1)
    from_upper = from_behind(slopes, "rows", -1)

    where = jnp.stack([(lax.axis_index("rows") - 1) * group_count, lax.axis_index("cov")])
    hot, label, valid, fixed_row, own_rows, own_coefs, design_here = pl.pallas_call(
        select_kernel,
        out_shape=(
            shape(3 * group_count, blocks, dtype=bf16),
            shape(share, LANES),
            shape(share, LANES),
            shape(1, size),
            shape(slope_rows, LANES),
            shape(size, blocks),
            shape(*design.shape, dtype=bf16),
        ),
        in_specs=[SMEM] + [HBM] * 6,
        out_specs=(VMEM,) * 7,
        scratch_shapes=[
            pltpu.VMEM((1, blocks), jnp.int32),
            pltpu.VMEM((blocks // LANES, LANES), jnp.int32),
            pltpu.VMEM((share, LANES), jnp.int32),
            pltpu.VMEM((size, group_count), f32),
            pltpu.VMEM((LANES, LANES), f32),
            pltpu.SemaphoreType.DMA((6,)),
        ],
        compiler_params=ROOM,
        cost_estimate=cost(10_000_000, 5_000_000),
        name="select",
    )(
        where,
        *(
            pltpu.with_memory_space_constraint(x, pltpu.HBM)
            for x in (
                block_group.reshape(1, blocks),
                block_fill.reshape(blocks // LANES, LANES),
                outcome,
                fixed_coef.reshape(1, size),
                slopes,
                design,
            )
        ),
    )

    partial = pl.pallas_call(
        predict_kernel,
        out_shape=shape(blocks, LANES),
        in_specs=[VMEM] * 6,
        out_specs=VMEM,
        scratch_shapes=[pltpu.VMEM((blocks, size), f32)],
        compiler_params=ROOM,
        name="predict",
    )(from_lower, from_upper, own_coefs, fixed_row, hot, design_here)

    received = exchange(partial.reshape(covs, share, LANES), "cov")
    spread = pl.pallas_call(
        residual_kernel,
        out_shape=shape(covs, share + slope_rows, LANES),
        in_specs=[VMEM] * 4,
        out_specs=VMEM,
        compiler_params=ROOM,
        name="residual",
    )(received, label, valid, own_rows)
    back = exchange(spread, "cov")

    fixed_parts, grads = pl.pallas_call(
        gradient_kernel,
        out_shape=(shape(rows, LANES), shape(blocks, LANES)),
        in_specs=[VMEM] * 2,
        out_specs=(VMEM,) * 2,
        compiler_params=ROOM,
        name="gradient",
    )(design_here, back)
    fixed_all = exchange(fixed_parts, "rows")

    to_lower, own, to_upper = pl.pallas_call(
        group_kernel,
        out_shape=(shape(size, group_count),) * 3,
        in_specs=[VMEM] * 4,
        out_specs=(VMEM,) * 3,
        compiler_params=ROOM,
        cost_estimate=cost(100_000_000, 5_000_000),
        name="group",
    )(grads, hot, back, precision)
    given_down = from_behind(to_lower, "rows", -1)
    given_up = from_behind(to_upper, "rows", 1)

    fixed_grad, slope_grad = pl.pallas_call(
        finish_kernel,
        out_shape=(shape(1, size), shape(size, group_count)),
        in_specs=[VMEM] * 5,
        out_specs=(VMEM, VMEM),
        compiler_params=ROOM,
        name="finish",
    )(fixed_all, fixed_row, own, given_down, given_up)
    return (fixed_grad.reshape(size), slope_grad)


def solution(mesh):
    return jax.shard_map(
        body,
        mesh=mesh,
        in_specs=(
            P("cov", "rows", None),
            P("rows", None),
            P("rows"),
            P("rows"),
            P("cov"),
            P("cov", "rows"),
            P("cov", None),
        ),
        out_specs=(P("cov"), P("cov", "rows")),
        check_vma=False,
    )
```

```python
import jax
import jax.numpy as jnp
from jax import lax
from jax.experimental import pallas as pl
from jax.experimental.pallas import tpu as pltpu
from jax.sharding import PartitionSpec as P

f32 = jnp.float32
bf16 = jnp.bfloat16
VMEM = pl.BlockSpec(memory_space=pltpu.VMEM)
SMEM = pl.BlockSpec(memory_space=pltpu.SMEM)
HBM = pl.BlockSpec(memory_space=pltpu.HBM)
LANES = 128
NEAR = 4
ROOM = pltpu.CompilerParams(vmem_limit_bytes=16 << 20)


def from_behind(shard, axis, by):
    peers = lax.axis_size(axis)
    pairs = [(i, i + by) for i in range(peers) if 0 <= i + by < peers]
    return lax.ppermute(shard, axis, pairs)


def exchange(parts, axis, groups=None):
    return lax.all_to_all(parts, axis, 0, 0, tiled=True, axis_index_groups=groups)


def cost(flops, size):
    return pl.CostEstimate(flops=flops, bytes_accessed=size, transcendentals=0)


def three_parts(x):
    a = x.astype(bf16)
    rest = x - a.astype(f32)
    b = rest.astype(bf16)
    c = (rest - b.astype(f32)).astype(bf16)
    return jnp.concatenate([a, b, c], axis=0)


def add_parts(x):
    size = x.shape[0] // 3
    return x[:size] + x[size : 2 * size] + x[2 * size :]


def select_kernel(
    where_ref, group_hbm, fill_hbm, outcome_hbm, fixed_hbm, slopes_hbm, design_hbm,
    hot_ref, label_ref, valid_ref, fixed_ref, slope_ref, coef_ref, design_ref,
    group_ref, fill_ref, outcome_ref, own_ref, sems,
):
    window, blocks = hot_ref.shape
    rows = label_ref.shape[0]
    size, groups = own_ref.shape
    start = pl.multiple_of(lax.rem(where_ref[1], NEAR) * rows, rows)
    copies = [
        pltpu.make_async_copy(group_hbm, group_ref, sems.at[0]),
        pltpu.make_async_copy(slopes_hbm, own_ref, sems.at[1]),
        pltpu.make_async_copy(fixed_hbm, fixed_ref, sems.at[2]),
        pltpu.make_async_copy(fill_hbm, fill_ref, sems.at[3]),
        pltpu.make_async_copy(outcome_hbm.at[pl.ds(start, rows)], outcome_ref, sems.at[4]),
        pltpu.make_async_copy(design_hbm, design_ref, sems.at[5]),
    ]
    for copy in copies:
        copy.start()
    for copy in copies[:5]:
        copy.wait()
    index = group_ref[...] - where_ref[0]
    for piece in range(0, window, groups):
        ids = lax.broadcasted_iota(jnp.int32, (groups, blocks), 0) + piece
        hot_ref[piece : piece + groups, :] = (ids == index).astype(f32).astype(bf16)
    own = own_ref[...]
    for half in range(groups // LANES):
        slope_ref[half * size : (half + 1) * size, :] = own[:, half * LANES : (half + 1) * LANES]
    coef_ref[...] = add_parts(
        jnp.dot(three_parts(own), hot_ref[groups : 2 * groups, :], preferred_element_type=f32)
    )
    fill = fill_ref[pl.ds(lax.rem(where_ref[1], NEAR), 1), :].astype(f32)
    column = jnp.broadcast_to(fill, (rows, rows)).T
    lane = lax.broadcasted_iota(jnp.int32, (rows, LANES), 1).astype(f32)
    valid_ref[...] = (lane < column).astype(f32)
    label_ref[...] = outcome_ref[...].astype(f32)
    copies[5].wait()


def predict_kernel(lower_ref, upper_ref, own_coef_ref, fixed_ref, hot_ref, design_ref, out_ref, coef_ref):
    size, groups = lower_ref.shape
    blocks = out_ref.shape[0]
    coefs = own_coef_ref[...]
    coefs += add_parts(
        jnp.dot(three_parts(lower_ref[...]), hot_ref[:groups, :], preferred_element_type=f32)
    )
    coefs += add_parts(
        jnp.dot(three_parts(upper_ref[...]), hot_ref[2 * groups :, :], preferred_element_type=f32)
    )
    padded = jnp.concatenate([coefs, jnp.zeros((LANES - size, blocks), f32)], axis=0)
    coef_ref[...] = padded.T[:, :size] + fixed_ref[...]
    step = 32

    def chunk(i, carry):
        start = pl.multiple_of(i * step, step)
        here = coef_ref[pl.ds(start, step), :]
        total = jnp.zeros((step, LANES), f32)
        for p in range(size):
            total = total + here[:, p : p + 1] * design_ref[p, pl.ds(start, step), :].astype(f32)
        out_ref[pl.ds(start, step), :] = total
        return carry

    lax.fori_loop(0, blocks // step, chunk, 0)


def spread_rows(out_ref, *pieces):
    at = 0
    for piece in pieces:
        size = piece.shape[0]
        out_ref[:, at : at + size, :] = jnp.broadcast_to(piece[None], (out_ref.shape[0],) + piece.shape)
        at += size


def gather_kernel(parts_ref, slope_ref, out_ref):
    spread_rows(out_ref, jnp.sum(parts_ref[...], axis=0), slope_ref[...])


def residual_kernel(parts_ref, label_ref, valid_ref, out_ref):
    rows = label_ref.shape[0]
    logits = jnp.sum(parts_ref[:, :rows, :], axis=0)
    residual = jnp.where(valid_ref[...] > 0.5, label_ref[...] - jax.nn.sigmoid(logits), 0.0)
    spread_rows(out_ref, residual, *(parts_ref[i, rows:, :] for i in range(parts_ref.shape[0])))


def gradient_kernel(design_ref, back_ref, fixed_ref, grad_ref):
    size, blocks, _ = design_ref.shape
    step = 32
    share = blocks // NEAR
    lane = lax.broadcasted_iota(jnp.int32, (step, LANES), 1)
    total = jnp.zeros((step, LANES), f32)
    for peer in range(NEAR):

        def chunk(i, total, peer=peer):
            inner = pl.multiple_of(i * step, step)
            start = pl.multiple_of(peer * share + i * step, step)
            residual = back_ref[peer, pl.ds(inner, step), :]
            grads = jnp.zeros((step, LANES), f32)
            for p in range(size):
                product = design_ref[p, pl.ds(start, step), :].astype(f32) * residual
                grads = jnp.where(lane == p, jnp.sum(product, axis=1, keepdims=True), grads)
            grad_ref[pl.ds(start, step), :] = grads
            return total + grads

        total = lax.fori_loop(0, share // step, chunk, total)
    fixed_ref[...] = jnp.broadcast_to(jnp.sum(total, axis=0, keepdims=True), fixed_ref.shape)


def group_kernel(grad_ref, hot_ref, back_ref, precision_ref, lower_ref, own_ref, upper_ref):
    size, groups = own_ref.shape
    halves = groups // LANES
    far = precision_ref.shape[1] // (size * NEAR)
    rows = back_ref.shape[1] - far * size * halves
    parts = three_parts(grad_ref[...].T[:size])
    sums = add_parts(
        lax.dot_general(parts, hot_ref[...], (((1,), (1,)), ((), ())), preferred_element_type=f32)
    )
    lower_ref[...] = sums[:, :groups]
    upper_ref[...] = sums[:, 2 * groups :]
    slopes = []
    for half in range(halves):
        starts = [rows + (i * halves + half) * size for i in range(far)]
        pieces = [back_ref[:, at : at + size, :].reshape(-1, LANES) for at in starts]
        slopes.append(jnp.concatenate(pieces, axis=0))
    prior = jnp.dot(
        precision_ref[...],
        jnp.concatenate(slopes, axis=1),
        precision=lax.Precision.HIGHEST,
        preferred_element_type=f32,
    )
    own_ref[...] = sums[:, groups : 2 * groups] - prior


def finish_kernel(fixed_all_ref, fixed_ref, own_ref, down_ref, up_ref, fixed_out, slope_out):
    size = fixed_ref.shape[1]
    fixed_out[...] = jnp.sum(fixed_all_ref[...], axis=0, keepdims=True)[:, :size] - fixed_ref[...]
    slope_out[...] = own_ref[...] + down_ref[...] + up_ref[...]


def shape(*dims, dtype=f32):
    return jax.ShapeDtypeStruct(dims, dtype)


def body(design, outcome, block_fill, block_group, fixed_coef, slopes, precision):
    size, group_count = slopes.shape
    blocks = block_group.shape[0]
    covs, rows = lax.axis_size("cov"), lax.axis_size("rows")
    far = covs // NEAR
    share = blocks // NEAR
    near_groups = [[i * NEAR + j for j in range(NEAR)] for i in range(far)]
    far_groups = [[i * NEAR + j for i in range(far)] for j in range(NEAR)]
    slope_rows = size * group_count // LANES

    from_lower = from_behind(slopes, "rows", 1)
    from_upper = from_behind(slopes, "rows", -1)

    where = jnp.stack([(lax.axis_index("rows") - 1) * group_count, lax.axis_index("cov")])
    hot, label, valid, fixed_row, own_rows, own_coefs, design_here = pl.pallas_call(
        select_kernel,
        out_shape=(
            shape(3 * group_count, blocks, dtype=bf16),
            shape(share, LANES),
            shape(share, LANES),
            shape(1, size),
            shape(slope_rows, LANES),
            shape(size, blocks),
            shape(*design.shape, dtype=bf16),
        ),
        in_specs=[SMEM] + [HBM] * 6,
        out_specs=(VMEM,) * 7,
        scratch_shapes=[
            pltpu.VMEM((1, blocks), jnp.int32),
            pltpu.VMEM((blocks // LANES, LANES), jnp.int32),
            pltpu.VMEM((share, LANES), jnp.int32),
            pltpu.VMEM((size, group_count), f32),
            pltpu.SemaphoreType.DMA((6,)),
        ],
        compiler_params=ROOM,
        cost_estimate=cost(10_000_000, 5_000_000),
        name="select",
    )(
        where,
        *(
            pltpu.with_memory_space_constraint(x, pltpu.HBM)
            for x in (
                block_group.reshape(1, blocks),
                block_fill.reshape(blocks // LANES, LANES),
                outcome,
                fixed_coef.reshape(1, size),
                slopes,
                design,
            )
        ),
    )

    partial = pl.pallas_call(
        predict_kernel,
        out_shape=shape(blocks, LANES),
        in_specs=[VMEM] * 6,
        out_specs=VMEM,
        scratch_shapes=[pltpu.VMEM((blocks, size), f32)],
        compiler_params=ROOM,
        name="predict",
    )(from_lower, from_upper, own_coefs, fixed_row, hot, design_here)

    received = exchange(partial.reshape(NEAR, share, LANES), "cov", near_groups)
    spread = pl.pallas_call(
        gather_kernel,
        out_shape=shape(far, share + slope_rows, LANES),
        in_specs=[VMEM] * 2,
        out_specs=VMEM,
        compiler_params=ROOM,
        name="gather",
    )(received, own_rows)
    received = exchange(spread, "cov", far_groups)
    spread = pl.pallas_call(
        residual_kernel,
        out_shape=shape(NEAR, share + far * slope_rows, LANES),
        in_specs=[VMEM] * 3,
        out_specs=VMEM,
        compiler_params=ROOM,
        name="residual",
    )(received, label, valid)
    back = exchange(spread, "cov", near_groups)

    fixed_parts, grads = pl.pallas_call(
        gradient_kernel,
        out_shape=(shape(rows, LANES), shape(blocks, LANES)),
        in_specs=[VMEM] * 2,
        out_specs=(VMEM,) * 2,
        compiler_params=ROOM,
        name="gradient",
    )(design_here, back)
    fixed_all = exchange(fixed_parts, "rows")

    to_lower, own, to_upper = pl.pallas_call(
        group_kernel,
        out_shape=(shape(size, group_count),) * 3,
        in_specs=[VMEM] * 4,
        out_specs=(VMEM,) * 3,
        compiler_params=ROOM,
        cost_estimate=cost(100_000_000, 5_000_000),
        name="group",
    )(grads, hot, back, precision)
    given_down = from_behind(to_lower, "rows", -1)
    given_up = from_behind(to_upper, "rows", 1)

    fixed_grad, slope_grad = pl.pallas_call(
        finish_kernel,
        out_shape=(shape(1, size), shape(size, group_count)),
        in_specs=[VMEM] * 5,
        out_specs=(VMEM, VMEM),
        compiler_params=ROOM,
        name="finish",
    )(fixed_all, fixed_row, own, given_down, given_up)
    return (fixed_grad.reshape(size), slope_grad)


def solution(mesh):
    return jax.shard_map(
        body,
        mesh=mesh,
        in_specs=(
            P("cov", "rows", None),
            P("rows", None),
            P("rows"),
            P("rows"),
            P("cov"),
            P("cov", "rows"),
            P("cov", None),
        ),
        out_specs=(P("cov"), P("cov", "rows")),
        check_vma=False,
    )
```

```python
import jax
import jax.numpy as jnp
from jax import lax
from jax.experimental import pallas as pl
from jax.experimental.pallas import tpu as pltpu
from jax.sharding import PartitionSpec as P

f32 = jnp.float32
bf16 = jnp.bfloat16
VMEM = pl.BlockSpec(memory_space=pltpu.VMEM)
SMEM = pl.BlockSpec(memory_space=pltpu.SMEM)
HBM = pl.BlockSpec(memory_space=pltpu.HBM)
LANES = 128
NEAR = 4
ROOM = pltpu.CompilerParams(vmem_limit_bytes=16 << 20)


def from_behind(shard, axis, by):
    peers = lax.axis_size(axis)
    pairs = [(i, i + by) for i in range(peers) if 0 <= i + by < peers]
    return lax.ppermute(shard, axis, pairs)


def exchange(parts, axis, groups=None):
    return lax.all_to_all(parts, axis, 0, 0, tiled=True, axis_index_groups=groups)


def cost(flops, size):
    return pl.CostEstimate(flops=flops, bytes_accessed=size, transcendentals=0)


def three_parts(x):
    a = x.astype(bf16)
    rest = x - a.astype(f32)
    b = rest.astype(bf16)
    c = (rest - b.astype(f32)).astype(bf16)
    return jnp.concatenate([a, b, c], axis=0)


def add_parts(x):
    size = x.shape[0] // 3
    return x[:size] + x[size : 2 * size] + x[2 * size :]


def in_rows(*arrays):
    pieces = [x[:, at : at + LANES] for x in arrays for at in range(0, x.shape[1], LANES)]
    return jnp.concatenate(pieces, axis=0)


def select_kernel(
    where_ref, group_hbm, fill_hbm, outcome_hbm, fixed_hbm, slopes_hbm, precision_hbm, design_hbm,
    hot_ref, label_ref, valid_ref, fixed_ref, prior_ref, coef_ref, design_ref,
    group_ref, fill_ref, outcome_ref, own_ref, precision_ref, sems,
):
    window, blocks = hot_ref.shape
    rows = label_ref.shape[0]
    size, groups = own_ref.shape
    start = pl.multiple_of(lax.rem(where_ref[1], NEAR) * rows, rows)
    copies = [
        pltpu.make_async_copy(group_hbm, group_ref, sems.at[0]),
        pltpu.make_async_copy(slopes_hbm, own_ref, sems.at[1]),
        pltpu.make_async_copy(fixed_hbm, fixed_ref, sems.at[2]),
        pltpu.make_async_copy(fill_hbm, fill_ref, sems.at[3]),
        pltpu.make_async_copy(outcome_hbm.at[pl.ds(start, rows)], outcome_ref, sems.at[4]),
        pltpu.make_async_copy(precision_hbm, precision_ref, sems.at[5]),
        pltpu.make_async_copy(design_hbm, design_ref, sems.at[6]),
    ]
    for copy in copies:
        copy.start()
    for copy in copies[:6]:
        copy.wait()
    index = group_ref[...] - where_ref[0]
    for piece in range(0, window, groups):
        ids = lax.broadcasted_iota(jnp.int32, (groups, blocks), 0) + piece
        hot_ref[piece : piece + groups, :] = (ids == index).astype(f32).astype(bf16)
    own = own_ref[...]
    prior_ref[...] = in_rows(own, precision_ref[...])
    coef_ref[...] = add_parts(
        jnp.dot(three_parts(own), hot_ref[groups : 2 * groups, :], preferred_element_type=f32)
    )
    fill = fill_ref[pl.ds(lax.rem(where_ref[1], NEAR), 1), :].astype(f32)
    column = jnp.broadcast_to(fill, (rows, rows)).T
    lane = lax.broadcasted_iota(jnp.int32, (rows, LANES), 1).astype(f32)
    valid_ref[...] = (lane < column).astype(f32)
    label_ref[...] = outcome_ref[...].astype(f32)
    copies[6].wait()


def predict_kernel(
    lower_ref, upper_ref, own_coef_ref, fixed_ref, hot_ref, design_ref, prior_ref, out_ref, coef_ref
):
    size, groups = lower_ref.shape
    blocks = hot_ref.shape[1]
    share = blocks // NEAR
    coefs = own_coef_ref[...]
    coefs += add_parts(
        jnp.dot(three_parts(lower_ref[...]), hot_ref[:groups, :], preferred_element_type=f32)
    )
    coefs += add_parts(
        jnp.dot(three_parts(upper_ref[...]), hot_ref[2 * groups :, :], preferred_element_type=f32)
    )
    padded = jnp.concatenate([coefs, jnp.zeros((LANES - size, blocks), f32)], axis=0)
    coef_ref[...] = padded.T[:, :size] + fixed_ref[...]
    step = 32
    for peer in range(NEAR):

        def chunk(i, carry, peer=peer):
            inner = pl.multiple_of(i * step, step)
            start = pl.multiple_of(peer * share + i * step, step)
            here = coef_ref[pl.ds(start, step), :]
            total = jnp.zeros((step, LANES), f32)
            for p in range(size):
                total = total + here[:, p : p + 1] * design_ref[p, pl.ds(start, step), :].astype(f32)
            out_ref[peer, pl.ds(inner, step), :] = total
            return carry

        lax.fori_loop(0, share // step, chunk, 0)
        out_ref[peer, share:, :] = prior_ref[...]


def gather_kernel(where_ref, parts_ref, out_ref, prior_ref):
    size = prior_ref.shape[0] // (out_ref.shape[0] * NEAR)
    rows = out_ref.shape[1] - size * (prior_ref.shape[1] // LANES)
    total = jnp.sum(parts_ref[:, :rows, :], axis=0)
    columns = [
        parts_ref[:, at : at + size, :].reshape(-1, LANES)
        for at in range(rows, parts_ref.shape[1], size)
    ]
    halves = prior_ref.shape[1] // LANES
    slopes = jnp.concatenate(columns[:halves], axis=1)
    precision = jnp.concatenate(columns[halves:], axis=1)
    prior_ref[...] = lax.dot_general(
        precision,
        slopes,
        (((0,), (0,)), ((), ())),
        precision=lax.Precision.HIGHEST,
        preferred_element_type=f32,
    )
    near = lax.rem(where_ref[1], NEAR)
    for i in range(out_ref.shape[0]):
        out_ref[i, :rows, :] = total
        part = prior_ref[pl.ds(pl.multiple_of((i * NEAR + near) * size, size), size), :]
        out_ref[i, rows:, :] = in_rows(part)


def residual_kernel(parts_ref, label_ref, valid_ref, out_ref, prior_ref):
    rows = label_ref.shape[0]
    logits = jnp.sum(parts_ref[:, :rows, :], axis=0)
    residual = jnp.where(valid_ref[...] > 0.5, label_ref[...] - jax.nn.sigmoid(logits), 0.0)
    out_ref[...] = jnp.broadcast_to(residual[None], out_ref.shape)
    prior_ref[...] = jnp.sum(parts_ref[:, rows:, :], axis=0)


def gradient_kernel(design_ref, back_ref, fixed_ref, grad_ref):
    size, blocks, _ = design_ref.shape
    step = 32
    share = blocks // NEAR
    lane = lax.broadcasted_iota(jnp.int32, (step, LANES), 1)
    total = jnp.zeros((step, LANES), f32)
    for peer in range(NEAR):

        def chunk(i, total, peer=peer):
            inner = pl.multiple_of(i * step, step)
            start = pl.multiple_of(peer * share + i * step, step)
            residual = back_ref[peer, pl.ds(inner, step), :]
            grads = jnp.zeros((step, LANES), f32)
            for p in range(size):
                product = design_ref[p, pl.ds(start, step), :].astype(f32) * residual
                grads = jnp.where(lane == p, jnp.sum(product, axis=1, keepdims=True), grads)
            grad_ref[pl.ds(start, step), :] = grads
            return total + grads

        total = lax.fori_loop(0, share // step, chunk, total)
    fixed_ref[...] = jnp.broadcast_to(jnp.sum(total, axis=0)[None, None], fixed_ref.shape)


def group_kernel(grad_ref, hot_ref, prior_ref, lower_ref, own_ref, upper_ref):
    size, groups = own_ref.shape
    parts = three_parts(grad_ref[...].T[:size])
    sums = add_parts(
        lax.dot_general(parts, hot_ref[...], (((1,), (1,)), ((), ())), preferred_element_type=f32)
    )
    lower_ref[...] = sums[:, :groups]
    upper_ref[...] = sums[:, 2 * groups :]
    halves = [prior_ref[at : at + size, :] for at in range(0, prior_ref.shape[0], size)]
    own_ref[...] = sums[:, groups : 2 * groups] - jnp.concatenate(halves, axis=1)


def finish_kernel(fixed_all_ref, fixed_ref, own_ref, down_ref, up_ref, fixed_out, slope_out):
    size = fixed_ref.shape[1]
    fixed_out[...] = jnp.sum(fixed_all_ref[...], axis=0)[:1, :size] - fixed_ref[...]
    slope_out[...] = own_ref[...] + down_ref[...] + up_ref[...]


def shape(*dims, dtype=f32):
    return jax.ShapeDtypeStruct(dims, dtype)


def body(design, outcome, block_fill, block_group, fixed_coef, slopes, precision):
    size, group_count = slopes.shape
    blocks = block_group.shape[0]
    covs, rows = lax.axis_size("cov"), lax.axis_size("rows")
    far = covs // NEAR
    share = blocks // NEAR
    near_groups = [[i * NEAR + j for j in range(NEAR)] for i in range(far)]
    far_groups = [[i * NEAR + j for i in range(far)] for j in range(NEAR)]
    slope_rows = size * group_count // LANES
    precision_rows = size * size * covs // LANES

    from_lower = from_behind(slopes, "rows", 1)
    from_upper = from_behind(slopes, "rows", -1)

    where = jnp.stack([(lax.axis_index("rows") - 1) * group_count, lax.axis_index("cov")])
    hot, label, valid, fixed_row, prior_rows, own_coefs, design_here = pl.pallas_call(
        select_kernel,
        out_shape=(
            shape(3 * group_count, blocks, dtype=bf16),
            shape(share, LANES),
            shape(share, LANES),
            shape(1, size),
            shape(slope_rows + precision_rows, LANES),
            shape(size, blocks),
            shape(*design.shape, dtype=bf16),
        ),
        in_specs=[SMEM] + [HBM] * 7,
        out_specs=(VMEM,) * 7,
        scratch_shapes=[
            pltpu.VMEM((1, blocks), jnp.int32),
            pltpu.VMEM((blocks // LANES, LANES), jnp.int32),
            pltpu.VMEM((share, LANES), jnp.int32),
            pltpu.VMEM((size, group_count), f32),
            pltpu.VMEM((size, covs * size), f32),
            pltpu.SemaphoreType.DMA((7,)),
        ],
        compiler_params=ROOM,
        cost_estimate=cost(10_000_000, 5_000_000),
        name="select",
    )(
        where,
        *(
            pltpu.with_memory_space_constraint(x, pltpu.HBM)
            for x in (
                block_group.reshape(1, blocks),
                block_fill.reshape(blocks // LANES, LANES),
                outcome,
                fixed_coef.reshape(1, size),
                slopes,
                precision,
                design,
            )
        ),
    )

    partial = pl.pallas_call(
        predict_kernel,
        out_shape=shape(NEAR, share + slope_rows + precision_rows, LANES),
        in_specs=[VMEM] * 7,
        out_specs=VMEM,
        scratch_shapes=[pltpu.VMEM((blocks, size), f32)],
        compiler_params=ROOM,
        name="predict",
    )(from_lower, from_upper, own_coefs, fixed_row, hot, design_here, prior_rows)

    received = exchange(partial, "cov", near_groups)
    spread = pl.pallas_call(
        gather_kernel,
        out_shape=shape(far, share + slope_rows, LANES),
        in_specs=[SMEM, VMEM],
        out_specs=VMEM,
        scratch_shapes=[pltpu.VMEM((covs * size, group_count), f32)],
        compiler_params=ROOM,
        name="gather",
    )(where, received)
    received = exchange(spread, "cov", far_groups)
    spread, prior = pl.pallas_call(
        residual_kernel,
        out_shape=(shape(NEAR, share, LANES), shape(slope_rows, LANES)),
        in_specs=[VMEM] * 3,
        out_specs=(VMEM, VMEM),
        compiler_params=ROOM,
        name="residual",
    )(received, label, valid)
    back = exchange(spread, "cov", near_groups)

    fixed_parts, grads = pl.pallas_call(
        gradient_kernel,
        out_shape=(shape(rows, 2, LANES), shape(blocks, LANES)),
        in_specs=[VMEM] * 2,
        out_specs=(VMEM,) * 2,
        compiler_params=ROOM,
        name="gradient",
    )(design_here, back)
    fixed_all = exchange(fixed_parts, "rows")

    to_lower, own, to_upper = pl.pallas_call(
        group_kernel,
        out_shape=(shape(size, group_count),) * 3,
        in_specs=[VMEM] * 3,
        out_specs=(VMEM,) * 3,
        compiler_params=ROOM,
        cost_estimate=cost(100_000_000, 5_000_000),
        name="group",
    )(grads, hot, prior)
    given_down = from_behind(to_lower, "rows", -1)
    given_up = from_behind(to_upper, "rows", 1)

    fixed_grad, slope_grad = pl.pallas_call(
        finish_kernel,
        out_shape=(shape(1, size), shape(size, group_count)),
        in_specs=[VMEM] * 5,
        out_specs=(VMEM, VMEM),
        compiler_params=ROOM,
        name="finish",
    )(fixed_all, fixed_row, own, given_down, given_up)
    return (fixed_grad.reshape(size), slope_grad)


def solution(mesh):
    return jax.shard_map(
        body,
        mesh=mesh,
        in_specs=(
            P("cov", "rows", None),
            P("rows", None),
            P("rows"),
            P("rows"),
            P("cov"),
            P("cov", "rows"),
            P("cov", None),
        ),
        out_specs=(P("cov"), P("cov", "rows")),
        check_vma=False,
    )
```

```python
import jax
import jax.numpy as jnp
from jax import lax
from jax.experimental import pallas as pl
from jax.experimental.pallas import tpu as pltpu
from jax.sharding import PartitionSpec as P

f32 = jnp.float32
bf16 = jnp.bfloat16
VMEM = pl.BlockSpec(memory_space=pltpu.VMEM)
HBM = pl.BlockSpec(memory_space=pltpu.HBM)
LANES = 128
NEAR = 4
ROOM = pltpu.CompilerParams(vmem_limit_bytes=16 << 20)


def swap(shard, axis, first):
    peers = lax.axis_size(axis)
    pairs = [(i, i + 1) for i in range(first, peers - 1, 2)]
    return lax.ppermute(shard, axis, pairs + [(j, i) for i, j in pairs])


def exchange(parts, axis, groups=None):
    return lax.all_to_all(parts, axis, 0, 0, tiled=True, axis_index_groups=groups)


def cost(flops, size):
    return pl.CostEstimate(flops=flops, bytes_accessed=size, transcendentals=0)


def three_parts(x):
    a = x.astype(bf16)
    rest = x - a.astype(f32)
    b = rest.astype(bf16)
    c = (rest - b.astype(f32)).astype(bf16)
    return jnp.concatenate([a, b, c], axis=0)


def add_parts(x):
    size = x.shape[0] // 3
    return x[:size] + x[size : 2 * size] + x[2 * size :]


def in_rows(x):
    return jnp.concatenate([x[:, at : at + LANES] for at in range(0, x.shape[1], LANES)], axis=0)


def select_kernel(
    group_hbm, fill_hbm, outcome_hbm, fixed_hbm, slopes_hbm, precision_hbm, design_hbm,
    hot_ref, label_ref, valid_ref, fixed_ref, prior_ref, coef_ref, design_ref,
    group_ref, fill_ref, outcome_ref, own_ref, precision_ref, sems,
):
    window, blocks = hot_ref.shape
    rows = label_ref.shape[0]
    size, groups = own_ref.shape
    near = lax.rem(lax.axis_index("cov"), NEAR)
    start = pl.multiple_of(near * rows, rows)
    copies = [
        pltpu.make_async_copy(group_hbm, group_ref, sems.at[0]),
        pltpu.make_async_copy(slopes_hbm, own_ref, sems.at[1]),
        pltpu.make_async_copy(precision_hbm, precision_ref, sems.at[2]),
        pltpu.make_async_copy(outcome_hbm.at[pl.ds(start, rows)], outcome_ref, sems.at[3]),
        pltpu.make_async_copy(fill_hbm, fill_ref, sems.at[4]),
        pltpu.make_async_copy(fixed_hbm, fixed_ref, sems.at[5]),
        pltpu.make_async_copy(design_hbm, design_ref, sems.at[6]),
    ]
    for copy in copies:
        copy.start()
    for copy in copies[:2]:
        copy.wait()
    index = group_ref[...] - (lax.axis_index("rows") - 1) * groups
    for piece in range(0, window, groups):
        ids = lax.broadcasted_iota(jnp.int32, (groups, blocks), 0) + piece
        hot_ref[piece : piece + groups, :] = (ids == index).astype(f32).astype(bf16)
    own = own_ref[...]
    coef_ref[...] = add_parts(
        jnp.dot(three_parts(own), hot_ref[groups : 2 * groups, :], preferred_element_type=f32)
    )
    for copy in copies[2:6]:
        copy.wait()
    slope_rows = in_rows(own)
    precision = precision_ref[...]
    place = lax.rem(lax.broadcasted_iota(jnp.int32, (size, LANES), 1) // size, NEAR)
    for peer in range(NEAR):
        kept = [
            jnp.where(place == peer, precision[:, at : at + LANES], 0.0)
            for at in range(0, precision.shape[1], LANES)
        ]
        prior_ref[peer, : slope_rows.shape[0], :] = slope_rows
        prior_ref[peer, slope_rows.shape[0] :, :] = kept[0] + pltpu.roll(kept[1], size, 1)
    fill = fill_ref[pl.ds(near, 1), :].astype(f32)
    column = jnp.broadcast_to(fill, (rows, rows)).T
    lane = lax.broadcasted_iota(jnp.int32, (rows, LANES), 1).astype(f32)
    valid_ref[...] = (lane < column).astype(f32)
    label_ref[...] = outcome_ref[...].astype(f32)
    copies[6].wait()


def predict_kernel(
    even_ref, odd_ref, own_coef_ref, fixed_ref, hot_ref, design_ref, prior_ref, out_ref, coef_ref
):
    size, groups = even_ref.shape
    blocks = hot_ref.shape[1]
    share = blocks // NEAR
    parity = lax.rem(lax.axis_index("rows"), 2)
    coefs = own_coef_ref[...]
    for ref, place in ((even_ref, 1 - parity), (odd_ref, parity)):
        piece = hot_ref[pl.ds(pl.multiple_of(place * 2 * groups, groups), groups), :]
        coefs += add_parts(jnp.dot(three_parts(ref[...]), piece, preferred_element_type=f32))
    padded = jnp.concatenate([coefs, jnp.zeros((LANES - size, blocks), f32)], axis=0)
    coef_ref[...] = padded.T[:, :size] + fixed_ref[...]

    def chunk(peer, carry):
        start = pl.multiple_of(peer * share, share)
        here = coef_ref[pl.ds(start, share), :]
        total = jnp.zeros((share, LANES), f32)
        for p in range(size):
            total = total + here[:, p : p + 1] * design_ref[p, pl.ds(start, share), :].astype(f32)
        out_ref[peer, :share, :] = total
        out_ref[peer, share:, :] = prior_ref[peer]
        return carry

    lax.fori_loop(0, NEAR, chunk, 0)


def gather_kernel(parts_ref, out_ref, prior_ref):
    groups = prior_ref.shape[1]
    halves = groups // LANES
    size = (parts_ref.shape[1] - out_ref.shape[1])
    rows = out_ref.shape[1] - size * halves
    far = out_ref.shape[0]
    total = jnp.sum(parts_ref[:, :rows, :], axis=0)
    columns = [
        parts_ref[:, at : at + size, :].reshape(-1, LANES)
        for at in range(rows, parts_ref.shape[1], size)
    ]
    prior_ref[...] = lax.dot_general(
        columns[halves],
        jnp.concatenate(columns[:halves], axis=1),
        (((0,), (0,)), ((), ())),
        precision=lax.Precision.HIGHEST,
        preferred_element_type=f32,
    )
    near = lax.rem(lax.axis_index("cov"), NEAR)
    pieces = LANES // size
    for i in range(far):
        place = lax.rem(near + i % 2 * NEAR + i // 2, pieces)
        out_ref[i, :rows, :] = total
        part = prior_ref[pl.ds(pl.multiple_of(place * size, size), size), :]
        out_ref[i, rows:, :] = in_rows(part)


def residual_kernel(parts_ref, label_ref, valid_ref, out_ref, prior_ref):
    rows = label_ref.shape[0]
    logits = jnp.sum(parts_ref[:, :rows, :], axis=0)
    residual = jnp.where(valid_ref[...] > 0.5, label_ref[...] - jax.nn.sigmoid(logits), 0.0)
    out_ref[...] = jnp.broadcast_to(residual[None], out_ref.shape)
    prior_ref[...] = jnp.sum(parts_ref[:, rows:, :], axis=0)


def gradient_kernel(design_ref, back_ref, fixed_ref, grad_ref):
    size, blocks, _ = design_ref.shape
    share = blocks // NEAR
    lane = lax.broadcasted_iota(jnp.int32, (share, LANES), 1)

    def chunk(peer, total):
        start = pl.multiple_of(peer * share, share)
        residual = back_ref[peer]
        grads = jnp.zeros((share, LANES), f32)
        for p in range(size):
            product = design_ref[p, pl.ds(start, share), :].astype(f32) * residual
            grads = jnp.where(lane == p, jnp.sum(product, axis=1, keepdims=True), grads)
        grad_ref[pl.ds(start, share), :] = grads
        return total + jnp.sum(grads, axis=0, keepdims=True)

    total = lax.fori_loop(0, NEAR, chunk, jnp.zeros((1, LANES), f32))
    fixed_ref[...] = jnp.broadcast_to(total[None], fixed_ref.shape)


def group_kernel(grad_ref, hot_ref, prior_ref, even_ref, odd_ref, own_ref):
    size, groups = own_ref.shape
    parts = three_parts(grad_ref[...].T[:size])
    sums = add_parts(
        lax.dot_general(parts, hot_ref[...], (((1,), (1,)), ((), ())), preferred_element_type=f32)
    )
    lower, upper = sums[:, :groups], sums[:, 2 * groups :]
    odd = lax.rem(lax.axis_index("rows"), 2) == 1
    even_ref[...] = jnp.where(odd, lower, upper)
    odd_ref[...] = jnp.where(odd, upper, lower)
    halves = [prior_ref[at : at + size, :] for at in range(0, prior_ref.shape[0], size)]
    own_ref[...] = sums[:, groups : 2 * groups] - jnp.concatenate(halves, axis=1)


def finish_kernel(fixed_all_ref, fixed_ref, own_ref, even_ref, odd_ref, fixed_out, slope_out):
    size = fixed_ref.shape[1]
    fixed_out[...] = jnp.sum(fixed_all_ref[...], axis=0)[:1, :size] - fixed_ref[...]
    slope_out[...] = own_ref[...] + even_ref[...] + odd_ref[...]


def shape(*dims, dtype=f32):
    return jax.ShapeDtypeStruct(dims, dtype)


def body(design, outcome, block_fill, block_group, fixed_coef, slopes, precision):
    size, group_count = slopes.shape
    blocks = block_group.shape[0]
    covs, rows = lax.axis_size("cov"), lax.axis_size("rows")
    far = covs // NEAR
    share = blocks // NEAR
    near_groups = [[i * NEAR + j for j in range(NEAR)] for i in range(far)]
    far_groups = [[i * NEAR + j for i in range(far)] for j in range(NEAR)]
    slope_rows = size * group_count // LANES

    from_even = swap(slopes, "rows", 0)
    from_odd = swap(slopes, "rows", 1)

    hot, label, valid, fixed_row, prior_rows, own_coefs, design_here = pl.pallas_call(
        select_kernel,
        out_shape=(
            shape(3 * group_count, blocks, dtype=bf16),
            shape(share, LANES),
            shape(share, LANES),
            shape(1, size),
            shape(NEAR, slope_rows + size, LANES),
            shape(size, blocks),
            shape(*design.shape, dtype=bf16),
        ),
        in_specs=[HBM] * 7,
        out_specs=(VMEM,) * 7,
        scratch_shapes=[
            pltpu.VMEM((1, blocks), jnp.int32),
            pltpu.VMEM((blocks // LANES, LANES), jnp.int32),
            pltpu.VMEM((share, LANES), jnp.int32),
            pltpu.VMEM((size, group_count), f32),
            pltpu.VMEM((size, covs * size), f32),
            pltpu.SemaphoreType.DMA((7,)),
        ],
        compiler_params=ROOM,
        cost_estimate=cost(10_000_000, 5_000_000),
        name="select",
    )(
        *(
            pltpu.with_memory_space_constraint(x, pltpu.HBM)
            for x in (
                block_group.reshape(1, blocks),
                block_fill.reshape(blocks // LANES, LANES),
                outcome,
                fixed_coef.reshape(1, size),
                slopes,
                precision,
                design,
            )
        ),
    )

    partial = pl.pallas_call(
        predict_kernel,
        out_shape=shape(NEAR, share + slope_rows + size, LANES),
        in_specs=[VMEM] * 7,
        out_specs=VMEM,
        scratch_shapes=[pltpu.VMEM((blocks, size), f32)],
        compiler_params=ROOM,
        name="predict",
    )(from_even, from_odd, own_coefs, fixed_row, hot, design_here, prior_rows)

    received = exchange(partial, "cov", near_groups)
    spread = pl.pallas_call(
        gather_kernel,
        out_shape=shape(far, share + slope_rows, LANES),
        in_specs=[VMEM],
        out_specs=VMEM,
        scratch_shapes=[pltpu.VMEM((LANES, group_count), f32)],
        compiler_params=ROOM,
        name="gather",
    )(received)
    received = exchange(spread, "cov", far_groups)
    spread, prior = pl.pallas_call(
        residual_kernel,
        out_shape=(shape(NEAR, share, LANES), shape(slope_rows, LANES)),
        in_specs=[VMEM] * 3,
        out_specs=(VMEM, VMEM),
        compiler_params=ROOM,
        name="residual",
    )(received, label, valid)
    back = exchange(spread, "cov", near_groups)

    fixed_parts, grads = pl.pallas_call(
        gradient_kernel,
        out_shape=(shape(rows, 2, LANES), shape(blocks, LANES)),
        in_specs=[VMEM] * 2,
        out_specs=(VMEM,) * 2,
        compiler_params=ROOM,
        name="gradient",
    )(design_here, back)
    fixed_all = exchange(fixed_parts, "rows")

    to_even, to_odd, own = pl.pallas_call(
        group_kernel,
        out_shape=(shape(size, group_count),) * 3,
        in_specs=[VMEM] * 3,
        out_specs=(VMEM,) * 3,
        compiler_params=ROOM,
        cost_estimate=cost(100_000_000, 5_000_000),
        name="group",
    )(grads, hot, prior)
    given_even = swap(to_even, "rows", 0)
    given_odd = swap(to_odd, "rows", 1)

    fixed_grad, slope_grad = pl.pallas_call(
        finish_kernel,
        out_shape=(shape(1, size), shape(size, group_count)),
        in_specs=[VMEM] * 5,
        out_specs=(VMEM, VMEM),
        compiler_params=ROOM,
        name="finish",
    )(fixed_all, fixed_row, own, given_even, given_odd)
    return (fixed_grad.reshape(size), slope_grad)


def solution(mesh):
    return jax.shard_map(
        body,
        mesh=mesh,
        in_specs=(
            P("cov", "rows", None),
            P("rows", None),
            P("rows"),
            P("rows"),
            P("cov"),
            P("cov", "rows"),
            P("cov", None),
        ),
        out_specs=(P("cov"), P("cov", "rows")),
        check_vma=False,
    )
```

```python
import jax
import jax.numpy as jnp
from jax import lax
from jax.experimental import pallas as pl
from jax.experimental.pallas import tpu as pltpu
from jax.sharding import PartitionSpec as P

f32 = jnp.float32
bf16 = jnp.bfloat16
VMEM = pl.BlockSpec(memory_space=pltpu.VMEM)
HBM = pl.BlockSpec(memory_space=pltpu.HBM)
LANES = 128
NEAR = 4
ROOM = pltpu.CompilerParams(vmem_limit_bytes=16 << 20)


def swap(shard, axis, first):
    peers = lax.axis_size(axis)
    pairs = [(i, i + 1) for i in range(first, peers - 1, 2)]
    return lax.ppermute(shard, axis, pairs + [(j, i) for i, j in pairs])


def place_along_cov():
    shift = lax.rem(lax.axis_index("rows"), 2) * (NEAR // 2)
    covs = lax.axis_size("cov")
    return lax.rem(lax.axis_index("cov") + covs - shift, covs), shift


def cov_groups():
    covs, rows = lax.axis_size("cov"), lax.axis_size("rows")
    near, far = [], []
    for row in range(rows):
        members = [row * covs + (c + row % 2 * (NEAR // 2)) % covs for c in range(covs)]
        near += [members[i : i + NEAR] for i in range(0, covs, NEAR)]
        far += [members[j::NEAR] for j in range(NEAR)]
    return near, far


def exchange(parts, axis, groups=None):
    return lax.all_to_all(parts, axis, 0, 0, tiled=True, axis_index_groups=groups)


def cost(flops, size):
    return pl.CostEstimate(flops=flops, bytes_accessed=size, transcendentals=0)


def three_parts(x):
    a = x.astype(bf16)
    rest = x - a.astype(f32)
    b = rest.astype(bf16)
    c = (rest - b.astype(f32)).astype(bf16)
    return jnp.concatenate([a, b, c], axis=0)


def add_parts(x):
    size = x.shape[0] // 3
    return x[:size] + x[size : 2 * size] + x[2 * size :]


def in_rows(x):
    return jnp.concatenate([x[:, at : at + LANES] for at in range(0, x.shape[1], LANES)], axis=0)


def select_kernel(
    group_hbm, fill_hbm, outcome_hbm, fixed_hbm, slopes_hbm, precision_hbm, design_hbm,
    hot_ref, label_ref, valid_ref, fixed_ref, prior_ref, coef_ref, design_ref,
    group_ref, fill_ref, outcome_ref, own_ref, precision_ref, sems,
):
    window, blocks = hot_ref.shape
    rows = label_ref.shape[0]
    size, groups = own_ref.shape
    place, shift = place_along_cov()
    near = lax.rem(place, NEAR)
    start = pl.multiple_of(near * rows, rows)
    copies = [
        pltpu.make_async_copy(group_hbm, group_ref, sems.at[0]),
        pltpu.make_async_copy(slopes_hbm, own_ref, sems.at[1]),
        pltpu.make_async_copy(precision_hbm, precision_ref, sems.at[2]),
        pltpu.make_async_copy(outcome_hbm.at[pl.ds(start, rows)], outcome_ref, sems.at[3]),
        pltpu.make_async_copy(fill_hbm, fill_ref, sems.at[4]),
        pltpu.make_async_copy(fixed_hbm, fixed_ref, sems.at[5]),
        pltpu.make_async_copy(design_hbm, design_ref, sems.at[6]),
    ]
    for copy in copies:
        copy.start()
    for copy in copies[:2]:
        copy.wait()
    index = group_ref[...] - (lax.axis_index("rows") - 1) * groups
    for piece in range(0, window, groups):
        ids = lax.broadcasted_iota(jnp.int32, (groups, blocks), 0) + piece
        hot_ref[piece : piece + groups, :] = (ids == index).astype(f32).astype(bf16)
    own = own_ref[...]
    coef_ref[...] = add_parts(
        jnp.dot(three_parts(own), hot_ref[groups : 2 * groups, :], preferred_element_type=f32)
    )
    for copy in copies[2:6]:
        copy.wait()
    slope_rows = in_rows(own)
    precision = precision_ref[...]
    columns = lax.rem(lax.broadcasted_iota(jnp.int32, (size, LANES), 1) // size, NEAR)
    for peer in range(NEAR):
        kept = [
            jnp.where(columns == lax.rem(peer + shift, NEAR), precision[:, at : at + LANES], 0.0)
            for at in range(0, precision.shape[1], LANES)
        ]
        prior_ref[peer, : slope_rows.shape[0], :] = slope_rows
        prior_ref[peer, slope_rows.shape[0] :, :] = kept[0] + pltpu.roll(kept[1], size, 1)
    fill = fill_ref[pl.ds(near, 1), :].astype(f32)
    column = jnp.broadcast_to(fill, (rows, rows)).T
    lane = lax.broadcasted_iota(jnp.int32, (rows, LANES), 1).astype(f32)
    valid_ref[...] = (lane < column).astype(f32)
    label_ref[...] = outcome_ref[...].astype(f32)
    copies[6].wait()


def predict_kernel(
    even_ref, odd_ref, own_coef_ref, fixed_ref, hot_ref, design_ref, prior_ref, out_ref, coef_ref
):
    size, groups = even_ref.shape
    blocks = hot_ref.shape[1]
    share = blocks // NEAR
    parity = lax.rem(lax.axis_index("rows"), 2)
    coefs = own_coef_ref[...]
    for ref, place in ((even_ref, 1 - parity), (odd_ref, parity)):
        piece = hot_ref[pl.ds(pl.multiple_of(place * 2 * groups, groups), groups), :]
        coefs += add_parts(jnp.dot(three_parts(ref[...]), piece, preferred_element_type=f32))
    padded = jnp.concatenate([coefs, jnp.zeros((LANES - size, blocks), f32)], axis=0)
    coef_ref[...] = padded.T[:, :size] + fixed_ref[...]

    def chunk(peer, carry):
        start = pl.multiple_of(peer * share, share)
        here = coef_ref[pl.ds(start, share), :]
        total = jnp.zeros((share, LANES), f32)
        for p in range(size):
            total = total + here[:, p : p + 1] * design_ref[p, pl.ds(start, share), :].astype(f32)
        out_ref[peer, :share, :] = total
        out_ref[peer, share:, :] = prior_ref[peer]
        return carry

    lax.fori_loop(0, NEAR, chunk, 0)


def gather_kernel(parts_ref, out_ref, prior_ref):
    groups = prior_ref.shape[1]
    halves = groups // LANES
    size = (parts_ref.shape[1] - out_ref.shape[1])
    rows = out_ref.shape[1] - size * halves
    far = out_ref.shape[0]
    total = jnp.sum(parts_ref[:, :rows, :], axis=0)
    columns = [
        parts_ref[:, at : at + size, :].reshape(-1, LANES)
        for at in range(rows, parts_ref.shape[1], size)
    ]
    prior_ref[...] = lax.dot_general(
        columns[halves],
        jnp.concatenate(columns[:halves], axis=1),
        (((0,), (0,)), ((), ())),
        precision=lax.Precision.HIGHEST,
        preferred_element_type=f32,
    )
    place, shift = place_along_cov()
    near = lax.rem(place, NEAR)
    pieces = LANES // size
    for i in range(far):
        cov = lax.rem(i * NEAR + near + shift, far * NEAR)
        piece = lax.rem(lax.rem(cov, pieces) + cov // pieces, pieces)
        out_ref[i, :rows, :] = total
        part = prior_ref[pl.ds(pl.multiple_of(piece * size, size), size), :]
        out_ref[i, rows:, :] = in_rows(part)


def residual_kernel(parts_ref, label_ref, valid_ref, out_ref, prior_ref):
    rows = label_ref.shape[0]
    logits = jnp.sum(parts_ref[:, :rows, :], axis=0)
    residual = jnp.where(valid_ref[...] > 0.5, label_ref[...] - jax.nn.sigmoid(logits), 0.0)
    out_ref[...] = jnp.broadcast_to(residual[None], out_ref.shape)
    prior_ref[...] = jnp.sum(parts_ref[:, rows:, :], axis=0)


def gradient_kernel(design_ref, back_ref, fixed_ref, grad_ref):
    size, blocks, _ = design_ref.shape
    share = blocks // NEAR
    lane = lax.broadcasted_iota(jnp.int32, (share, LANES), 1)

    def chunk(peer, total):
        start = pl.multiple_of(peer * share, share)
        residual = back_ref[peer]
        grads = jnp.zeros((share, LANES), f32)
        for p in range(size):
            product = design_ref[p, pl.ds(start, share), :].astype(f32) * residual
            grads = jnp.where(lane == p, jnp.sum(product, axis=1, keepdims=True), grads)
        grad_ref[pl.ds(start, share), :] = grads
        return total + jnp.sum(grads, axis=0, keepdims=True)

    total = lax.fori_loop(0, NEAR, chunk, jnp.zeros((1, LANES), f32))
    fixed_ref[...] = jnp.broadcast_to(total[None], fixed_ref.shape)


def group_kernel(grad_ref, hot_ref, prior_ref, even_ref, odd_ref, own_ref):
    size, groups = own_ref.shape
    parts = three_parts(grad_ref[...].T[:size])
    sums = add_parts(
        lax.dot_general(parts, hot_ref[...], (((1,), (1,)), ((), ())), preferred_element_type=f32)
    )
    lower, upper = sums[:, :groups], sums[:, 2 * groups :]
    odd = lax.rem(lax.axis_index("rows"), 2) == 1
    even_ref[...] = jnp.where(odd, lower, upper)
    odd_ref[...] = jnp.where(odd, upper, lower)
    halves = [prior_ref[at : at + size, :] for at in range(0, prior_ref.shape[0], size)]
    own_ref[...] = sums[:, groups : 2 * groups] - jnp.concatenate(halves, axis=1)


def finish_kernel(fixed_all_ref, fixed_ref, own_ref, even_ref, odd_ref, fixed_out, slope_out):
    size = fixed_ref.shape[1]
    fixed_out[...] = jnp.sum(fixed_all_ref[...], axis=0)[:1, :size] - fixed_ref[...]
    slope_out[...] = own_ref[...] + even_ref[...] + odd_ref[...]


def shape(*dims, dtype=f32):
    return jax.ShapeDtypeStruct(dims, dtype)


def body(design, outcome, block_fill, block_group, fixed_coef, slopes, precision):
    size, group_count = slopes.shape
    blocks = block_group.shape[0]
    covs, rows = lax.axis_size("cov"), lax.axis_size("rows")
    far = covs // NEAR
    share = blocks // NEAR
    near_groups, far_groups = cov_groups()
    slope_rows = size * group_count // LANES

    from_even = swap(slopes, "rows", 0)
    from_odd = swap(slopes, "rows", 1)

    hot, label, valid, fixed_row, prior_rows, own_coefs, design_here = pl.pallas_call(
        select_kernel,
        out_shape=(
            shape(3 * group_count, blocks, dtype=bf16),
            shape(share, LANES),
            shape(share, LANES),
            shape(1, size),
            shape(NEAR, slope_rows + size, LANES),
            shape(size, blocks),
            shape(*design.shape, dtype=bf16),
        ),
        in_specs=[HBM] * 7,
        out_specs=(VMEM,) * 7,
        scratch_shapes=[
            pltpu.VMEM((1, blocks), jnp.int32),
            pltpu.VMEM((blocks // LANES, LANES), jnp.int32),
            pltpu.VMEM((share, LANES), jnp.int32),
            pltpu.VMEM((size, group_count), f32),
            pltpu.VMEM((size, covs * size), f32),
            pltpu.SemaphoreType.DMA((7,)),
        ],
        compiler_params=ROOM,
        cost_estimate=cost(10_000_000, 5_000_000),
        name="select",
    )(
        *(
            pltpu.with_memory_space_constraint(x, pltpu.HBM)
            for x in (
                block_group.reshape(1, blocks),
                block_fill.reshape(blocks // LANES, LANES),
                outcome,
                fixed_coef.reshape(1, size),
                slopes,
                precision,
                design,
            )
        ),
    )

    partial = pl.pallas_call(
        predict_kernel,
        out_shape=shape(NEAR, share + slope_rows + size, LANES),
        in_specs=[VMEM] * 7,
        out_specs=VMEM,
        scratch_shapes=[pltpu.VMEM((blocks, size), f32)],
        compiler_params=ROOM,
        name="predict",
    )(from_even, from_odd, own_coefs, fixed_row, hot, design_here, prior_rows)

    received = exchange(partial, ("rows", "cov"), near_groups)
    spread = pl.pallas_call(
        gather_kernel,
        out_shape=shape(far, share + slope_rows, LANES),
        in_specs=[VMEM],
        out_specs=VMEM,
        scratch_shapes=[pltpu.VMEM((LANES, group_count), f32)],
        compiler_params=ROOM,
        name="gather",
    )(received)
    received = exchange(spread, ("rows", "cov"), far_groups)
    spread, prior = pl.pallas_call(
        residual_kernel,
        out_shape=(shape(NEAR, share, LANES), shape(slope_rows, LANES)),
        in_specs=[VMEM] * 3,
        out_specs=(VMEM, VMEM),
        compiler_params=ROOM,
        name="residual",
    )(received, label, valid)
    back = exchange(spread, ("rows", "cov"), near_groups)

    fixed_parts, grads = pl.pallas_call(
        gradient_kernel,
        out_shape=(shape(rows, 2, LANES), shape(blocks, LANES)),
        in_specs=[VMEM] * 2,
        out_specs=(VMEM,) * 2,
        compiler_params=ROOM,
        name="gradient",
    )(design_here, back)
    fixed_all = exchange(fixed_parts, "rows")

    to_even, to_odd, own = pl.pallas_call(
        group_kernel,
        out_shape=(shape(size, group_count),) * 3,
        in_specs=[VMEM] * 3,
        out_specs=(VMEM,) * 3,
        compiler_params=ROOM,
        cost_estimate=cost(100_000_000, 5_000_000),
        name="group",
    )(grads, hot, prior)
    given_even = swap(to_even, "rows", 0)
    given_odd = swap(to_odd, "rows", 1)

    fixed_grad, slope_grad = pl.pallas_call(
        finish_kernel,
        out_shape=(shape(1, size), shape(size, group_count)),
        in_specs=[VMEM] * 5,
        out_specs=(VMEM, VMEM),
        compiler_params=ROOM,
        name="finish",
    )(fixed_all, fixed_row, own, given_even, given_odd)
    return (fixed_grad.reshape(size), slope_grad)


def solution(mesh):
    return jax.shard_map(
        body,
        mesh=mesh,
        in_specs=(
            P("cov", "rows", None),
            P("rows", None),
            P("rows"),
            P("rows"),
            P("cov"),
            P("cov", "rows"),
            P("cov", None),
        ),
        out_specs=(P("cov"), P("cov", "rows")),
        check_vma=False,
    )
```

```python
import jax
import jax.numpy as jnp
from jax import lax
from jax.experimental import pallas as pl
from jax.experimental.pallas import tpu as pltpu
from jax.sharding import PartitionSpec as P

f32 = jnp.float32
bf16 = jnp.bfloat16
VMEM = pl.BlockSpec(memory_space=pltpu.VMEM)
HBM = pl.BlockSpec(memory_space=pltpu.HBM)
LANES = 128
NEAR = 4
ROOM = pltpu.CompilerParams(vmem_limit_bytes=16 << 20)


def swap(shard, axis, first):
    peers = lax.axis_size(axis)
    pairs = [(i, i + 1) for i in range(first, peers - 1, 2)]
    return lax.ppermute(shard, axis, pairs + [(j, i) for i, j in pairs])


def place_along_cov():
    shift = lax.rem(lax.axis_index("rows"), 2) * (NEAR // 2)
    covs = lax.axis_size("cov")
    return lax.rem(lax.axis_index("cov") + covs - shift, covs), shift


def cov_groups():
    covs, rows = lax.axis_size("cov"), lax.axis_size("rows")
    near, far = [], []
    for row in range(rows):
        members = [row * covs + (c + row % 2 * (NEAR // 2)) % covs for c in range(covs)]
        near += [members[i : i + NEAR] for i in range(0, covs, NEAR)]
        far += [members[j::NEAR] for j in range(NEAR)]
    return near, far


def exchange(parts, axis, groups=None):
    return lax.all_to_all(parts, axis, 0, 0, tiled=True, axis_index_groups=groups)


def cost(flops, size):
    return pl.CostEstimate(flops=flops, bytes_accessed=size, transcendentals=0)


def three_parts(x):
    a = x.astype(bf16)
    rest = x - a.astype(f32)
    b = rest.astype(bf16)
    c = (rest - b.astype(f32)).astype(bf16)
    return jnp.concatenate([a, b, c], axis=0)


def add_parts(x):
    size = x.shape[0] // 3
    return x[:size] + x[size : 2 * size] + x[2 * size :]


def in_rows(x):
    return jnp.concatenate([x[:, at : at + LANES] for at in range(0, x.shape[1], LANES)], axis=0)


def select_kernel(
    group_hbm, fill_hbm, outcome_hbm, fixed_hbm, slopes_hbm, precision_hbm, design_hbm,
    hot_ref, label_ref, valid_ref, fixed_ref, prior_ref, coef_ref, spread_ref, design_ref,
    group_ref, fill_ref, outcome_ref, own_ref, precision_ref, sems,
):
    window, blocks = hot_ref.shape
    rows = label_ref.shape[0]
    size, groups = own_ref.shape
    place, shift = place_along_cov()
    near = lax.rem(place, NEAR)
    start = pl.multiple_of(near * rows, rows)
    copies = [
        pltpu.make_async_copy(group_hbm, group_ref, sems.at[0]),
        pltpu.make_async_copy(slopes_hbm, own_ref, sems.at[1]),
        pltpu.make_async_copy(precision_hbm, precision_ref, sems.at[2]),
        pltpu.make_async_copy(outcome_hbm.at[pl.ds(start, rows)], outcome_ref, sems.at[3]),
        pltpu.make_async_copy(fill_hbm, fill_ref, sems.at[4]),
        pltpu.make_async_copy(fixed_hbm, fixed_ref, sems.at[5]),
        pltpu.make_async_copy(design_hbm, design_ref, sems.at[6]),
    ]
    for copy in copies:
        copy.start()
    for copy in copies[:2]:
        copy.wait()
    index = group_ref[...] - (lax.axis_index("rows") - 1) * groups
    for piece in range(0, window, groups):
        ids = lax.broadcasted_iota(jnp.int32, (groups, blocks), 0) + piece
        hot_ref[piece : piece + groups, :] = (ids == index).astype(f32).astype(bf16)
    own = own_ref[...]
    coef_ref[...] = add_parts(
        jnp.dot(three_parts(own), hot_ref[groups : 2 * groups, :], preferred_element_type=f32)
    )
    for copy in copies[2:6]:
        copy.wait()
    across = lax.broadcasted_iota(jnp.int32, (size, size), 0)
    along = lax.broadcasted_iota(jnp.int32, (size, size), 1)
    fixed = jnp.where(across == along, jnp.broadcast_to(fixed_ref[...], (size, size)), 0.0)
    coef_ref[...] += jnp.sum(fixed, axis=1, keepdims=True)
    part = lax.broadcasted_iota(jnp.int32, (LANES, LANES), 0)
    for p in range(size):
        ones = (lax.rem(part, size) == p) & (part < 3 * size)
        spread_ref[:, p * LANES : (p + 1) * LANES] = ones.astype(f32).astype(bf16)
    slope_rows = in_rows(own)
    precision = precision_ref[...]
    columns = lax.rem(lax.broadcasted_iota(jnp.int32, (size, LANES), 1) // size, NEAR)
    for peer in range(NEAR):
        kept = [
            jnp.where(columns == lax.rem(peer + shift, NEAR), precision[:, at : at + LANES], 0.0)
            for at in range(0, precision.shape[1], LANES)
        ]
        prior_ref[peer, : slope_rows.shape[0], :] = slope_rows
        prior_ref[peer, slope_rows.shape[0] :, :] = kept[0] + pltpu.roll(kept[1], size, 1)
    fill = fill_ref[pl.ds(near, 1), :].astype(f32)
    column = jnp.broadcast_to(fill, (rows, rows)).T
    lane = lax.broadcasted_iota(jnp.int32, (rows, LANES), 1).astype(f32)
    valid_ref[...] = (lane < column).astype(f32)
    label_ref[...] = outcome_ref[...].astype(f32)
    copies[6].wait()


def predict_kernel(
    even_ref, odd_ref, own_coef_ref, hot_ref, spread_ref, design_ref, prior_ref, out_ref, coef_ref
):
    size, groups = even_ref.shape
    blocks = hot_ref.shape[1]
    share = blocks // NEAR
    parity = lax.rem(lax.axis_index("rows"), 2)
    coefs = own_coef_ref[...]
    for ref, place in ((even_ref, 1 - parity), (odd_ref, parity)):
        piece = hot_ref[pl.ds(pl.multiple_of(place * 2 * groups, groups), groups), :]
        coefs += add_parts(jnp.dot(three_parts(ref[...]), piece, preferred_element_type=f32))
    parts = three_parts(coefs).astype(f32)
    padded = jnp.concatenate([parts, jnp.zeros((LANES - 3 * size, blocks), f32)], axis=0)
    coef_ref[...] = padded.T.astype(bf16)

    def chunk(peer, carry):
        start = pl.multiple_of(peer * share, share)
        here = coef_ref[pl.ds(start, share), :]
        total = jnp.zeros((share, LANES), f32)
        for p in range(0, size, 2):
            wide = jnp.dot(
                here, spread_ref[:, p * LANES : (p + 2) * LANES], preferred_element_type=f32
            )
            total = total + wide[:, :LANES] * design_ref[p, pl.ds(start, share), :].astype(f32)
            total = total + wide[:, LANES:] * design_ref[p + 1, pl.ds(start, share), :].astype(f32)
        out_ref[peer, :share, :] = total
        out_ref[peer, share:, :] = prior_ref[peer]
        return carry

    lax.fori_loop(0, NEAR, chunk, 0)


def gather_kernel(parts_ref, out_ref, prior_ref):
    groups = prior_ref.shape[1]
    halves = groups // LANES
    size = (parts_ref.shape[1] - out_ref.shape[1])
    rows = out_ref.shape[1] - size * halves
    far = out_ref.shape[0]
    total = jnp.sum(parts_ref[:, :rows, :], axis=0)
    columns = [
        parts_ref[:, at : at + size, :].reshape(-1, LANES)
        for at in range(rows, parts_ref.shape[1], size)
    ]
    prior_ref[...] = lax.dot_general(
        columns[halves],
        jnp.concatenate(columns[:halves], axis=1),
        (((0,), (0,)), ((), ())),
        precision=lax.Precision.HIGHEST,
        preferred_element_type=f32,
    )
    place, shift = place_along_cov()
    near = lax.rem(place, NEAR)
    pieces = LANES // size
    for i in range(far):
        cov = lax.rem(i * NEAR + near + shift, far * NEAR)
        piece = lax.rem(lax.rem(cov, pieces) + cov // pieces, pieces)
        out_ref[i, :rows, :] = total
        part = prior_ref[pl.ds(pl.multiple_of(piece * size, size), size), :]
        out_ref[i, rows:, :] = in_rows(part)


def residual_kernel(parts_ref, label_ref, valid_ref, out_ref, prior_ref):
    rows = label_ref.shape[0]
    logits = jnp.sum(parts_ref[:, :rows, :], axis=0)
    residual = jnp.where(valid_ref[...] > 0.5, label_ref[...] - jax.nn.sigmoid(logits), 0.0)
    out_ref[...] = jnp.broadcast_to(residual[None], out_ref.shape)
    prior_ref[...] = jnp.sum(parts_ref[:, rows:, :], axis=0)


def fixed_kernel(design_ref, back_ref, fixed_ref):
    size, blocks, _ = design_ref.shape
    share = blocks // NEAR
    step = 64

    def chunk(i, totals):
        start = pl.multiple_of(i * step, step)
        inner = pl.multiple_of(lax.rem(start, share), step)
        residual = back_ref[start // share, pl.ds(inner, step), :]
        new = []
        for p in range(size):
            product = design_ref[p, pl.ds(start, step), :].astype(f32) * residual
            new.append(totals[p] + jnp.sum(product.reshape(step // 8, 8, LANES), axis=0))
        return tuple(new)

    zero = jnp.zeros((8, LANES), f32)
    totals = lax.fori_loop(0, blocks // step, chunk, (zero,) * size)
    lane = lax.broadcasted_iota(jnp.int32, (8, LANES), 1)
    row = zero
    for p in range(size):
        row = jnp.where(lane == p, jnp.sum(totals[p], axis=1, keepdims=True), row)
    row = jnp.sum(row, axis=0, keepdims=True)
    fixed_ref[...] = jnp.broadcast_to(row[None], fixed_ref.shape)


def group_kernel(design_ref, back_ref, hot_ref, prior_ref, even_ref, odd_ref, own_ref, grad_ref):
    size, groups = own_ref.shape
    blocks = design_ref.shape[1]
    share = blocks // NEAR
    lane = lax.broadcasted_iota(jnp.int32, (share, LANES), 1)

    def chunk(peer, carry):
        start = pl.multiple_of(peer * share, share)
        residual = back_ref[peer]
        grads = jnp.zeros((share, LANES), f32)
        for p in range(size):
            product = design_ref[p, pl.ds(start, share), :].astype(f32) * residual
            grads = jnp.where(lane == p, jnp.sum(product, axis=1, keepdims=True), grads)
        grad_ref[pl.ds(start, share), :] = grads
        return carry

    lax.fori_loop(0, NEAR, chunk, 0)
    parts = three_parts(grad_ref[...].T[:size])
    sums = add_parts(
        lax.dot_general(parts, hot_ref[...], (((1,), (1,)), ((), ())), preferred_element_type=f32)
    )
    lower, upper = sums[:, :groups], sums[:, 2 * groups :]
    odd = lax.rem(lax.axis_index("rows"), 2) == 1
    even_ref[...] = jnp.where(odd, lower, upper)
    odd_ref[...] = jnp.where(odd, upper, lower)
    halves = [prior_ref[at : at + size, :] for at in range(0, prior_ref.shape[0], size)]
    own_ref[...] = sums[:, groups : 2 * groups] - jnp.concatenate(halves, axis=1)


def finish_kernel(fixed_all_ref, fixed_ref, own_ref, even_ref, odd_ref, fixed_out, slope_out):
    size = fixed_ref.shape[1]
    fixed_out[...] = jnp.sum(fixed_all_ref[...], axis=0)[:1, :size] - fixed_ref[...]
    slope_out[...] = own_ref[...] + even_ref[...] + odd_ref[...]


def shape(*dims, dtype=f32):
    return jax.ShapeDtypeStruct(dims, dtype)


def body(design, outcome, block_fill, block_group, fixed_coef, slopes, precision):
    size, group_count = slopes.shape
    blocks = block_group.shape[0]
    covs, rows = lax.axis_size("cov"), lax.axis_size("rows")
    far = covs // NEAR
    share = blocks // NEAR
    near_groups, far_groups = cov_groups()
    slope_rows = size * group_count // LANES

    from_even = swap(slopes, "rows", 0)
    from_odd = swap(slopes, "rows", 1)

    hot, label, valid, fixed_row, prior_rows, own_coefs, spread_hot, design_here = pl.pallas_call(
        select_kernel,
        out_shape=(
            shape(3 * group_count, blocks, dtype=bf16),
            shape(share, LANES),
            shape(share, LANES),
            shape(1, size),
            shape(NEAR, slope_rows + size, LANES),
            shape(size, blocks),
            shape(LANES, size * LANES, dtype=bf16),
            shape(*design.shape, dtype=bf16),
        ),
        in_specs=[HBM] * 7,
        out_specs=(VMEM,) * 8,
        scratch_shapes=[
            pltpu.VMEM((1, blocks), jnp.int32),
            pltpu.VMEM((blocks // LANES, LANES), jnp.int32),
            pltpu.VMEM((share, LANES), jnp.int32),
            pltpu.VMEM((size, group_count), f32),
            pltpu.VMEM((size, covs * size), f32),
            pltpu.SemaphoreType.DMA((7,)),
        ],
        compiler_params=ROOM,
        cost_estimate=cost(10_000_000, 5_000_000),
        name="select",
    )(
        *(
            pltpu.with_memory_space_constraint(x, pltpu.HBM)
            for x in (
                block_group.reshape(1, blocks),
                block_fill.reshape(blocks // LANES, LANES),
                outcome,
                fixed_coef.reshape(1, size),
                slopes,
                precision,
                design,
            )
        ),
    )

    partial = pl.pallas_call(
        predict_kernel,
        out_shape=shape(NEAR, share + slope_rows + size, LANES),
        in_specs=[VMEM] * 7,
        out_specs=VMEM,
        scratch_shapes=[pltpu.VMEM((blocks, LANES), bf16)],
        compiler_params=ROOM,
        name="predict",
    )(from_even, from_odd, own_coefs, hot, spread_hot, design_here, prior_rows)

    received = exchange(partial, ("rows", "cov"), near_groups)
    spread = pl.pallas_call(
        gather_kernel,
        out_shape=shape(far, share + slope_rows, LANES),
        in_specs=[VMEM],
        out_specs=VMEM,
        scratch_shapes=[pltpu.VMEM((LANES, group_count), f32)],
        compiler_params=ROOM,
        name="gather",
    )(received)
    received = exchange(spread, ("rows", "cov"), far_groups)
    spread, prior = pl.pallas_call(
        residual_kernel,
        out_shape=(shape(NEAR, share, LANES), shape(slope_rows, LANES)),
        in_specs=[VMEM] * 3,
        out_specs=(VMEM, VMEM),
        compiler_params=ROOM,
        name="residual",
    )(received, label, valid)
    back = exchange(spread, ("rows", "cov"), near_groups)

    fixed_parts = pl.pallas_call(
        fixed_kernel,
        out_shape=shape(rows, 2, LANES),
        in_specs=[VMEM] * 2,
        out_specs=VMEM,
        compiler_params=ROOM,
        name="fixed",
    )(design_here, back)
    fixed_all = exchange(fixed_parts, "rows")

    to_even, to_odd, own = pl.pallas_call(
        group_kernel,
        out_shape=(shape(size, group_count),) * 3,
        in_specs=[VMEM] * 4,
        out_specs=(VMEM,) * 3,
        scratch_shapes=[pltpu.VMEM((blocks, LANES), f32)],
        compiler_params=ROOM,
        cost_estimate=cost(100_000_000, 5_000_000),
        name="group",
    )(design_here, back, hot, prior)
    given_even = swap(to_even, "rows", 0)
    given_odd = swap(to_odd, "rows", 1)

    fixed_grad, slope_grad = pl.pallas_call(
        finish_kernel,
        out_shape=(shape(1, size), shape(size, group_count)),
        in_specs=[VMEM] * 5,
        out_specs=(VMEM, VMEM),
        compiler_params=ROOM,
        name="finish",
    )(fixed_all, fixed_row, own, given_even, given_odd)
    return (fixed_grad.reshape(size), slope_grad)


def solution(mesh):
    return jax.shard_map(
        body,
        mesh=mesh,
        in_specs=(
            P("cov", "rows", None),
            P("rows", None),
            P("rows"),
            P("rows"),
            P("cov"),
            P("cov", "rows"),
            P("cov", None),
        ),
        out_specs=(P("cov"), P("cov", "rows")),
        check_vma=False,
    )
```

```python
import jax
import jax.numpy as jnp
from jax import lax
from jax.experimental import pallas as pl
from jax.experimental.pallas import tpu as pltpu
from jax.sharding import PartitionSpec as P

f32 = jnp.float32
bf16 = jnp.bfloat16
VMEM = pl.BlockSpec(memory_space=pltpu.VMEM)
HBM = pl.BlockSpec(memory_space=pltpu.HBM)
LANES = 128
NEAR = 4
ROOM = pltpu.CompilerParams(vmem_limit_bytes=16 << 20)


def swap(shard, axis, first):
    peers = lax.axis_size(axis)
    pairs = [(i, i + 1) for i in range(first, peers - 1, 2)]
    return lax.ppermute(shard, axis, pairs + [(j, i) for i, j in pairs])


def place_along_cov():
    shift = lax.rem(lax.axis_index("rows"), 2) * (NEAR // 2)
    covs = lax.axis_size("cov")
    return lax.rem(lax.axis_index("cov") + covs - shift, covs), shift


def far_partners(i, odd):
    a, b = i + 1 - 2 * (i % 2), 3 - i
    return a + odd * (b - a), b + odd * (a - b)


def cov_groups():
    covs, rows = lax.axis_size("cov"), lax.axis_size("rows")
    near, first, second = [], [], []
    for row in range(rows):
        members = [row * covs + (c + row % 2 * (NEAR // 2)) % covs for c in range(covs)]
        near += [members[i : i + NEAR] for i in range(0, covs, NEAR)]
        for i in (0, 2):
            for pairs, partner in zip((first, second), far_partners(i, row % 2)):
                pairs += [[members[i * NEAR + j], members[partner * NEAR + j]] for j in range(NEAR)]
    return near, first, second


def exchange(parts, axis, groups=None):
    return lax.all_to_all(parts, axis, 0, 0, tiled=True, axis_index_groups=groups)


def cost(flops, size):
    return pl.CostEstimate(flops=flops, bytes_accessed=size, transcendentals=0)


def three_parts(x):
    a = x.astype(bf16)
    rest = x - a.astype(f32)
    b = rest.astype(bf16)
    c = (rest - b.astype(f32)).astype(bf16)
    return jnp.concatenate([a, b, c], axis=0)


def add_parts(x):
    size = x.shape[0] // 3
    return x[:size] + x[size : 2 * size] + x[2 * size :]


def in_rows(x):
    return jnp.concatenate([x[:, at : at + LANES] for at in range(0, x.shape[1], LANES)], axis=0)


def select_kernel(
    group_hbm, fill_hbm, outcome_hbm, fixed_hbm, slopes_hbm, precision_hbm, design_hbm,
    hot_ref, label_ref, valid_ref, fixed_ref, prior_ref, coef_ref, spread_ref, design_ref,
    group_ref, fill_ref, outcome_ref, own_ref, precision_ref, sems,
):
    window, blocks = hot_ref.shape
    rows = label_ref.shape[0]
    size, groups = own_ref.shape
    place, shift = place_along_cov()
    near = lax.rem(place, NEAR)
    start = pl.multiple_of(near * rows, rows)
    copies = [
        pltpu.make_async_copy(group_hbm, group_ref, sems.at[0]),
        pltpu.make_async_copy(slopes_hbm, own_ref, sems.at[1]),
        pltpu.make_async_copy(precision_hbm, precision_ref, sems.at[2]),
        pltpu.make_async_copy(outcome_hbm.at[pl.ds(start, rows)], outcome_ref, sems.at[3]),
        pltpu.make_async_copy(fill_hbm, fill_ref, sems.at[4]),
        pltpu.make_async_copy(fixed_hbm, fixed_ref, sems.at[5]),
        pltpu.make_async_copy(design_hbm, design_ref, sems.at[6]),
    ]
    for copy in copies:
        copy.start()
    for copy in copies[:2]:
        copy.wait()
    index = group_ref[...] - (lax.axis_index("rows") - 1) * groups
    for piece in range(0, window, groups):
        ids = lax.broadcasted_iota(jnp.int32, (groups, blocks), 0) + piece
        hot_ref[piece : piece + groups, :] = (ids == index).astype(f32).astype(bf16)
    own = own_ref[...]
    coef_ref[...] = add_parts(
        jnp.dot(three_parts(own), hot_ref[groups : 2 * groups, :], preferred_element_type=f32)
    )
    for copy in copies[2:6]:
        copy.wait()
    across = lax.broadcasted_iota(jnp.int32, (size, size), 0)
    along = lax.broadcasted_iota(jnp.int32, (size, size), 1)
    fixed = jnp.where(across == along, jnp.broadcast_to(fixed_ref[...], (size, size)), 0.0)
    coef_ref[...] += jnp.sum(fixed, axis=1, keepdims=True)
    part = lax.broadcasted_iota(jnp.int32, (LANES, LANES), 0)
    for p in range(size):
        ones = (lax.rem(part, size) == p) & (part < 3 * size)
        spread_ref[:, p * LANES : (p + 1) * LANES] = ones.astype(f32).astype(bf16)
    slope_rows = in_rows(own)
    precision = precision_ref[...]
    columns = lax.rem(lax.broadcasted_iota(jnp.int32, (size, LANES), 1) // size, NEAR)
    for peer in range(NEAR):
        kept = [
            jnp.where(columns == lax.rem(peer + shift, NEAR), precision[:, at : at + LANES], 0.0)
            for at in range(0, precision.shape[1], LANES)
        ]
        prior_ref[peer, : slope_rows.shape[0], :] = slope_rows
        prior_ref[peer, slope_rows.shape[0] :, :] = kept[0] + pltpu.roll(kept[1], size, 1)
    fill = fill_ref[pl.ds(near, 1), :].astype(f32)
    column = jnp.broadcast_to(fill, (rows, rows)).T
    lane = lax.broadcasted_iota(jnp.int32, (rows, LANES), 1).astype(f32)
    valid_ref[...] = (lane < column).astype(f32)
    label_ref[...] = outcome_ref[...].astype(f32)
    copies[6].wait()


def predict_kernel(
    even_ref, odd_ref, own_coef_ref, hot_ref, spread_ref, design_ref, prior_ref, out_ref, coef_ref
):
    size, groups = even_ref.shape
    blocks = hot_ref.shape[1]
    share = blocks // NEAR
    parity = lax.rem(lax.axis_index("rows"), 2)
    coefs = own_coef_ref[...]
    for ref, place in ((even_ref, 1 - parity), (odd_ref, parity)):
        piece = hot_ref[pl.ds(pl.multiple_of(place * 2 * groups, groups), groups), :]
        coefs += add_parts(jnp.dot(three_parts(ref[...]), piece, preferred_element_type=f32))
    parts = three_parts(coefs).astype(f32)
    padded = jnp.concatenate([parts, jnp.zeros((LANES - 3 * size, blocks), f32)], axis=0)
    coef_ref[...] = padded.T.astype(bf16)

    def chunk(peer, carry):
        start = pl.multiple_of(peer * share, share)
        here = coef_ref[pl.ds(start, share), :]
        total = jnp.zeros((share, LANES), f32)
        for p in range(0, size, 2):
            wide = jnp.dot(
                here, spread_ref[:, p * LANES : (p + 2) * LANES], preferred_element_type=f32
            )
            total = total + wide[:, :LANES] * design_ref[p, pl.ds(start, share), :].astype(f32)
            total = total + wide[:, LANES:] * design_ref[p + 1, pl.ds(start, share), :].astype(f32)
        out_ref[peer, :share, :] = total
        out_ref[peer, share:, :] = prior_ref[peer]
        return carry

    lax.fori_loop(0, NEAR, chunk, 0)


def gather_kernel(parts_ref, out_ref, prior_ref):
    groups = prior_ref.shape[1]
    halves = groups // LANES
    size = out_ref.shape[1] - parts_ref.shape[1]
    rows = parts_ref.shape[1] - size * (halves + 1)
    total = jnp.sum(parts_ref[:, :rows, :], axis=0)
    columns = [
        parts_ref[:, at : at + size, :].reshape(-1, LANES)
        for at in range(rows, parts_ref.shape[1], size)
    ]
    prior_ref[...] = lax.dot_general(
        columns[halves],
        jnp.concatenate(columns[:halves], axis=1),
        (((0,), (0,)), ((), ())),
        precision=lax.Precision.HIGHEST,
        preferred_element_type=f32,
    )
    place, shift = place_along_cov()
    near, group = lax.rem(place, NEAR), place // NEAR
    odd = lax.rem(lax.axis_index("rows"), 2)
    parity = lax.rem(group, 2)
    partner, _ = far_partners(group, odd)
    pieces = LANES // size
    for k in range(out_ref.shape[0]):
        target = jnp.where(parity == k, group, partner)
        _, beyond = far_partners(target, odd)
        out_ref[k, :rows, :] = total
        for at, member in ((rows, target), (rows + halves * size, beyond)):
            cov = lax.rem(member * NEAR + near + shift, lax.axis_size("cov"))
            piece = lax.rem(lax.rem(cov, pieces) + cov // pieces, pieces)
            part = prior_ref[pl.ds(pl.multiple_of(piece * size, size), size), :]
            out_ref[k, at : at + halves * size, :] = in_rows(part)


def relay_kernel(parts_ref, out_ref):
    rows = 2 * out_ref.shape[1] - parts_ref.shape[1]
    size = out_ref.shape[1] - rows
    total = jnp.sum(parts_ref[...], axis=0)
    place, _ = place_along_cov()
    parity = lax.rem(place // NEAR, 2)
    for k in range(out_ref.shape[0]):
        out_ref[k, :rows, :] = total[:rows]
        out_ref[k, rows:, :] = jnp.where(
            parity == k, total[rows : rows + size], total[rows + size :]
        )


def residual_kernel(parts_ref, label_ref, valid_ref, out_ref, prior_ref):
    rows = label_ref.shape[0]
    logits = jnp.sum(parts_ref[:, :rows, :], axis=0)
    residual = jnp.where(valid_ref[...] > 0.5, label_ref[...] - jax.nn.sigmoid(logits), 0.0)
    out_ref[...] = jnp.broadcast_to(residual[None], out_ref.shape)
    prior_ref[...] = jnp.sum(parts_ref[:, rows:, :], axis=0)


def gradient_kernel(design_ref, back_ref, fixed_ref, grad_ref):
    size, blocks, _ = design_ref.shape
    share = blocks // NEAR
    lane = lax.broadcasted_iota(jnp.int32, (share, LANES), 1)

    def chunk(peer, total):
        start = pl.multiple_of(peer * share, share)
        residual = back_ref[peer]
        grads = jnp.zeros((share, LANES), f32)
        for p in range(size):
            product = design_ref[p, pl.ds(start, share), :].astype(f32) * residual
            grads = jnp.where(lane == p, jnp.sum(product, axis=1, keepdims=True), grads)
        grad_ref[pl.ds(start, share), :] = grads
        return total + jnp.sum(grads, axis=0, keepdims=True)

    total = lax.fori_loop(0, NEAR, chunk, jnp.zeros((1, LANES), f32))
    fixed_ref[...] = jnp.broadcast_to(total[None], fixed_ref.shape)


def group_kernel(grad_ref, hot_ref, prior_ref, even_ref, odd_ref, own_ref):
    size, groups = own_ref.shape
    parts = three_parts(grad_ref[...].T[:size])
    sums = add_parts(
        lax.dot_general(parts, hot_ref[...], (((1,), (1,)), ((), ())), preferred_element_type=f32)
    )
    lower, upper = sums[:, :groups], sums[:, 2 * groups :]
    odd = lax.rem(lax.axis_index("rows"), 2) == 1
    even_ref[...] = jnp.where(odd, lower, upper)
    odd_ref[...] = jnp.where(odd, upper, lower)
    halves = [prior_ref[at : at + size, :] for at in range(0, prior_ref.shape[0], size)]
    own_ref[...] = sums[:, groups : 2 * groups] - jnp.concatenate(halves, axis=1)


def finish_kernel(fixed_all_ref, fixed_ref, own_ref, even_ref, odd_ref, fixed_out, slope_out):
    size = fixed_ref.shape[1]
    fixed_out[...] = jnp.sum(fixed_all_ref[...], axis=0)[:1, :size] - fixed_ref[...]
    slope_out[...] = own_ref[...] + even_ref[...] + odd_ref[...]


def shape(*dims, dtype=f32):
    return jax.ShapeDtypeStruct(dims, dtype)


def body(design, outcome, block_fill, block_group, fixed_coef, slopes, precision):
    size, group_count = slopes.shape
    blocks = block_group.shape[0]
    covs, rows = lax.axis_size("cov"), lax.axis_size("rows")
    share = blocks // NEAR
    near_groups, first_pairs, second_pairs = cov_groups()
    slope_rows = size * group_count // LANES

    from_even = swap(slopes, "rows", 0)
    from_odd = swap(slopes, "rows", 1)

    hot, label, valid, fixed_row, prior_rows, own_coefs, spread_hot, design_here = pl.pallas_call(
        select_kernel,
        out_shape=(
            shape(3 * group_count, blocks, dtype=bf16),
            shape(share, LANES),
            shape(share, LANES),
            shape(1, size),
            shape(NEAR, slope_rows + size, LANES),
            shape(size, blocks),
            shape(LANES, size * LANES, dtype=bf16),
            shape(*design.shape, dtype=bf16),
        ),
        in_specs=[HBM] * 7,
        out_specs=(VMEM,) * 8,
        scratch_shapes=[
            pltpu.VMEM((1, blocks), jnp.int32),
            pltpu.VMEM((blocks // LANES, LANES), jnp.int32),
            pltpu.VMEM((share, LANES), jnp.int32),
            pltpu.VMEM((size, group_count), f32),
            pltpu.VMEM((size, covs * size), f32),
            pltpu.SemaphoreType.DMA((7,)),
        ],
        compiler_params=ROOM,
        cost_estimate=cost(10_000_000, 5_000_000),
        name="select",
    )(
        *(
            pltpu.with_memory_space_constraint(x, pltpu.HBM)
            for x in (
                block_group.reshape(1, blocks),
                block_fill.reshape(blocks // LANES, LANES),
                outcome,
                fixed_coef.reshape(1, size),
                slopes,
                precision,
                design,
            )
        ),
    )

    partial = pl.pallas_call(
        predict_kernel,
        out_shape=shape(NEAR, share + slope_rows + size, LANES),
        in_specs=[VMEM] * 7,
        out_specs=VMEM,
        scratch_shapes=[pltpu.VMEM((blocks, LANES), bf16)],
        compiler_params=ROOM,
        name="predict",
    )(from_even, from_odd, own_coefs, hot, spread_hot, design_here, prior_rows)

    received = exchange(partial, ("rows", "cov"), near_groups)
    spread = pl.pallas_call(
        gather_kernel,
        out_shape=shape(2, share + 2 * slope_rows, LANES),
        in_specs=[VMEM],
        out_specs=VMEM,
        scratch_shapes=[pltpu.VMEM((LANES, group_count), f32)],
        compiler_params=ROOM,
        name="gather",
    )(received)
    received = exchange(spread, ("rows", "cov"), first_pairs)
    spread = pl.pallas_call(
        relay_kernel,
        out_shape=shape(2, share + slope_rows, LANES),
        in_specs=[VMEM],
        out_specs=VMEM,
        compiler_params=ROOM,
        name="relay",
    )(received)
    received = exchange(spread, ("rows", "cov"), second_pairs)
    spread, prior = pl.pallas_call(
        residual_kernel,
        out_shape=(shape(NEAR, share, LANES), shape(slope_rows, LANES)),
        in_specs=[VMEM] * 3,
        out_specs=(VMEM, VMEM),
        compiler_params=ROOM,
        name="residual",
    )(received, label, valid)
    back = exchange(spread, ("rows", "cov"), near_groups)

    fixed_parts, grads = pl.pallas_call(
        gradient_kernel,
        out_shape=(shape(rows, 2, LANES), shape(blocks, LANES)),
        in_specs=[VMEM] * 2,
        out_specs=(VMEM,) * 2,
        compiler_params=ROOM,
        name="gradient",
    )(design_here, back)
    fixed_all = exchange(fixed_parts, "rows")

    to_even, to_odd, own = pl.pallas_call(
        group_kernel,
        out_shape=(shape(size, group_count),) * 3,
        in_specs=[VMEM] * 3,
        out_specs=(VMEM,) * 3,
        compiler_params=ROOM,
        cost_estimate=cost(100_000_000, 5_000_000),
        name="group",
    )(grads, hot, prior)
    given_even = swap(to_even, "rows", 0)
    given_odd = swap(to_odd, "rows", 1)

    fixed_grad, slope_grad = pl.pallas_call(
        finish_kernel,
        out_shape=(shape(1, size), shape(size, group_count)),
        in_specs=[VMEM] * 5,
        out_specs=(VMEM, VMEM),
        compiler_params=ROOM,
        name="finish",
    )(fixed_all, fixed_row, own, given_even, given_odd)
    return (fixed_grad.reshape(size), slope_grad)


def solution(mesh):
    return jax.shard_map(
        body,
        mesh=mesh,
        in_specs=(
            P("cov", "rows", None),
            P("rows", None),
            P("rows"),
            P("rows"),
            P("cov"),
            P("cov", "rows"),
            P("cov", None),
        ),
        out_specs=(P("cov"), P("cov", "rows")),
        check_vma=False,
    )
```

```python
import jax
import jax.numpy as jnp
from jax import lax
from jax.experimental import pallas as pl
from jax.experimental.pallas import tpu as pltpu
from jax.sharding import PartitionSpec as P

f32 = jnp.float32
bf16 = jnp.bfloat16
VMEM = pl.BlockSpec(memory_space=pltpu.VMEM)
HBM = pl.BlockSpec(memory_space=pltpu.HBM)
LANES = 128
NEAR = 4
ROOM = pltpu.CompilerParams(vmem_limit_bytes=16 << 20)


def swap(shard, axis, first):
    peers = lax.axis_size(axis)
    pairs = [(i, i + 1) for i in range(first, peers - 1, 2)]
    return lax.ppermute(shard, axis, pairs + [(j, i) for i, j in pairs])


def place_along_cov():
    shift = lax.rem(lax.axis_index("rows"), 2) * (NEAR // 2)
    covs = lax.axis_size("cov")
    return lax.rem(lax.axis_index("cov") + covs - shift, covs), shift


def far_partners(i, odd):
    a, b = i + 1 - 2 * (i % 2), 3 - i
    return a + odd * (b - a), b + odd * (a - b)


def cov_groups():
    covs, rows = lax.axis_size("cov"), lax.axis_size("rows")
    near, first, second = [], [], []
    for row in range(rows):
        members = [row * covs + (c + row % 2 * (NEAR // 2)) % covs for c in range(covs)]
        near += [members[i : i + NEAR] for i in range(0, covs, NEAR)]
        for i in (0, 2):
            for pairs, partner in zip((first, second), far_partners(i, row % 2)):
                for j in range(NEAR):
                    a, b = members[i * NEAR + j], members[partner * NEAR + j]
                    pairs += [(a, b), (b, a)]
    return near, first, second


def exchange(parts, axis, groups=None):
    return lax.all_to_all(parts, axis, 0, 0, tiled=True, axis_index_groups=groups)


def cost(flops, size):
    return pl.CostEstimate(flops=flops, bytes_accessed=size, transcendentals=0)


def three_parts(x):
    a = x.astype(bf16)
    rest = x - a.astype(f32)
    b = rest.astype(bf16)
    c = (rest - b.astype(f32)).astype(bf16)
    return jnp.concatenate([a, b, c], axis=0)


def add_parts(x):
    size = x.shape[0] // 3
    return x[:size] + x[size : 2 * size] + x[2 * size :]


def in_rows(x):
    return jnp.concatenate([x[:, at : at + LANES] for at in range(0, x.shape[1], LANES)], axis=0)


def select_kernel(
    group_hbm, fill_hbm, outcome_hbm, fixed_hbm, slopes_hbm, precision_hbm, design_hbm,
    hot_ref, label_ref, valid_ref, fixed_ref, prior_ref, coef_ref, spread_ref, design_ref,
    group_ref, fill_ref, outcome_ref, own_ref, precision_ref, sems,
):
    window, blocks = hot_ref.shape
    rows = label_ref.shape[0]
    size, groups = own_ref.shape
    place, shift = place_along_cov()
    near = lax.rem(place, NEAR)
    start = pl.multiple_of(near * rows, rows)
    copies = [
        pltpu.make_async_copy(group_hbm, group_ref, sems.at[0]),
        pltpu.make_async_copy(slopes_hbm, own_ref, sems.at[1]),
        pltpu.make_async_copy(precision_hbm, precision_ref, sems.at[2]),
        pltpu.make_async_copy(outcome_hbm.at[pl.ds(start, rows)], outcome_ref, sems.at[3]),
        pltpu.make_async_copy(fill_hbm, fill_ref, sems.at[4]),
        pltpu.make_async_copy(fixed_hbm, fixed_ref, sems.at[5]),
        pltpu.make_async_copy(design_hbm, design_ref, sems.at[6]),
    ]
    for copy in copies:
        copy.start()
    for copy in copies[:2]:
        copy.wait()
    index = group_ref[...] - (lax.axis_index("rows") - 1) * groups
    for piece in range(0, window, groups):
        ids = lax.broadcasted_iota(jnp.int32, (groups, blocks), 0) + piece
        hot_ref[piece : piece + groups, :] = (ids == index).astype(f32).astype(bf16)
    own = own_ref[...]
    coef_ref[...] = add_parts(
        jnp.dot(three_parts(own), hot_ref[groups : 2 * groups, :], preferred_element_type=f32)
    )
    for copy in copies[2:6]:
        copy.wait()
    across = lax.broadcasted_iota(jnp.int32, (size, size), 0)
    along = lax.broadcasted_iota(jnp.int32, (size, size), 1)
    fixed = jnp.where(across == along, jnp.broadcast_to(fixed_ref[...], (size, size)), 0.0)
    coef_ref[...] += jnp.sum(fixed, axis=1, keepdims=True)
    part = lax.broadcasted_iota(jnp.int32, (LANES, LANES), 0)
    for p in range(size):
        ones = (lax.rem(part, size) == p) & (part < 3 * size)
        spread_ref[:, p * LANES : (p + 1) * LANES] = ones.astype(f32).astype(bf16)
    slope_rows = in_rows(own)
    precision = precision_ref[...]
    columns = lax.rem(lax.broadcasted_iota(jnp.int32, (size, LANES), 1) // size, NEAR)
    for peer in range(NEAR):
        kept = [
            jnp.where(columns == lax.rem(peer + shift, NEAR), precision[:, at : at + LANES], 0.0)
            for at in range(0, precision.shape[1], LANES)
        ]
        prior_ref[peer, : slope_rows.shape[0], :] = slope_rows
        prior_ref[peer, slope_rows.shape[0] :, :] = kept[0] + pltpu.roll(kept[1], size, 1)
    fill = fill_ref[pl.ds(near, 1), :].astype(f32)
    column = jnp.broadcast_to(fill, (rows, rows)).T
    lane = lax.broadcasted_iota(jnp.int32, (rows, LANES), 1).astype(f32)
    valid_ref[...] = (lane < column).astype(f32)
    label_ref[...] = outcome_ref[...].astype(f32)
    copies[6].wait()


def predict_kernel(
    even_ref, odd_ref, own_coef_ref, hot_ref, spread_ref, design_ref, prior_ref, out_ref, coef_ref
):
    size, groups = even_ref.shape
    blocks = hot_ref.shape[1]
    share = blocks // NEAR
    parity = lax.rem(lax.axis_index("rows"), 2)
    coefs = own_coef_ref[...]
    for ref, place in ((even_ref, 1 - parity), (odd_ref, parity)):
        piece = hot_ref[pl.ds(pl.multiple_of(place * 2 * groups, groups), groups), :]
        coefs += add_parts(jnp.dot(three_parts(ref[...]), piece, preferred_element_type=f32))
    parts = three_parts(coefs).astype(f32)
    padded = jnp.concatenate([parts, jnp.zeros((LANES - 3 * size, blocks), f32)], axis=0)
    coef_ref[...] = padded.T.astype(bf16)

    def chunk(peer, carry):
        start = pl.multiple_of(peer * share, share)
        here = coef_ref[pl.ds(start, share), :]
        total = jnp.zeros((share, LANES), f32)
        for p in range(0, size, 2):
            wide = jnp.dot(
                here, spread_ref[:, p * LANES : (p + 2) * LANES], preferred_element_type=f32
            )
            total = total + wide[:, :LANES] * design_ref[p, pl.ds(start, share), :].astype(f32)
            total = total + wide[:, LANES:] * design_ref[p + 1, pl.ds(start, share), :].astype(f32)
        out_ref[peer, :share, :] = total
        out_ref[peer, share:, :] = prior_ref[peer]
        return carry

    lax.fori_loop(0, NEAR, chunk, 0)


def gather_kernel(parts_ref, keep_ref, send_ref, prior_ref):
    groups = prior_ref.shape[1]
    halves = groups // LANES
    size = keep_ref.shape[0] - parts_ref.shape[1]
    rows = parts_ref.shape[1] - size * (halves + 1)
    total = jnp.sum(parts_ref[:, :rows, :], axis=0)
    columns = [
        parts_ref[:, at : at + size, :].reshape(-1, LANES)
        for at in range(rows, parts_ref.shape[1], size)
    ]
    prior_ref[...] = lax.dot_general(
        columns[halves],
        jnp.concatenate(columns[:halves], axis=1),
        (((0,), (0,)), ((), ())),
        precision=lax.Precision.HIGHEST,
        preferred_element_type=f32,
    )
    place, shift = place_along_cov()
    near, group = lax.rem(place, NEAR), place // NEAR
    odd = lax.rem(lax.axis_index("rows"), 2)
    partner, _ = far_partners(group, odd)
    pieces = LANES // size
    for ref, target in ((keep_ref, group), (send_ref, partner)):
        _, beyond = far_partners(target, odd)
        ref[:rows, :] = total
        for at, member in ((rows, target), (rows + halves * size, beyond)):
            cov = lax.rem(member * NEAR + near + shift, lax.axis_size("cov"))
            piece = lax.rem(lax.rem(cov, pieces) + cov // pieces, pieces)
            part = prior_ref[pl.ds(pl.multiple_of(piece * size, size), size), :]
            ref[at : at + halves * size, :] = in_rows(part)


def relay_kernel(kept_ref, received_ref, keep_ref, send_ref):
    rows = 2 * keep_ref.shape[0] - kept_ref.shape[0]
    last = keep_ref.shape[0]
    total = kept_ref[...] + received_ref[...]
    keep_ref[...] = total[:last]
    send_ref[:rows, :] = total[:rows]
    send_ref[rows:, :] = total[last:]


def residual_kernel(kept_ref, received_ref, label_ref, valid_ref, out_ref, prior_ref):
    rows = label_ref.shape[0]
    total = kept_ref[...] + received_ref[...]
    residual = jnp.where(valid_ref[...] > 0.5, label_ref[...] - jax.nn.sigmoid(total[:rows]), 0.0)
    out_ref[...] = jnp.broadcast_to(residual[None], out_ref.shape)
    prior_ref[...] = total[rows:]


def gradient_kernel(design_ref, back_ref, fixed_ref, grad_ref):
    size, blocks, _ = design_ref.shape
    share = blocks // NEAR
    lane = lax.broadcasted_iota(jnp.int32, (share, LANES), 1)

    def chunk(peer, total):
        start = pl.multiple_of(peer * share, share)
        residual = back_ref[peer]
        grads = jnp.zeros((share, LANES), f32)
        for p in range(size):
            product = design_ref[p, pl.ds(start, share), :].astype(f32) * residual
            grads = jnp.where(lane == p, jnp.sum(product, axis=1, keepdims=True), grads)
        grad_ref[pl.ds(start, share), :] = grads
        return total + jnp.sum(grads, axis=0, keepdims=True)

    total = lax.fori_loop(0, NEAR, chunk, jnp.zeros((1, LANES), f32))
    fixed_ref[...] = jnp.broadcast_to(total[None], fixed_ref.shape)


def group_kernel(grad_ref, hot_ref, prior_ref, even_ref, odd_ref, own_ref):
    size, groups = own_ref.shape
    parts = three_parts(grad_ref[...].T[:size])
    sums = add_parts(
        lax.dot_general(parts, hot_ref[...], (((1,), (1,)), ((), ())), preferred_element_type=f32)
    )
    lower, upper = sums[:, :groups], sums[:, 2 * groups :]
    odd = lax.rem(lax.axis_index("rows"), 2) == 1
    even_ref[...] = jnp.where(odd, lower, upper)
    odd_ref[...] = jnp.where(odd, upper, lower)
    halves = [prior_ref[at : at + size, :] for at in range(0, prior_ref.shape[0], size)]
    own_ref[...] = sums[:, groups : 2 * groups] - jnp.concatenate(halves, axis=1)


def finish_kernel(fixed_all_ref, fixed_ref, own_ref, even_ref, odd_ref, fixed_out, slope_out):
    size = fixed_ref.shape[1]
    fixed_out[...] = jnp.sum(fixed_all_ref[...], axis=0)[:1, :size] - fixed_ref[...]
    slope_out[...] = own_ref[...] + even_ref[...] + odd_ref[...]


def shape(*dims, dtype=f32):
    return jax.ShapeDtypeStruct(dims, dtype)


def body(design, outcome, block_fill, block_group, fixed_coef, slopes, precision):
    size, group_count = slopes.shape
    blocks = block_group.shape[0]
    covs, rows = lax.axis_size("cov"), lax.axis_size("rows")
    share = blocks // NEAR
    near_groups, first_pairs, second_pairs = cov_groups()
    slope_rows = size * group_count // LANES

    from_even = swap(slopes, "rows", 0)
    from_odd = swap(slopes, "rows", 1)

    hot, label, valid, fixed_row, prior_rows, own_coefs, spread_hot, design_here = pl.pallas_call(
        select_kernel,
        out_shape=(
            shape(3 * group_count, blocks, dtype=bf16),
            shape(share, LANES),
            shape(share, LANES),
            shape(1, size),
            shape(NEAR, slope_rows + size, LANES),
            shape(size, blocks),
            shape(LANES, size * LANES, dtype=bf16),
            shape(*design.shape, dtype=bf16),
        ),
        in_specs=[HBM] * 7,
        out_specs=(VMEM,) * 8,
        scratch_shapes=[
            pltpu.VMEM((1, blocks), jnp.int32),
            pltpu.VMEM((blocks // LANES, LANES), jnp.int32),
            pltpu.VMEM((share, LANES), jnp.int32),
            pltpu.VMEM((size, group_count), f32),
            pltpu.VMEM((size, covs * size), f32),
            pltpu.SemaphoreType.DMA((7,)),
        ],
        compiler_params=ROOM,
        cost_estimate=cost(10_000_000, 5_000_000),
        name="select",
    )(
        *(
            pltpu.with_memory_space_constraint(x, pltpu.HBM)
            for x in (
                block_group.reshape(1, blocks),
                block_fill.reshape(blocks // LANES, LANES),
                outcome,
                fixed_coef.reshape(1, size),
                slopes,
                precision,
                design,
            )
        ),
    )

    partial = pl.pallas_call(
        predict_kernel,
        out_shape=shape(NEAR, share + slope_rows + size, LANES),
        in_specs=[VMEM] * 7,
        out_specs=VMEM,
        scratch_shapes=[pltpu.VMEM((blocks, LANES), bf16)],
        compiler_params=ROOM,
        name="predict",
    )(from_even, from_odd, own_coefs, hot, spread_hot, design_here, prior_rows)

    received = exchange(partial, ("rows", "cov"), near_groups)
    kept, sent = pl.pallas_call(
        gather_kernel,
        out_shape=(shape(share + 2 * slope_rows, LANES),) * 2,
        in_specs=[VMEM],
        out_specs=(VMEM, VMEM),
        scratch_shapes=[pltpu.VMEM((LANES, group_count), f32)],
        compiler_params=ROOM,
        name="gather",
    )(received)
    received = lax.ppermute(sent, ("rows", "cov"), first_pairs)
    kept, sent = pl.pallas_call(
        relay_kernel,
        out_shape=(shape(share + slope_rows, LANES),) * 2,
        in_specs=[VMEM] * 2,
        out_specs=(VMEM, VMEM),
        compiler_params=ROOM,
        name="relay",
    )(kept, received)
    received = lax.ppermute(sent, ("rows", "cov"), second_pairs)
    spread, prior = pl.pallas_call(
        residual_kernel,
        out_shape=(shape(NEAR, share, LANES), shape(slope_rows, LANES)),
        in_specs=[VMEM] * 4,
        out_specs=(VMEM, VMEM),
        compiler_params=ROOM,
        name="residual",
    )(kept, received, label, valid)
    back = exchange(spread, ("rows", "cov"), near_groups)

    fixed_parts, grads = pl.pallas_call(
        gradient_kernel,
        out_shape=(shape(rows, 2, LANES), shape(blocks, LANES)),
        in_specs=[VMEM] * 2,
        out_specs=(VMEM,) * 2,
        compiler_params=ROOM,
        name="gradient",
    )(design_here, back)
    fixed_all = exchange(fixed_parts, "rows")

    to_even, to_odd, own = pl.pallas_call(
        group_kernel,
        out_shape=(shape(size, group_count),) * 3,
        in_specs=[VMEM] * 3,
        out_specs=(VMEM,) * 3,
        compiler_params=ROOM,
        cost_estimate=cost(100_000_000, 5_000_000),
        name="group",
    )(grads, hot, prior)
    given_even = swap(to_even, "rows", 0)
    given_odd = swap(to_odd, "rows", 1)

    fixed_grad, slope_grad = pl.pallas_call(
        finish_kernel,
        out_shape=(shape(1, size), shape(size, group_count)),
        in_specs=[VMEM] * 5,
        out_specs=(VMEM, VMEM),
        compiler_params=ROOM,
        name="finish",
    )(fixed_all, fixed_row, own, given_even, given_odd)
    return (fixed_grad.reshape(size), slope_grad)


def solution(mesh):
    return jax.shard_map(
        body,
        mesh=mesh,
        in_specs=(
            P("cov", "rows", None),
            P("rows", None),
            P("rows"),
            P("rows"),
            P("cov"),
            P("cov", "rows"),
            P("cov", None),
        ),
        out_specs=(P("cov"), P("cov", "rows")),
        check_vma=False,
    )
```

```python
import jax
import jax.numpy as jnp
from jax import lax
from jax.experimental import pallas as pl
from jax.experimental.pallas import tpu as pltpu
from jax.sharding import PartitionSpec as P

f32 = jnp.float32
bf16 = jnp.bfloat16
VMEM = pl.BlockSpec(memory_space=pltpu.VMEM)
HBM = pl.BlockSpec(memory_space=pltpu.HBM)
LANES = 128
NEAR = 4
ROOM = pltpu.CompilerParams(vmem_limit_bytes=16 << 20)


def swap(shard, axis, first):
    peers = lax.axis_size(axis)
    pairs = [(i, i + 1) for i in range(first, peers - 1, 2)]
    return lax.ppermute(shard, axis, pairs + [(j, i) for i, j in pairs])


def place_along_cov():
    shift = lax.rem(lax.axis_index("rows"), 2) * (NEAR // 2)
    covs = lax.axis_size("cov")
    return lax.rem(lax.axis_index("cov") + covs - shift, covs), shift


def far_partners(i, odd):
    a, b = i + 1 - 2 * (i % 2), 3 - i
    return a + odd * (b - a), b + odd * (a - b)


def cov_groups():
    covs, rows = lax.axis_size("cov"), lax.axis_size("rows")
    near, first, second = [], [], []
    for row in range(rows):
        members = [row * covs + (c + row % 2 * (NEAR // 2)) % covs for c in range(covs)]
        near += [members[i : i + NEAR] for i in range(0, covs, NEAR)]
        for i in (0, 2):
            for pairs, partner in zip((first, second), far_partners(i, row % 2)):
                for j in range(NEAR):
                    a, b = members[i * NEAR + j], members[partner * NEAR + j]
                    pairs += [(a, b), (b, a)]
    return near, first, second


def exchange(parts, axis, groups=None):
    return lax.all_to_all(parts, axis, 0, 0, tiled=True, axis_index_groups=groups)


def cost(flops, size):
    return pl.CostEstimate(flops=flops, bytes_accessed=size, transcendentals=0)


def three_parts(x):
    a = x.astype(bf16)
    rest = x - a.astype(f32)
    b = rest.astype(bf16)
    c = (rest - b.astype(f32)).astype(bf16)
    return jnp.concatenate([a, b, c], axis=0)


def add_parts(x):
    size = x.shape[0] // 3
    return x[:size] + x[size : 2 * size] + x[2 * size :]


def in_rows(x):
    return jnp.concatenate([x[:, at : at + LANES] for at in range(0, x.shape[1], LANES)], axis=0)


def select_kernel(
    group_hbm, fill_hbm, outcome_hbm, fixed_hbm, slopes_hbm, precision_hbm, design_hbm,
    hot_ref, label_ref, valid_ref, fixed_ref, prior_ref, coef_ref, spread_ref, design_ref,
    group_ref, fill_ref, outcome_ref, own_ref, precision_ref, sems,
):
    window, blocks = hot_ref.shape
    rows = label_ref.shape[0]
    size, groups = own_ref.shape
    place, shift = place_along_cov()
    near = lax.rem(place, NEAR)
    start = pl.multiple_of(near * rows, rows)
    copies = [
        pltpu.make_async_copy(group_hbm, group_ref, sems.at[0]),
        pltpu.make_async_copy(slopes_hbm, own_ref, sems.at[1]),
        pltpu.make_async_copy(precision_hbm, precision_ref, sems.at[2]),
        pltpu.make_async_copy(outcome_hbm.at[pl.ds(start, rows)], outcome_ref, sems.at[3]),
        pltpu.make_async_copy(fill_hbm, fill_ref, sems.at[4]),
        pltpu.make_async_copy(fixed_hbm, fixed_ref, sems.at[5]),
    ]
    quarter = size // 4
    copies += [
        pltpu.make_async_copy(
            design_hbm.at[pl.ds(i * quarter, quarter)],
            design_ref.at[pl.ds(i * quarter, quarter)],
            sems.at[6 + i],
        )
        for i in range(4)
    ]
    for copy in copies:
        copy.start()
    for copy in copies[:2]:
        copy.wait()
    index = group_ref[...] - (lax.axis_index("rows") - 1) * groups
    for piece in range(0, window, groups):
        ids = lax.broadcasted_iota(jnp.int32, (groups, blocks), 0) + piece
        hot_ref[piece : piece + groups, :] = (ids == index).astype(f32).astype(bf16)
    own = own_ref[...]
    coef_ref[...] = add_parts(
        jnp.dot(three_parts(own), hot_ref[groups : 2 * groups, :], preferred_element_type=f32)
    )
    for copy in copies[2:6]:
        copy.wait()
    across = lax.broadcasted_iota(jnp.int32, (size, size), 0)
    along = lax.broadcasted_iota(jnp.int32, (size, size), 1)
    fixed = jnp.where(across == along, jnp.broadcast_to(fixed_ref[...], (size, size)), 0.0)
    coef_ref[...] += jnp.sum(fixed, axis=1, keepdims=True)
    part = lax.broadcasted_iota(jnp.int32, (LANES, LANES), 0)
    for p in range(size):
        ones = (lax.rem(part, size) == p) & (part < 3 * size)
        spread_ref[:, p * LANES : (p + 1) * LANES] = ones.astype(f32).astype(bf16)
    slope_rows = in_rows(own)
    precision = precision_ref[...]
    columns = lax.rem(lax.broadcasted_iota(jnp.int32, (size, LANES), 1) // size, NEAR)
    for peer in range(NEAR):
        kept = [
            jnp.where(columns == lax.rem(peer + shift, NEAR), precision[:, at : at + LANES], 0.0)
            for at in range(0, precision.shape[1], LANES)
        ]
        prior_ref[peer, : slope_rows.shape[0], :] = slope_rows
        prior_ref[peer, slope_rows.shape[0] :, :] = kept[0] + pltpu.roll(kept[1], size, 1)
    fill = fill_ref[pl.ds(near, 1), :].astype(f32)
    column = jnp.broadcast_to(fill, (rows, rows)).T
    lane = lax.broadcasted_iota(jnp.int32, (rows, LANES), 1).astype(f32)
    valid_ref[...] = (lane < column).astype(f32)
    label_ref[...] = outcome_ref[...].astype(f32)
    for copy in copies[6:]:
        copy.wait()


def predict_kernel(
    even_ref, odd_ref, own_coef_ref, hot_ref, spread_ref, design_ref, prior_ref, out_ref, coef_ref
):
    size, groups = even_ref.shape
    blocks = hot_ref.shape[1]
    share = blocks // NEAR
    parity = lax.rem(lax.axis_index("rows"), 2)
    coefs = own_coef_ref[...]
    for ref, place in ((even_ref, 1 - parity), (odd_ref, parity)):
        piece = hot_ref[pl.ds(pl.multiple_of(place * 2 * groups, groups), groups), :]
        coefs += add_parts(jnp.dot(three_parts(ref[...]), piece, preferred_element_type=f32))
    parts = three_parts(coefs).astype(f32)
    padded = jnp.concatenate([parts, jnp.zeros((LANES - 3 * size, blocks), f32)], axis=0)
    coef_ref[...] = padded.T.astype(bf16)

    step = 2 * share

    def chunk(i, carry):
        start = pl.multiple_of(i * step, step)
        here = coef_ref[pl.ds(start, step), :]
        total = jnp.zeros((step, LANES), f32)
        for p in range(0, size, 2):
            wide = jnp.dot(
                here, spread_ref[:, p * LANES : (p + 2) * LANES], preferred_element_type=f32
            )
            total = total + wide[:, :LANES] * design_ref[p, pl.ds(start, step), :].astype(f32)
            total = total + wide[:, LANES:] * design_ref[p + 1, pl.ds(start, step), :].astype(f32)
        for k in range(2):
            out_ref[2 * i + k, :share, :] = total[k * share : (k + 1) * share]
            out_ref[2 * i + k, share:, :] = prior_ref[2 * i + k]
        return carry

    lax.fori_loop(0, NEAR // 2, chunk, 0)


def gather_kernel(parts_ref, keep_ref, send_ref, prior_ref):
    groups = prior_ref.shape[1]
    halves = groups // LANES
    size = keep_ref.shape[0] - parts_ref.shape[1]
    rows = parts_ref.shape[1] - size * (halves + 1)
    total = jnp.sum(parts_ref[:, :rows, :], axis=0)
    columns = [
        parts_ref[:, at : at + size, :].reshape(-1, LANES)
        for at in range(rows, parts_ref.shape[1], size)
    ]
    prior_ref[...] = lax.dot_general(
        columns[halves],
        jnp.concatenate(columns[:halves], axis=1),
        (((0,), (0,)), ((), ())),
        precision=lax.Precision.HIGHEST,
        preferred_element_type=f32,
    )
    place, shift = place_along_cov()
    near, group = lax.rem(place, NEAR), place // NEAR
    odd = lax.rem(lax.axis_index("rows"), 2)
    partner, _ = far_partners(group, odd)
    pieces = LANES // size
    for ref, target in ((keep_ref, group), (send_ref, partner)):
        _, beyond = far_partners(target, odd)
        ref[:rows, :] = total
        for at, member in ((rows, target), (rows + halves * size, beyond)):
            cov = lax.rem(member * NEAR + near + shift, lax.axis_size("cov"))
            piece = lax.rem(lax.rem(cov, pieces) + cov // pieces, pieces)
            part = prior_ref[pl.ds(pl.multiple_of(piece * size, size), size), :]
            ref[at : at + halves * size, :] = in_rows(part)


def relay_kernel(kept_ref, received_ref, keep_ref, send_ref):
    rows = 2 * keep_ref.shape[0] - kept_ref.shape[0]
    last = keep_ref.shape[0]
    total = kept_ref[...] + received_ref[...]
    keep_ref[...] = total[:last]
    send_ref[:rows, :] = total[:rows]
    send_ref[rows:, :] = total[last:]


def residual_kernel(kept_ref, received_ref, label_ref, valid_ref, out_ref, prior_ref):
    rows = label_ref.shape[0]
    total = kept_ref[...] + received_ref[...]
    residual = jnp.where(valid_ref[...] > 0.5, label_ref[...] - jax.nn.sigmoid(total[:rows]), 0.0)
    out_ref[...] = jnp.broadcast_to(residual[None], out_ref.shape)
    prior_ref[...] = total[rows:]


def gradient_kernel(design_ref, back_ref, fixed_ref, grad_ref):
    size, blocks, _ = design_ref.shape
    share = blocks // NEAR
    lane = lax.broadcasted_iota(jnp.int32, (share, LANES), 1)

    def chunk(peer, total):
        start = pl.multiple_of(peer * share, share)
        residual = back_ref[peer]
        grads = jnp.zeros((share, LANES), f32)
        for p in range(size):
            product = design_ref[p, pl.ds(start, share), :].astype(f32) * residual
            grads = jnp.where(lane == p, jnp.sum(product, axis=1, keepdims=True), grads)
        grad_ref[pl.ds(start, share), :] = grads
        return total + jnp.sum(grads, axis=0, keepdims=True)

    total = lax.fori_loop(0, NEAR, chunk, jnp.zeros((1, LANES), f32))
    fixed_ref[...] = jnp.broadcast_to(total[None], fixed_ref.shape)


def group_kernel(grad_ref, hot_ref, prior_ref, even_ref, odd_ref, own_ref):
    size, groups = own_ref.shape
    parts = three_parts(grad_ref[...].T[:size])
    sums = add_parts(
        lax.dot_general(parts, hot_ref[...], (((1,), (1,)), ((), ())), preferred_element_type=f32)
    )
    lower, upper = sums[:, :groups], sums[:, 2 * groups :]
    odd = lax.rem(lax.axis_index("rows"), 2) == 1
    even_ref[...] = jnp.where(odd, lower, upper)
    odd_ref[...] = jnp.where(odd, upper, lower)
    halves = [prior_ref[at : at + size, :] for at in range(0, prior_ref.shape[0], size)]
    own_ref[...] = sums[:, groups : 2 * groups] - jnp.concatenate(halves, axis=1)


def finish_kernel(fixed_all_ref, fixed_ref, own_ref, even_ref, odd_ref, fixed_out, slope_out):
    size = fixed_ref.shape[1]
    fixed_out[...] = jnp.sum(fixed_all_ref[...], axis=0)[:1, :size] - fixed_ref[...]
    slope_out[...] = own_ref[...] + even_ref[...] + odd_ref[...]


def shape(*dims, dtype=f32):
    return jax.ShapeDtypeStruct(dims, dtype)


def body(design, outcome, block_fill, block_group, fixed_coef, slopes, precision):
    size, group_count = slopes.shape
    blocks = block_group.shape[0]
    covs, rows = lax.axis_size("cov"), lax.axis_size("rows")
    share = blocks // NEAR
    near_groups, first_pairs, second_pairs = cov_groups()
    slope_rows = size * group_count // LANES

    from_even = swap(slopes, "rows", 0)
    from_odd = swap(slopes, "rows", 1)

    hot, label, valid, fixed_row, prior_rows, own_coefs, spread_hot, design_here = pl.pallas_call(
        select_kernel,
        out_shape=(
            shape(3 * group_count, blocks, dtype=bf16),
            shape(share, LANES),
            shape(share, LANES),
            shape(1, size),
            shape(NEAR, slope_rows + size, LANES),
            shape(size, blocks),
            shape(LANES, size * LANES, dtype=bf16),
            shape(*design.shape, dtype=bf16),
        ),
        in_specs=[HBM] * 7,
        out_specs=(VMEM,) * 8,
        scratch_shapes=[
            pltpu.VMEM((1, blocks), jnp.int32),
            pltpu.VMEM((blocks // LANES, LANES), jnp.int32),
            pltpu.VMEM((share, LANES), jnp.int32),
            pltpu.VMEM((size, group_count), f32),
            pltpu.VMEM((size, covs * size), f32),
            pltpu.SemaphoreType.DMA((10,)),
        ],
        compiler_params=ROOM,
        cost_estimate=cost(10_000_000, 5_000_000),
        name="select",
    )(
        *(
            pltpu.with_memory_space_constraint(x, pltpu.HBM)
            for x in (
                block_group.reshape(1, blocks),
                block_fill.reshape(blocks // LANES, LANES),
                outcome,
                fixed_coef.reshape(1, size),
                slopes,
                precision,
                design,
            )
        ),
    )

    partial = pl.pallas_call(
        predict_kernel,
        out_shape=shape(NEAR, share + slope_rows + size, LANES),
        in_specs=[VMEM] * 7,
        out_specs=VMEM,
        scratch_shapes=[pltpu.VMEM((blocks, LANES), bf16)],
        compiler_params=ROOM,
        name="predict",
    )(from_even, from_odd, own_coefs, hot, spread_hot, design_here, prior_rows)

    received = exchange(partial, ("rows", "cov"), near_groups)
    kept, sent = pl.pallas_call(
        gather_kernel,
        out_shape=(shape(share + 2 * slope_rows, LANES),) * 2,
        in_specs=[VMEM],
        out_specs=(VMEM, VMEM),
        scratch_shapes=[pltpu.VMEM((LANES, group_count), f32)],
        compiler_params=ROOM,
        name="gather",
    )(received)
    received = lax.ppermute(sent, ("rows", "cov"), first_pairs)
    kept, sent = pl.pallas_call(
        relay_kernel,
        out_shape=(shape(share + slope_rows, LANES),) * 2,
        in_specs=[VMEM] * 2,
        out_specs=(VMEM, VMEM),
        compiler_params=ROOM,
        name="relay",
    )(kept, received)
    received = lax.ppermute(sent, ("rows", "cov"), second_pairs)
    spread, prior = pl.pallas_call(
        residual_kernel,
        out_shape=(shape(NEAR, share, LANES), shape(slope_rows, LANES)),
        in_specs=[VMEM] * 4,
        out_specs=(VMEM, VMEM),
        compiler_params=ROOM,
        name="residual",
    )(kept, received, label, valid)
    back = exchange(spread, ("rows", "cov"), near_groups)

    fixed_parts, grads = pl.pallas_call(
        gradient_kernel,
        out_shape=(shape(rows, 2, LANES), shape(blocks, LANES)),
        in_specs=[VMEM] * 2,
        out_specs=(VMEM,) * 2,
        compiler_params=ROOM,
        name="gradient",
    )(design_here, back)
    fixed_all = exchange(fixed_parts, "rows")

    to_even, to_odd, own = pl.pallas_call(
        group_kernel,
        out_shape=(shape(size, group_count),) * 3,
        in_specs=[VMEM] * 3,
        out_specs=(VMEM,) * 3,
        compiler_params=ROOM,
        cost_estimate=cost(100_000_000, 5_000_000),
        name="group",
    )(grads, hot, prior)
    given_even = swap(to_even, "rows", 0)
    given_odd = swap(to_odd, "rows", 1)

    fixed_grad, slope_grad = pl.pallas_call(
        finish_kernel,
        out_shape=(shape(1, size), shape(size, group_count)),
        in_specs=[VMEM] * 5,
        out_specs=(VMEM, VMEM),
        compiler_params=ROOM,
        name="finish",
    )(fixed_all, fixed_row, own, given_even, given_odd)
    return (fixed_grad.reshape(size), slope_grad)


def solution(mesh):
    return jax.shard_map(
        body,
        mesh=mesh,
        in_specs=(
            P("cov", "rows", None),
            P("rows", None),
            P("rows"),
            P("rows"),
            P("cov"),
            P("cov", "rows"),
            P("cov", None),
        ),
        out_specs=(P("cov"), P("cov", "rows")),
        check_vma=False,
    )
```

```python
import jax
import jax.numpy as jnp
from jax import lax
from jax.experimental import pallas as pl
from jax.experimental.pallas import tpu as pltpu
from jax.sharding import PartitionSpec as P

f32 = jnp.float32
bf16 = jnp.bfloat16
VMEM = pl.BlockSpec(memory_space=pltpu.VMEM)
HBM = pl.BlockSpec(memory_space=pltpu.HBM)
LANES = 128
NEAR = 4
ROOM = pltpu.CompilerParams(vmem_limit_bytes=16 << 20)


def swap(shard, axis, first):
    peers = lax.axis_size(axis)
    pairs = [(i, i + 1) for i in range(first, peers - 1, 2)]
    return lax.ppermute(shard, axis, pairs + [(j, i) for i, j in pairs])


def place_along_cov():
    shift = lax.rem(lax.axis_index("rows"), 2) * (NEAR // 2)
    covs = lax.axis_size("cov")
    return lax.rem(lax.axis_index("cov") + covs - shift, covs), shift


def far_partners(i, odd):
    a, b = i + 1 - 2 * (i % 2), 3 - i
    return a + odd * (b - a), b + odd * (a - b)


def cov_groups():
    covs, rows = lax.axis_size("cov"), lax.axis_size("rows")
    near, first, second, across, beside = [], [], [], [], []
    for row in range(rows):
        members = [row * covs + (c + row % 2 * (NEAR // 2)) % covs for c in range(covs)]
        near += [members[i : i + NEAR] for i in range(0, covs, NEAR)]
        across += [(m, members[c ^ 2]) for c, m in enumerate(members)]
        beside += [(m, members[c ^ 1]) for c, m in enumerate(members)]
        for i in (0, 2):
            for pairs, partner in zip((first, second), far_partners(i, row % 2)):
                for j in range(NEAR):
                    a, b = members[i * NEAR + j], members[partner * NEAR + j]
                    pairs += [(a, b), (b, a)]
    return near, first, second, across, beside


def exchange(parts, axis, groups=None):
    return lax.all_to_all(parts, axis, 0, 0, tiled=True, axis_index_groups=groups)


def cost(flops, size):
    return pl.CostEstimate(flops=flops, bytes_accessed=size, transcendentals=0)


def three_parts(x):
    a = x.astype(bf16)
    rest = x - a.astype(f32)
    b = rest.astype(bf16)
    c = (rest - b.astype(f32)).astype(bf16)
    return jnp.concatenate([a, b, c], axis=0)


def add_parts(x):
    size = x.shape[0] // 3
    return x[:size] + x[size : 2 * size] + x[2 * size :]


def in_rows(x):
    return jnp.concatenate([x[:, at : at + LANES] for at in range(0, x.shape[1], LANES)], axis=0)


def select_kernel(
    group_hbm, fill_hbm, outcome_hbm, fixed_hbm, slopes_hbm, precision_hbm, design_hbm,
    hot_ref, label_ref, valid_ref, fixed_ref, prior_ref, coef_ref, spread_ref, design_ref,
    group_ref, fill_ref, outcome_ref, own_ref, precision_ref, sems,
):
    window, blocks = hot_ref.shape
    rows = label_ref.shape[0]
    size, groups = own_ref.shape
    place, shift = place_along_cov()
    near = lax.rem(place, NEAR)
    start = pl.multiple_of(near * rows, rows)
    copies = [
        pltpu.make_async_copy(group_hbm, group_ref, sems.at[0]),
        pltpu.make_async_copy(slopes_hbm, own_ref, sems.at[1]),
        pltpu.make_async_copy(precision_hbm, precision_ref, sems.at[2]),
        pltpu.make_async_copy(outcome_hbm.at[pl.ds(start, rows)], outcome_ref, sems.at[3]),
        pltpu.make_async_copy(fill_hbm, fill_ref, sems.at[4]),
        pltpu.make_async_copy(fixed_hbm, fixed_ref, sems.at[5]),
    ]
    quarter = size // 4
    copies += [
        pltpu.make_async_copy(
            design_hbm.at[pl.ds(i * quarter, quarter)],
            design_ref.at[pl.ds(i * quarter, quarter)],
            sems.at[6 + i],
        )
        for i in range(4)
    ]
    for copy in copies:
        copy.start()
    for copy in copies[:2]:
        copy.wait()
    index = group_ref[...] - (lax.axis_index("rows") - 1) * groups
    for piece in range(0, window, groups):
        ids = lax.broadcasted_iota(jnp.int32, (groups, blocks), 0) + piece
        hot_ref[piece : piece + groups, :] = (ids == index).astype(f32).astype(bf16)
    own = own_ref[...]
    coef_ref[...] = add_parts(
        jnp.dot(three_parts(own), hot_ref[groups : 2 * groups, :], preferred_element_type=f32)
    )
    for copy in copies[2:6]:
        copy.wait()
    across = lax.broadcasted_iota(jnp.int32, (size, size), 0)
    along = lax.broadcasted_iota(jnp.int32, (size, size), 1)
    fixed = jnp.where(across == along, jnp.broadcast_to(fixed_ref[...], (size, size)), 0.0)
    coef_ref[...] += jnp.sum(fixed, axis=1, keepdims=True)
    part = lax.broadcasted_iota(jnp.int32, (LANES, LANES), 0)
    for p in range(size):
        ones = (lax.rem(part, size) == p) & (part < 3 * size)
        spread_ref[:, p * LANES : (p + 1) * LANES] = ones.astype(f32).astype(bf16)
    slope_rows = in_rows(own)
    precision = precision_ref[...]
    columns = lax.rem(lax.broadcasted_iota(jnp.int32, (size, LANES), 1) // size, NEAR)
    for peer in range(NEAR):
        kept = [
            jnp.where(columns == lax.rem(peer + shift, NEAR), precision[:, at : at + LANES], 0.0)
            for at in range(0, precision.shape[1], LANES)
        ]
        prior_ref[peer, : slope_rows.shape[0], :] = slope_rows
        prior_ref[peer, slope_rows.shape[0] :, :] = kept[0] + pltpu.roll(kept[1], size, 1)
    fill = fill_ref[pl.ds(near, 1), :].astype(f32)
    column = jnp.broadcast_to(fill, (rows, rows)).T
    lane = lax.broadcasted_iota(jnp.int32, (rows, LANES), 1).astype(f32)
    valid_ref[...] = (lane < column).astype(f32)
    label_ref[...] = outcome_ref[...].astype(f32)
    for copy in copies[6:]:
        copy.wait()


def predict_kernel(
    even_ref, odd_ref, own_coef_ref, hot_ref, spread_ref, design_ref, prior_ref, out_ref, coef_ref
):
    size, groups = even_ref.shape
    blocks = hot_ref.shape[1]
    share = blocks // NEAR
    parity = lax.rem(lax.axis_index("rows"), 2)
    coefs = own_coef_ref[...]
    for ref, place in ((even_ref, 1 - parity), (odd_ref, parity)):
        piece = hot_ref[pl.ds(pl.multiple_of(place * 2 * groups, groups), groups), :]
        coefs += add_parts(jnp.dot(three_parts(ref[...]), piece, preferred_element_type=f32))
    parts = three_parts(coefs).astype(f32)
    padded = jnp.concatenate([parts, jnp.zeros((LANES - 3 * size, blocks), f32)], axis=0)
    coef_ref[...] = padded.T.astype(bf16)

    step = 2 * share

    def chunk(i, carry):
        start = pl.multiple_of(i * step, step)
        here = coef_ref[pl.ds(start, step), :]
        total = jnp.zeros((step, LANES), f32)
        for p in range(0, size, 2):
            wide = jnp.dot(
                here, spread_ref[:, p * LANES : (p + 2) * LANES], preferred_element_type=f32
            )
            total = total + wide[:, :LANES] * design_ref[p, pl.ds(start, step), :].astype(f32)
            total = total + wide[:, LANES:] * design_ref[p + 1, pl.ds(start, step), :].astype(f32)
        for k in range(2):
            out_ref[2 * i + k, :share, :] = total[k * share : (k + 1) * share]
            out_ref[2 * i + k, share:, :] = prior_ref[2 * i + k]
        return carry

    lax.fori_loop(0, NEAR // 2, chunk, 0)


def gather_kernel(parts_ref, keep_ref, send_ref, prior_ref):
    groups = prior_ref.shape[1]
    halves = groups // LANES
    size = keep_ref.shape[0] - parts_ref.shape[1]
    rows = parts_ref.shape[1] - size * (halves + 1)
    total = jnp.sum(parts_ref[:, :rows, :], axis=0)
    columns = [
        parts_ref[:, at : at + size, :].reshape(-1, LANES)
        for at in range(rows, parts_ref.shape[1], size)
    ]
    prior_ref[...] = lax.dot_general(
        columns[halves],
        jnp.concatenate(columns[:halves], axis=1),
        (((0,), (0,)), ((), ())),
        precision=lax.Precision.HIGHEST,
        preferred_element_type=f32,
    )
    place, shift = place_along_cov()
    near, group = lax.rem(place, NEAR), place // NEAR
    odd = lax.rem(lax.axis_index("rows"), 2)
    partner, _ = far_partners(group, odd)
    pieces = LANES // size
    for ref, target in ((keep_ref, group), (send_ref, partner)):
        _, beyond = far_partners(target, odd)
        ref[:rows, :] = total
        for at, member in ((rows, target), (rows + halves * size, beyond)):
            cov = lax.rem(member * NEAR + near + shift, lax.axis_size("cov"))
            piece = lax.rem(lax.rem(cov, pieces) + cov // pieces, pieces)
            part = prior_ref[pl.ds(pl.multiple_of(piece * size, size), size), :]
            ref[at : at + halves * size, :] = in_rows(part)


def relay_kernel(kept_ref, received_ref, keep_ref, send_ref):
    rows = 2 * keep_ref.shape[0] - kept_ref.shape[0]
    last = keep_ref.shape[0]
    total = kept_ref[...] + received_ref[...]
    keep_ref[...] = total[:last]
    send_ref[:rows, :] = total[:rows]
    send_ref[rows:, :] = total[last:]


def residual_kernel(kept_ref, received_ref, label_ref, valid_ref, out_ref, prior_ref):
    rows = label_ref.shape[0]
    total = kept_ref[...] + received_ref[...]
    residual = jnp.where(valid_ref[...] > 0.5, label_ref[...] - jax.nn.sigmoid(total[:rows]), 0.0)
    out_ref[...] = residual
    prior_ref[...] = total[rows:]


def join_kernel(own_ref, across_ref, out_ref):
    share = own_ref.shape[0]
    out_ref[:share, :] = own_ref[...]
    out_ref[share:, :] = across_ref[...]


def block_gradients(design_ref, residual, start):
    size = design_ref.shape[0]
    share = residual.shape[0]
    lane = lax.broadcasted_iota(jnp.int32, (share, LANES), 1)
    grads = jnp.zeros((share, LANES), f32)
    for p in range(size):
        product = design_ref[p, pl.ds(start, share), :].astype(f32) * residual
        grads = jnp.where(lane == p, jnp.sum(product, axis=1, keepdims=True), grads)
    return grads


def half_kernel(design_ref, residual_ref, grad_ref):
    share = grad_ref.shape[1]
    near = lax.rem(place_along_cov()[0], NEAR)

    def chunk(k, carry):
        start = pl.multiple_of(lax.rem(near + 2 * k, NEAR) * share, share)
        residual = residual_ref[pl.ds(pl.multiple_of(k * share, share), share), :]
        grad_ref[k] = block_gradients(design_ref, residual, start)
        return carry

    lax.fori_loop(0, 2, chunk, 0)


def rest_kernel(design_ref, residual_ref, half_ref, fixed_ref, grad_ref):
    share = half_ref.shape[1]
    near = lax.rem(place_along_cov()[0], NEAR)
    beside = near + 1 - 2 * lax.rem(near, 2)

    def chunk(k, total):
        start = pl.multiple_of(lax.rem(beside + 2 * k, NEAR) * share, share)
        residual = residual_ref[pl.ds(pl.multiple_of(k * share, share), share), :]
        grads = block_gradients(design_ref, residual, start)
        grad_ref[pl.ds(start, share), :] = grads
        half = half_ref[k]
        grad_ref[pl.ds(pl.multiple_of(lax.rem(near + 2 * k, NEAR) * share, share), share), :] = half
        return total + jnp.sum(grads + half, axis=0, keepdims=True)

    total = lax.fori_loop(0, 2, chunk, jnp.zeros((1, LANES), f32))
    fixed_ref[...] = jnp.broadcast_to(total[None], fixed_ref.shape)


def group_kernel(grad_ref, hot_ref, prior_ref, even_ref, odd_ref, own_ref):
    size, groups = own_ref.shape
    parts = three_parts(grad_ref[...].T[:size])
    sums = add_parts(
        lax.dot_general(parts, hot_ref[...], (((1,), (1,)), ((), ())), preferred_element_type=f32)
    )
    lower, upper = sums[:, :groups], sums[:, 2 * groups :]
    odd = lax.rem(lax.axis_index("rows"), 2) == 1
    even_ref[...] = jnp.where(odd, lower, upper)
    odd_ref[...] = jnp.where(odd, upper, lower)
    halves = [prior_ref[at : at + size, :] for at in range(0, prior_ref.shape[0], size)]
    own_ref[...] = sums[:, groups : 2 * groups] - jnp.concatenate(halves, axis=1)


def finish_kernel(fixed_all_ref, fixed_ref, own_ref, even_ref, odd_ref, fixed_out, slope_out):
    size = fixed_ref.shape[1]
    fixed_out[...] = jnp.sum(fixed_all_ref[...], axis=0)[:1, :size] - fixed_ref[...]
    slope_out[...] = own_ref[...] + even_ref[...] + odd_ref[...]


def shape(*dims, dtype=f32):
    return jax.ShapeDtypeStruct(dims, dtype)


def body(design, outcome, block_fill, block_group, fixed_coef, slopes, precision):
    size, group_count = slopes.shape
    blocks = block_group.shape[0]
    covs, rows = lax.axis_size("cov"), lax.axis_size("rows")
    share = blocks // NEAR
    near_groups, first_pairs, second_pairs, across_pairs, beside_pairs = cov_groups()
    slope_rows = size * group_count // LANES

    from_even = swap(slopes, "rows", 0)
    from_odd = swap(slopes, "rows", 1)

    hot, label, valid, fixed_row, prior_rows, own_coefs, spread_hot, design_here = pl.pallas_call(
        select_kernel,
        out_shape=(
            shape(3 * group_count, blocks, dtype=bf16),
            shape(share, LANES),
            shape(share, LANES),
            shape(1, size),
            shape(NEAR, slope_rows + size, LANES),
            shape(size, blocks),
            shape(LANES, size * LANES, dtype=bf16),
            shape(*design.shape, dtype=bf16),
        ),
        in_specs=[HBM] * 7,
        out_specs=(VMEM,) * 8,
        scratch_shapes=[
            pltpu.VMEM((1, blocks), jnp.int32),
            pltpu.VMEM((blocks // LANES, LANES), jnp.int32),
            pltpu.VMEM((share, LANES), jnp.int32),
            pltpu.VMEM((size, group_count), f32),
            pltpu.VMEM((size, covs * size), f32),
            pltpu.SemaphoreType.DMA((10,)),
        ],
        compiler_params=ROOM,
        cost_estimate=cost(10_000_000, 5_000_000),
        name="select",
    )(
        *(
            pltpu.with_memory_space_constraint(x, pltpu.HBM)
            for x in (
                block_group.reshape(1, blocks),
                block_fill.reshape(blocks // LANES, LANES),
                outcome,
                fixed_coef.reshape(1, size),
                slopes,
                precision,
                design,
            )
        ),
    )

    partial = pl.pallas_call(
        predict_kernel,
        out_shape=shape(NEAR, share + slope_rows + size, LANES),
        in_specs=[VMEM] * 7,
        out_specs=VMEM,
        scratch_shapes=[pltpu.VMEM((blocks, LANES), bf16)],
        compiler_params=ROOM,
        name="predict",
    )(from_even, from_odd, own_coefs, hot, spread_hot, design_here, prior_rows)

    received = exchange(partial, ("rows", "cov"), near_groups)
    kept, sent = pl.pallas_call(
        gather_kernel,
        out_shape=(shape(share + 2 * slope_rows, LANES),) * 2,
        in_specs=[VMEM],
        out_specs=(VMEM, VMEM),
        scratch_shapes=[pltpu.VMEM((LANES, group_count), f32)],
        compiler_params=ROOM,
        name="gather",
    )(received)
    received = lax.ppermute(sent, ("rows", "cov"), first_pairs)
    kept, sent = pl.pallas_call(
        relay_kernel,
        out_shape=(shape(share + slope_rows, LANES),) * 2,
        in_specs=[VMEM] * 2,
        out_specs=(VMEM, VMEM),
        compiler_params=ROOM,
        name="relay",
    )(kept, received)
    received = lax.ppermute(sent, ("rows", "cov"), second_pairs)
    residual, prior = pl.pallas_call(
        residual_kernel,
        out_shape=(shape(share, LANES), shape(slope_rows, LANES)),
        in_specs=[VMEM] * 4,
        out_specs=(VMEM, VMEM),
        compiler_params=ROOM,
        name="residual",
    )(kept, received, label, valid)
    across = lax.ppermute(residual, ("rows", "cov"), across_pairs)
    joined = pl.pallas_call(
        join_kernel,
        out_shape=shape(2 * share, LANES),
        in_specs=[VMEM] * 2,
        out_specs=VMEM,
        compiler_params=ROOM,
        name="join",
    )(residual, across)
    beside = lax.ppermute(joined, ("rows", "cov"), beside_pairs)
    half = pl.pallas_call(
        half_kernel,
        out_shape=shape(2, share, LANES),
        in_specs=[VMEM] * 2,
        out_specs=VMEM,
        compiler_params=ROOM,
        cost_estimate=cost(10_000_000, 2_000_000),
        name="half",
    )(design_here, joined)
    fixed_parts, grads = pl.pallas_call(
        rest_kernel,
        out_shape=(shape(rows, 2, LANES), shape(blocks, LANES)),
        in_specs=[VMEM] * 3,
        out_specs=(VMEM,) * 2,
        compiler_params=ROOM,
        name="rest",
    )(design_here, beside, half)
    fixed_all = exchange(fixed_parts, "rows")

    to_even, to_odd, own = pl.pallas_call(
        group_kernel,
        out_shape=(shape(size, group_count),) * 3,
        in_specs=[VMEM] * 3,
        out_specs=(VMEM,) * 3,
        compiler_params=ROOM,
        cost_estimate=cost(100_000_000, 5_000_000),
        name="group",
    )(grads, hot, prior)
    given_even = swap(to_even, "rows", 0)
    given_odd = swap(to_odd, "rows", 1)

    fixed_grad, slope_grad = pl.pallas_call(
        finish_kernel,
        out_shape=(shape(1, size), shape(size, group_count)),
        in_specs=[VMEM] * 5,
        out_specs=(VMEM, VMEM),
        compiler_params=ROOM,
        name="finish",
    )(fixed_all, fixed_row, own, given_even, given_odd)
    return (fixed_grad.reshape(size), slope_grad)


def solution(mesh):
    return jax.shard_map(
        body,
        mesh=mesh,
        in_specs=(
            P("cov", "rows", None),
            P("rows", None),
            P("rows"),
            P("rows"),
            P("cov"),
            P("cov", "rows"),
            P("cov", None),
        ),
        out_specs=(P("cov"), P("cov", "rows")),
        check_vma=False,
    )
```

```python
import jax
import jax.numpy as jnp
from jax import lax
from jax.experimental import pallas as pl
from jax.experimental.pallas import tpu as pltpu
from jax.sharding import PartitionSpec as P

f32 = jnp.float32
bf16 = jnp.bfloat16
VMEM = pl.BlockSpec(memory_space=pltpu.VMEM)
HBM = pl.BlockSpec(memory_space=pltpu.HBM)
LANES = 128
NEAR = 4
ROOM = pltpu.CompilerParams(vmem_limit_bytes=16 << 20)


def swap(shard, axis, first):
    peers = lax.axis_size(axis)
    pairs = [(i, i + 1) for i in range(first, peers - 1, 2)]
    return lax.ppermute(shard, axis, pairs + [(j, i) for i, j in pairs])


def place_along_cov():
    shift = lax.rem(lax.axis_index("rows"), 2) * (NEAR // 2)
    covs = lax.axis_size("cov")
    return lax.rem(lax.axis_index("cov") + covs - shift, covs), shift


def far_partners(i, odd):
    a, b = i + 1 - 2 * (i % 2), 3 - i
    return a + odd * (b - a), b + odd * (a - b)


def cov_groups():
    covs, rows = lax.axis_size("cov"), lax.axis_size("rows")
    near, first, second = [], [], []
    for row in range(rows):
        members = [row * covs + (c + row % 2 * (NEAR // 2)) % covs for c in range(covs)]
        near += [members[i : i + NEAR] for i in range(0, covs, NEAR)]
        for i in (0, 2):
            for pairs, partner in zip((first, second), far_partners(i, row % 2)):
                for j in range(NEAR):
                    a, b = members[i * NEAR + j], members[partner * NEAR + j]
                    pairs += [(a, b), (b, a)]
    return near, first, second


def exchange(parts, axis, groups=None):
    return lax.all_to_all(parts, axis, 0, 0, tiled=True, axis_index_groups=groups)


def cost(flops, size):
    return pl.CostEstimate(flops=flops, bytes_accessed=size, transcendentals=0)


def three_parts(x):
    a = x.astype(bf16)
    rest = x - a.astype(f32)
    b = rest.astype(bf16)
    c = (rest - b.astype(f32)).astype(bf16)
    return jnp.concatenate([a, b, c], axis=0)


def add_parts(x):
    size = x.shape[0] // 3
    return x[:size] + x[size : 2 * size] + x[2 * size :]


def in_rows(x):
    return jnp.concatenate([x[:, at : at + LANES] for at in range(0, x.shape[1], LANES)], axis=0)


def select_kernel(
    group_hbm, fill_hbm, outcome_hbm, fixed_hbm, slopes_hbm, precision_hbm, design_hbm,
    hot_ref, label_ref, valid_ref, fixed_ref, prior_ref, coef_ref, spread_ref, design_ref,
    group_ref, fill_ref, outcome_ref, own_ref, precision_ref, sems,
):
    window, blocks = hot_ref.shape
    rows = label_ref.shape[0]
    size, groups = own_ref.shape
    place, shift = place_along_cov()
    near = lax.rem(place, NEAR)
    start = pl.multiple_of(near * rows, rows)
    copies = [
        pltpu.make_async_copy(group_hbm, group_ref, sems.at[0]),
        pltpu.make_async_copy(slopes_hbm, own_ref, sems.at[1]),
        pltpu.make_async_copy(precision_hbm, precision_ref, sems.at[2]),
        pltpu.make_async_copy(outcome_hbm.at[pl.ds(start, rows)], outcome_ref, sems.at[3]),
        pltpu.make_async_copy(fill_hbm, fill_ref, sems.at[4]),
        pltpu.make_async_copy(fixed_hbm, fixed_ref, sems.at[5]),
    ]
    quarter = size // 4
    copies += [
        pltpu.make_async_copy(
            design_hbm.at[pl.ds(i * quarter, quarter)],
            design_ref.at[pl.ds(i * quarter, quarter)],
            sems.at[6 + i],
        )
        for i in range(4)
    ]
    for copy in copies:
        copy.start()
    for copy in copies[:2]:
        copy.wait()
    index = group_ref[...] - (lax.axis_index("rows") - 1) * groups
    for piece in range(0, window, groups):
        ids = lax.broadcasted_iota(jnp.int32, (groups, blocks), 0) + piece
        hot_ref[piece : piece + groups, :] = (ids == index).astype(f32).astype(bf16)
    own = own_ref[...]
    coef_ref[...] = add_parts(
        jnp.dot(three_parts(own), hot_ref[groups : 2 * groups, :], preferred_element_type=f32)
    )
    for copy in copies[2:6]:
        copy.wait()
    across = lax.broadcasted_iota(jnp.int32, (size, size), 0)
    along = lax.broadcasted_iota(jnp.int32, (size, size), 1)
    fixed = jnp.where(across == along, jnp.broadcast_to(fixed_ref[...], (size, size)), 0.0)
    coef_ref[...] += jnp.sum(fixed, axis=1, keepdims=True)
    part = lax.broadcasted_iota(jnp.int32, (LANES, LANES), 0)
    for p in range(size):
        ones = (lax.rem(part, size) == p) & (part < 3 * size)
        spread_ref[:, p * LANES : (p + 1) * LANES] = ones.astype(f32).astype(bf16)
    slope_rows = in_rows(own)
    precision = precision_ref[...]
    columns = lax.rem(lax.broadcasted_iota(jnp.int32, (size, LANES), 1) // size, NEAR)
    for peer in range(NEAR):
        kept = [
            jnp.where(columns == lax.rem(peer + shift, NEAR), precision[:, at : at + LANES], 0.0)
            for at in range(0, precision.shape[1], LANES)
        ]
        prior_ref[peer, : slope_rows.shape[0], :] = slope_rows
        both = kept[0] + pltpu.roll(kept[1], size, 1)
        packed = both[: size // 2] + pltpu.roll(both[size // 2 :], 2 * size, 1)
        prior_ref[peer, slope_rows.shape[0] :, :] = packed
    fill = fill_ref[pl.ds(near, 1), :].astype(f32)
    column = jnp.broadcast_to(fill, (rows, rows)).T
    lane = lax.broadcasted_iota(jnp.int32, (rows, LANES), 1).astype(f32)
    valid_ref[...] = (lane < column).astype(f32)
    label_ref[...] = outcome_ref[...].astype(f32)
    for copy in copies[6:]:
        copy.wait()


def predict_kernel(
    even_ref, odd_ref, own_coef_ref, hot_ref, spread_ref, design_ref, prior_ref, out_ref, coef_ref
):
    size, groups = even_ref.shape
    blocks = hot_ref.shape[1]
    share = blocks // NEAR
    parity = lax.rem(lax.axis_index("rows"), 2)
    coefs = own_coef_ref[...]
    for ref, place in ((even_ref, 1 - parity), (odd_ref, parity)):
        piece = hot_ref[pl.ds(pl.multiple_of(place * 2 * groups, groups), groups), :]
        coefs += add_parts(jnp.dot(three_parts(ref[...]), piece, preferred_element_type=f32))
    parts = three_parts(coefs).astype(f32)
    padded = jnp.concatenate([parts, jnp.zeros((LANES - 3 * size, blocks), f32)], axis=0)
    coef_ref[...] = padded.T.astype(bf16)

    step = 2 * share

    def chunk(i, carry):
        start = pl.multiple_of(i * step, step)
        here = coef_ref[pl.ds(start, step), :]
        total = jnp.zeros((step, LANES), f32)
        for p in range(0, size, 2):
            wide = jnp.dot(
                here, spread_ref[:, p * LANES : (p + 2) * LANES], preferred_element_type=f32
            )
            total = total + wide[:, :LANES] * design_ref[p, pl.ds(start, step), :].astype(f32)
            total = total + wide[:, LANES:] * design_ref[p + 1, pl.ds(start, step), :].astype(f32)
        for k in range(2):
            out_ref[2 * i + k, :share, :] = total[k * share : (k + 1) * share]
            out_ref[2 * i + k, share:, :] = prior_ref[2 * i + k]
        return carry

    lax.fori_loop(0, NEAR // 2, chunk, 0)


def gather_kernel(parts_ref, keep_ref, send_ref, prior_ref):
    groups = prior_ref.shape[1]
    halves = groups // LANES
    size = 2 * (keep_ref.shape[0] - parts_ref.shape[1]) // (2 * halves - 1)
    rows = keep_ref.shape[0] - 2 * size * halves
    total = jnp.sum(parts_ref[:, :rows, :], axis=0)
    columns = [
        parts_ref[:, at : at + size, :].reshape(-1, LANES)
        for at in range(rows, rows + size * halves, size)
    ]
    packed = [parts_ref[n, rows + size * halves :, :] for n in range(parts_ref.shape[0])]
    unpacked = [x for y in packed for x in (y, pltpu.roll(y, LANES - 2 * size, 1))]
    prior_ref[...] = lax.dot_general(
        jnp.concatenate(unpacked, axis=0),
        jnp.concatenate(columns, axis=1),
        (((0,), (0,)), ((), ())),
        precision=lax.Precision.HIGHEST,
        preferred_element_type=f32,
    )
    place, shift = place_along_cov()
    near, group = lax.rem(place, NEAR), place // NEAR
    odd = lax.rem(lax.axis_index("rows"), 2)
    partner, _ = far_partners(group, odd)
    pieces = LANES // size
    for ref, target in ((keep_ref, group), (send_ref, partner)):
        _, beyond = far_partners(target, odd)
        ref[:rows, :] = total
        for at, member in ((rows, target), (rows + halves * size, beyond)):
            cov = lax.rem(member * NEAR + near + shift, lax.axis_size("cov"))
            piece = lax.rem(lax.rem(cov, pieces) + cov // pieces, pieces)
            part = prior_ref[pl.ds(pl.multiple_of(piece * size, size), size), :]
            ref[at : at + halves * size, :] = in_rows(part)


def relay_kernel(kept_ref, received_ref, keep_ref, send_ref):
    rows = 2 * keep_ref.shape[0] - kept_ref.shape[0]
    last = keep_ref.shape[0]
    total = kept_ref[...] + received_ref[...]
    keep_ref[...] = total[:last]
    send_ref[:rows, :] = total[:rows]
    send_ref[rows:, :] = total[last:]


def residual_kernel(kept_ref, received_ref, label_ref, valid_ref, out_ref, prior_ref):
    rows = label_ref.shape[0]
    total = kept_ref[...] + received_ref[...]
    residual = jnp.where(valid_ref[...] > 0.5, label_ref[...] - jax.nn.sigmoid(total[:rows]), 0.0)
    out_ref[...] = jnp.broadcast_to(residual[None], out_ref.shape)
    prior_ref[...] = total[rows:]


def gradient_kernel(design_ref, back_ref, fixed_ref, grad_ref):
    size, blocks, _ = design_ref.shape
    share = blocks // NEAR
    lane = lax.broadcasted_iota(jnp.int32, (share, LANES), 1)

    def chunk(peer, total):
        start = pl.multiple_of(peer * share, share)
        residual = back_ref[peer]
        grads = jnp.zeros((share, LANES), f32)
        for p in range(size):
            product = design_ref[p, pl.ds(start, share), :].astype(f32) * residual
            grads = jnp.where(lane == p, jnp.sum(product, axis=1, keepdims=True), grads)
        grad_ref[pl.ds(start, share), :] = grads
        return total + jnp.sum(grads, axis=0, keepdims=True)

    total = lax.fori_loop(0, NEAR, chunk, jnp.zeros((1, LANES), f32))
    fixed_ref[...] = jnp.broadcast_to(total[None], fixed_ref.shape)


def group_kernel(grad_ref, hot_ref, prior_ref, even_ref, odd_ref, own_ref):
    size, groups = own_ref.shape
    parts = three_parts(grad_ref[...].T[:size])
    sums = add_parts(
        lax.dot_general(parts, hot_ref[...], (((1,), (1,)), ((), ())), preferred_element_type=f32)
    )
    lower, upper = sums[:, :groups], sums[:, 2 * groups :]
    odd = lax.rem(lax.axis_index("rows"), 2) == 1
    even_ref[...] = jnp.where(odd, lower, upper)
    odd_ref[...] = jnp.where(odd, upper, lower)
    halves = [prior_ref[at : at + size, :] for at in range(0, prior_ref.shape[0], size)]
    own_ref[...] = sums[:, groups : 2 * groups] - jnp.concatenate(halves, axis=1)


def finish_kernel(fixed_all_ref, fixed_ref, own_ref, even_ref, odd_ref, fixed_out, slope_out):
    size = fixed_ref.shape[1]
    fixed_out[...] = jnp.sum(fixed_all_ref[...], axis=0)[:1, :size] - fixed_ref[...]
    slope_out[...] = own_ref[...] + even_ref[...] + odd_ref[...]


def shape(*dims, dtype=f32):
    return jax.ShapeDtypeStruct(dims, dtype)


def body(design, outcome, block_fill, block_group, fixed_coef, slopes, precision):
    size, group_count = slopes.shape
    blocks = block_group.shape[0]
    covs, rows = lax.axis_size("cov"), lax.axis_size("rows")
    share = blocks // NEAR
    near_groups, first_pairs, second_pairs = cov_groups()
    slope_rows = size * group_count // LANES

    from_even = swap(slopes, "rows", 0)
    from_odd = swap(slopes, "rows", 1)

    hot, label, valid, fixed_row, prior_rows, own_coefs, spread_hot, design_here = pl.pallas_call(
        select_kernel,
        out_shape=(
            shape(3 * group_count, blocks, dtype=bf16),
            shape(share, LANES),
            shape(share, LANES),
            shape(1, size),
            shape(NEAR, slope_rows + size // 2, LANES),
            shape(size, blocks),
            shape(LANES, size * LANES, dtype=bf16),
            shape(*design.shape, dtype=bf16),
        ),
        in_specs=[HBM] * 7,
        out_specs=(VMEM,) * 8,
        scratch_shapes=[
            pltpu.VMEM((1, blocks), jnp.int32),
            pltpu.VMEM((blocks // LANES, LANES), jnp.int32),
            pltpu.VMEM((share, LANES), jnp.int32),
            pltpu.VMEM((size, group_count), f32),
            pltpu.VMEM((size, covs * size), f32),
            pltpu.SemaphoreType.DMA((10,)),
        ],
        compiler_params=ROOM,
        cost_estimate=cost(10_000_000, 5_000_000),
        name="select",
    )(
        *(
            pltpu.with_memory_space_constraint(x, pltpu.HBM)
            for x in (
                block_group.reshape(1, blocks),
                block_fill.reshape(blocks // LANES, LANES),
                outcome,
                fixed_coef.reshape(1, size),
                slopes,
                precision,
                design,
            )
        ),
    )

    partial = pl.pallas_call(
        predict_kernel,
        out_shape=shape(NEAR, share + slope_rows + size // 2, LANES),
        in_specs=[VMEM] * 7,
        out_specs=VMEM,
        scratch_shapes=[pltpu.VMEM((blocks, LANES), bf16)],
        compiler_params=ROOM,
        name="predict",
    )(from_even, from_odd, own_coefs, hot, spread_hot, design_here, prior_rows)

    received = exchange(partial, ("rows", "cov"), near_groups)
    kept, sent = pl.pallas_call(
        gather_kernel,
        out_shape=(shape(share + 2 * slope_rows, LANES),) * 2,
        in_specs=[VMEM],
        out_specs=(VMEM, VMEM),
        scratch_shapes=[pltpu.VMEM((LANES, group_count), f32)],
        compiler_params=ROOM,
        name="gather",
    )(received)
    received = lax.ppermute(sent, ("rows", "cov"), first_pairs)
    kept, sent = pl.pallas_call(
        relay_kernel,
        out_shape=(shape(share + slope_rows, LANES),) * 2,
        in_specs=[VMEM] * 2,
        out_specs=(VMEM, VMEM),
        compiler_params=ROOM,
        name="relay",
    )(kept, received)
    received = lax.ppermute(sent, ("rows", "cov"), second_pairs)
    spread, prior = pl.pallas_call(
        residual_kernel,
        out_shape=(shape(NEAR, share, LANES), shape(slope_rows, LANES)),
        in_specs=[VMEM] * 4,
        out_specs=(VMEM, VMEM),
        compiler_params=ROOM,
        name="residual",
    )(kept, received, label, valid)
    back = exchange(spread, ("rows", "cov"), near_groups)

    fixed_parts, grads = pl.pallas_call(
        gradient_kernel,
        out_shape=(shape(rows, 2, LANES), shape(blocks, LANES)),
        in_specs=[VMEM] * 2,
        out_specs=(VMEM,) * 2,
        compiler_params=ROOM,
        name="gradient",
    )(design_here, back)
    fixed_all = exchange(fixed_parts, "rows")

    to_even, to_odd, own = pl.pallas_call(
        group_kernel,
        out_shape=(shape(size, group_count),) * 3,
        in_specs=[VMEM] * 3,
        out_specs=(VMEM,) * 3,
        compiler_params=ROOM,
        cost_estimate=cost(100_000_000, 5_000_000),
        name="group",
    )(grads, hot, prior)
    given_even = swap(to_even, "rows", 0)
    given_odd = swap(to_odd, "rows", 1)

    fixed_grad, slope_grad = pl.pallas_call(
        finish_kernel,
        out_shape=(shape(1, size), shape(size, group_count)),
        in_specs=[VMEM] * 5,
        out_specs=(VMEM, VMEM),
        compiler_params=ROOM,
        name="finish",
    )(fixed_all, fixed_row, own, given_even, given_odd)
    return (fixed_grad.reshape(size), slope_grad)


def solution(mesh):
    return jax.shard_map(
        body,
        mesh=mesh,
        in_specs=(
            P("cov", "rows", None),
            P("rows", None),
            P("rows"),
            P("rows"),
            P("cov"),
            P("cov", "rows"),
            P("cov", None),
        ),
        out_specs=(P("cov"), P("cov", "rows")),
        check_vma=False,
    )
```

```python
import jax
import jax.numpy as jnp
from jax import lax
from jax.experimental import pallas as pl
from jax.experimental.pallas import tpu as pltpu
from jax.sharding import PartitionSpec as P

f32 = jnp.float32
bf16 = jnp.bfloat16
VMEM = pl.BlockSpec(memory_space=pltpu.VMEM)
HBM = pl.BlockSpec(memory_space=pltpu.HBM)
LANES = 128
NEAR = 4
ROOM = pltpu.CompilerParams(vmem_limit_bytes=16 << 20)


def swap(shard, axis, first):
    peers = lax.axis_size(axis)
    pairs = [(i, i + 1) for i in range(first, peers - 1, 2)]
    return lax.ppermute(shard, axis, pairs + [(j, i) for i, j in pairs])


def place_along_cov():
    shift = lax.rem(lax.axis_index("rows"), 2) * (NEAR // 2)
    covs = lax.axis_size("cov")
    return lax.rem(lax.axis_index("cov") + covs - shift, covs), shift


def far_partners(i, odd):
    a, b = i + 1 - 2 * (i % 2), 3 - i
    return a + odd * (b - a), b + odd * (a - b)


def cov_groups():
    covs, rows = lax.axis_size("cov"), lax.axis_size("rows")
    near, first, second = [], [], []
    for row in range(rows):
        members = [row * covs + (c + row % 2 * (NEAR // 2)) % covs for c in range(covs)]
        near += [members[i : i + NEAR] for i in range(0, covs, NEAR)]
        for i in (0, 2):
            for pairs, partner in zip((first, second), far_partners(i, row % 2)):
                for j in range(NEAR):
                    a, b = members[i * NEAR + j], members[partner * NEAR + j]
                    pairs += [(a, b), (b, a)]
    return near, first, second


def exchange(parts, axis, groups=None):
    return lax.all_to_all(parts, axis, 0, 0, tiled=True, axis_index_groups=groups)


def cost(flops, size):
    return pl.CostEstimate(flops=flops, bytes_accessed=size, transcendentals=0)


def three_parts(x):
    a = x.astype(bf16)
    rest = x - a.astype(f32)
    b = rest.astype(bf16)
    c = (rest - b.astype(f32)).astype(bf16)
    return jnp.concatenate([a, b, c], axis=0)


def add_parts(x):
    size = x.shape[0] // 3
    return x[:size] + x[size : 2 * size] + x[2 * size :]


def in_rows(x):
    return jnp.concatenate([x[:, at : at + LANES] for at in range(0, x.shape[1], LANES)], axis=0)


def select_kernel(
    group_hbm, fill_hbm, outcome_hbm, fixed_hbm, slopes_hbm, precision_hbm, design_hbm,
    hot_ref, label_ref, valid_ref, fixed_ref, prior_ref, coef_ref, spread_ref, design_ref,
    group_ref, fill_ref, outcome_ref, own_ref, precision_ref, sems,
):
    window, blocks = hot_ref.shape
    rows = label_ref.shape[0]
    size, groups = own_ref.shape
    place, shift = place_along_cov()
    near = lax.rem(place, NEAR)
    start = pl.multiple_of(near * rows, rows)
    copies = [
        pltpu.make_async_copy(group_hbm, group_ref, sems.at[0]),
        pltpu.make_async_copy(slopes_hbm, own_ref, sems.at[1]),
        pltpu.make_async_copy(precision_hbm, precision_ref, sems.at[2]),
        pltpu.make_async_copy(outcome_hbm.at[pl.ds(start, rows)], outcome_ref, sems.at[3]),
        pltpu.make_async_copy(fill_hbm, fill_ref, sems.at[4]),
        pltpu.make_async_copy(fixed_hbm, fixed_ref, sems.at[5]),
    ]
    quarter = size // 4
    copies += [
        pltpu.make_async_copy(
            design_hbm.at[pl.ds(i * quarter, quarter)],
            design_ref.at[pl.ds(i * quarter, quarter)],
            sems.at[6 + i],
        )
        for i in range(4)
    ]
    for copy in copies:
        copy.start()
    for copy in copies[:2]:
        copy.wait()
    index = group_ref[...] - (lax.axis_index("rows") - 1) * groups
    for piece in range(0, window, groups):
        ids = lax.broadcasted_iota(jnp.int32, (groups, blocks), 0) + piece
        hot_ref[piece : piece + groups, :] = (ids == index).astype(f32).astype(bf16)
    own = own_ref[...]
    coef_ref[...] = add_parts(
        jnp.dot(three_parts(own), hot_ref[groups : 2 * groups, :], preferred_element_type=f32)
    )
    for copy in copies[2:6]:
        copy.wait()
    across = lax.broadcasted_iota(jnp.int32, (size, size), 0)
    along = lax.broadcasted_iota(jnp.int32, (size, size), 1)
    fixed = jnp.where(across == along, jnp.broadcast_to(fixed_ref[...], (size, size)), 0.0)
    coef_ref[...] += jnp.sum(fixed, axis=1, keepdims=True)
    part = lax.broadcasted_iota(jnp.int32, (LANES, LANES), 0)
    for p in range(size):
        ones = (lax.rem(part, size) == p) & (part < 3 * size)
        spread_ref[:, p * LANES : (p + 1) * LANES] = ones.astype(f32).astype(bf16)
    slope_rows = in_rows(own)
    precision = precision_ref[...]
    columns = lax.rem(lax.broadcasted_iota(jnp.int32, (size, LANES), 1) // size, NEAR)
    for peer in range(NEAR):
        kept = [
            jnp.where(columns == lax.rem(peer + shift, NEAR), precision[:, at : at + LANES], 0.0)
            for at in range(0, precision.shape[1], LANES)
        ]
        prior_ref[peer, : slope_rows.shape[0], :] = slope_rows
        both = kept[0] + pltpu.roll(kept[1], size, 1)
        packed = both[: size // 2] + pltpu.roll(both[size // 2 :], 2 * size, 1)
        prior_ref[peer, slope_rows.shape[0] :, :] = packed
    fill = fill_ref[pl.ds(near, 1), :].astype(f32)
    column = jnp.broadcast_to(fill, (rows, rows)).T
    lane = lax.broadcasted_iota(jnp.int32, (rows, LANES), 1).astype(f32)
    valid_ref[...] = (lane < column).astype(f32)
    label_ref[...] = outcome_ref[...].astype(f32)
    for copy in copies[6:]:
        copy.wait()


def predict_kernel(
    even_ref, odd_ref, own_coef_ref, hot_ref, spread_ref, design_ref, prior_ref, out_ref, coef_ref
):
    size, groups = even_ref.shape
    blocks = hot_ref.shape[1]
    share = blocks // NEAR
    parity = lax.rem(lax.axis_index("rows"), 2)
    coefs = own_coef_ref[...]
    for ref, place in ((even_ref, 1 - parity), (odd_ref, parity)):
        piece = hot_ref[pl.ds(pl.multiple_of(place * 2 * groups, groups), groups), :]
        coefs += add_parts(jnp.dot(three_parts(ref[...]), piece, preferred_element_type=f32))
    parts = three_parts(coefs).astype(f32)
    padded = jnp.concatenate([parts, jnp.zeros((LANES - 3 * size, blocks), f32)], axis=0)
    coef_ref[...] = padded.T.astype(bf16)

    step = 2 * share

    def chunk(i, carry):
        start = pl.multiple_of(i * step, step)
        here = coef_ref[pl.ds(start, step), :]
        total = jnp.zeros((step, LANES), f32)
        for p in range(0, size, 2):
            wide = jnp.dot(
                here, spread_ref[:, p * LANES : (p + 2) * LANES], preferred_element_type=f32
            )
            total = total + wide[:, :LANES] * design_ref[p, pl.ds(start, step), :].astype(f32)
            total = total + wide[:, LANES:] * design_ref[p + 1, pl.ds(start, step), :].astype(f32)
        for k in range(2):
            out_ref[2 * i + k, :share, :] = total[k * share : (k + 1) * share]
            out_ref[2 * i + k, share:, :] = prior_ref[2 * i + k]
        return carry

    lax.fori_loop(0, NEAR // 2, chunk, 0)


def gather_kernel(parts_ref, keep_ref, send_ref, prior_ref):
    groups = prior_ref.shape[1]
    halves = groups // LANES
    size = 2 * (keep_ref.shape[0] - parts_ref.shape[1]) // (2 * halves - 1)
    rows = keep_ref.shape[0] - 2 * size * halves
    total = jnp.sum(parts_ref[:, :rows, :], axis=0)
    columns = [
        parts_ref[:, at : at + size, :].reshape(-1, LANES)
        for at in range(rows, rows + size * halves, size)
    ]
    packed = [parts_ref[n, rows + size * halves :, :] for n in range(parts_ref.shape[0])]
    unpacked = [x for y in packed for x in (y, pltpu.roll(y, LANES - 2 * size, 1))]
    prior_ref[...] = lax.dot_general(
        jnp.concatenate(unpacked, axis=0),
        jnp.concatenate(columns, axis=1),
        (((0,), (0,)), ((), ())),
        precision=lax.Precision.HIGHEST,
        preferred_element_type=f32,
    )
    place, shift = place_along_cov()
    near, group = lax.rem(place, NEAR), place // NEAR
    odd = lax.rem(lax.axis_index("rows"), 2)
    partner, _ = far_partners(group, odd)
    pieces = LANES // size
    for ref, target in ((keep_ref, group), (send_ref, partner)):
        _, beyond = far_partners(target, odd)
        ref[:rows, :] = total
        for at, member in ((rows, target), (rows + halves * size, beyond)):
            cov = lax.rem(member * NEAR + near + shift, lax.axis_size("cov"))
            piece = lax.rem(lax.rem(cov, pieces) + cov // pieces, pieces)
            part = prior_ref[pl.ds(pl.multiple_of(piece * size, size), size), :]
            ref[at : at + halves * size, :] = in_rows(part)


def relay_kernel(kept_ref, received_ref, keep_ref, send_ref):
    rows = 2 * keep_ref.shape[0] - kept_ref.shape[0]
    last = keep_ref.shape[0]
    total = kept_ref[...] + received_ref[...]
    keep_ref[...] = total[:last]
    send_ref[:rows, :] = total[:rows]
    send_ref[rows:, :] = total[last:]


def residual_kernel(kept_ref, received_ref, label_ref, valid_ref, out_ref, prior_ref):
    rows = label_ref.shape[0]
    total = kept_ref[...] + received_ref[...]
    residual = jnp.where(valid_ref[...] > 0.5, label_ref[...] - jax.nn.sigmoid(total[:rows]), 0.0)
    out_ref[...] = jnp.broadcast_to(residual[None], out_ref.shape)
    prior_ref[...] = total[rows:]


def gradient_kernel(design_ref, back_ref, fixed_ref, grad_ref):
    size, blocks, _ = design_ref.shape
    share = blocks // NEAR
    lane = lax.broadcasted_iota(jnp.int32, (share, LANES), 1)

    def chunk(peer, total):
        start = pl.multiple_of(peer * share, share)
        residual = back_ref[peer]
        grads = jnp.zeros((share, LANES), f32)
        for p in range(size):
            product = design_ref[p, pl.ds(start, share), :].astype(f32) * residual
            grads = jnp.where(lane == p, jnp.sum(product, axis=1, keepdims=True), grads)
        grad_ref[pl.ds(start, share), :] = grads
        return total + jnp.sum(grads, axis=0, keepdims=True)

    total = lax.fori_loop(0, NEAR, chunk, jnp.zeros((1, LANES), f32))
    fixed_ref[...] = jnp.broadcast_to(total[None], fixed_ref.shape)


def group_kernel(grad_ref, hot_ref, prior_ref, even_ref, odd_ref, own_ref):
    size, groups = own_ref.shape
    parts = three_parts(grad_ref[...].T[:size])
    sums = add_parts(
        lax.dot_general(parts, hot_ref[...], (((1,), (1,)), ((), ())), preferred_element_type=f32)
    )
    lower, upper = sums[:, :groups], sums[:, 2 * groups :]
    odd = lax.rem(lax.axis_index("rows"), 2) == 1
    even_ref[...] = jnp.where(odd, lower, upper)
    odd_ref[...] = jnp.where(odd, upper, lower)
    halves = [prior_ref[at : at + size, :] for at in range(0, prior_ref.shape[0], size)]
    own_ref[...] = sums[:, groups : 2 * groups] - jnp.concatenate(halves, axis=1)


def slope_kernel(own_ref, even_ref, odd_ref, out_ref):
    out_ref[...] = own_ref[...] + even_ref[...] + odd_ref[...]


def finish_kernel(fixed_all_ref, fixed_ref, out_ref):
    size = fixed_ref.shape[1]
    out_ref[...] = jnp.sum(fixed_all_ref[...], axis=0)[:1, :size] - fixed_ref[...]


def shape(*dims, dtype=f32):
    return jax.ShapeDtypeStruct(dims, dtype)


def body(design, outcome, block_fill, block_group, fixed_coef, slopes, precision):
    size, group_count = slopes.shape
    blocks = block_group.shape[0]
    covs, rows = lax.axis_size("cov"), lax.axis_size("rows")
    share = blocks // NEAR
    near_groups, first_pairs, second_pairs = cov_groups()
    slope_rows = size * group_count // LANES

    from_even = swap(slopes, "rows", 0)
    from_odd = swap(slopes, "rows", 1)

    hot, label, valid, fixed_row, prior_rows, own_coefs, spread_hot, design_here = pl.pallas_call(
        select_kernel,
        out_shape=(
            shape(3 * group_count, blocks, dtype=bf16),
            shape(share, LANES),
            shape(share, LANES),
            shape(1, size),
            shape(NEAR, slope_rows + size // 2, LANES),
            shape(size, blocks),
            shape(LANES, size * LANES, dtype=bf16),
            shape(*design.shape, dtype=bf16),
        ),
        in_specs=[HBM] * 7,
        out_specs=(VMEM,) * 8,
        scratch_shapes=[
            pltpu.VMEM((1, blocks), jnp.int32),
            pltpu.VMEM((blocks // LANES, LANES), jnp.int32),
            pltpu.VMEM((share, LANES), jnp.int32),
            pltpu.VMEM((size, group_count), f32),
            pltpu.VMEM((size, covs * size), f32),
            pltpu.SemaphoreType.DMA((10,)),
        ],
        compiler_params=ROOM,
        cost_estimate=cost(10_000_000, 5_000_000),
        name="select",
    )(
        *(
            pltpu.with_memory_space_constraint(x, pltpu.HBM)
            for x in (
                block_group.reshape(1, blocks),
                block_fill.reshape(blocks // LANES, LANES),
                outcome,
                fixed_coef.reshape(1, size),
                slopes,
                precision,
                design,
            )
        ),
    )

    partial = pl.pallas_call(
        predict_kernel,
        out_shape=shape(NEAR, share + slope_rows + size // 2, LANES),
        in_specs=[VMEM] * 7,
        out_specs=VMEM,
        scratch_shapes=[pltpu.VMEM((blocks, LANES), bf16)],
        compiler_params=ROOM,
        name="predict",
    )(from_even, from_odd, own_coefs, hot, spread_hot, design_here, prior_rows)

    received = exchange(partial, ("rows", "cov"), near_groups)
    kept, sent = pl.pallas_call(
        gather_kernel,
        out_shape=(shape(share + 2 * slope_rows, LANES),) * 2,
        in_specs=[VMEM],
        out_specs=(VMEM, VMEM),
        scratch_shapes=[pltpu.VMEM((LANES, group_count), f32)],
        compiler_params=ROOM,
        name="gather",
    )(received)
    received = lax.ppermute(sent, ("rows", "cov"), first_pairs)
    kept, sent = pl.pallas_call(
        relay_kernel,
        out_shape=(shape(share + slope_rows, LANES),) * 2,
        in_specs=[VMEM] * 2,
        out_specs=(VMEM, VMEM),
        compiler_params=ROOM,
        name="relay",
    )(kept, received)
    received = lax.ppermute(sent, ("rows", "cov"), second_pairs)
    spread, prior = pl.pallas_call(
        residual_kernel,
        out_shape=(shape(NEAR, share, LANES), shape(slope_rows, LANES)),
        in_specs=[VMEM] * 4,
        out_specs=(VMEM, VMEM),
        compiler_params=ROOM,
        name="residual",
    )(kept, received, label, valid)
    back = exchange(spread, ("rows", "cov"), near_groups)

    fixed_parts, grads = pl.pallas_call(
        gradient_kernel,
        out_shape=(shape(rows, 2, LANES), shape(blocks, LANES)),
        in_specs=[VMEM] * 2,
        out_specs=(VMEM,) * 2,
        compiler_params=ROOM,
        name="gradient",
    )(design_here, back)
    fixed_all = exchange(fixed_parts, "rows")

    to_even, to_odd, own = pl.pallas_call(
        group_kernel,
        out_shape=(shape(size, group_count),) * 3,
        in_specs=[VMEM] * 3,
        out_specs=(VMEM,) * 3,
        compiler_params=ROOM,
        cost_estimate=cost(100_000_000, 5_000_000),
        name="group",
    )(grads, hot, prior)
    given_even = swap(to_even, "rows", 0)
    given_odd = swap(to_odd, "rows", 1)

    slope_grad = pl.pallas_call(
        slope_kernel,
        out_shape=shape(size, group_count),
        in_specs=[VMEM] * 3,
        out_specs=VMEM,
        compiler_params=ROOM,
        cost_estimate=cost(10_000, 100_000),
        name="slope",
    )(own, given_even, given_odd)
    fixed_grad = pl.pallas_call(
        finish_kernel,
        out_shape=shape(1, size),
        in_specs=[VMEM] * 2,
        out_specs=VMEM,
        compiler_params=ROOM,
        name="finish",
    )(fixed_all, fixed_row)
    return (fixed_grad.reshape(size), slope_grad)


def solution(mesh):
    return jax.shard_map(
        body,
        mesh=mesh,
        in_specs=(
            P("cov", "rows", None),
            P("rows", None),
            P("rows"),
            P("rows"),
            P("cov"),
            P("cov", "rows"),
            P("cov", None),
        ),
        out_specs=(P("cov"), P("cov", "rows")),
        check_vma=False,
    )
```

```python
import jax
import jax.numpy as jnp
from jax import lax
from jax.experimental import pallas as pl
from jax.experimental.pallas import tpu as pltpu
from jax.sharding import PartitionSpec as P

f32 = jnp.float32
bf16 = jnp.bfloat16
VMEM = pl.BlockSpec(memory_space=pltpu.VMEM)
HBM = pl.BlockSpec(memory_space=pltpu.HBM)
LANES = 128
NEAR = 4
ROOM = pltpu.CompilerParams(vmem_limit_bytes=16 << 20)


def swap(shard, axis, first):
    peers = lax.axis_size(axis)
    pairs = [(i, i + 1) for i in range(first, peers - 1, 2)]
    return lax.ppermute(shard, axis, pairs + [(j, i) for i, j in pairs])


def place_along_cov():
    shift = lax.rem(lax.axis_index("rows"), 2) * (NEAR // 2)
    covs = lax.axis_size("cov")
    return lax.rem(lax.axis_index("cov") + covs - shift, covs), shift


def far_partners(i, odd):
    a, b = i + 1 - 2 * (i % 2), 3 - i
    return a + odd * (b - a), b + odd * (a - b)


def cov_groups():
    covs, rows = lax.axis_size("cov"), lax.axis_size("rows")
    near, first, second = [], [], []
    for row in range(rows):
        members = [row * covs + (c + row % 2 * (NEAR // 2)) % covs for c in range(covs)]
        near += [members[i : i + NEAR] for i in range(0, covs, NEAR)]
        for i in (0, 2):
            for pairs, partner in zip((first, second), far_partners(i, row % 2)):
                for j in range(NEAR):
                    a, b = members[i * NEAR + j], members[partner * NEAR + j]
                    pairs += [(a, b), (b, a)]
    return near, first, second


def exchange(parts, axis, groups=None):
    return lax.all_to_all(parts, axis, 0, 0, tiled=True, axis_index_groups=groups)


def cost(flops, size):
    return pl.CostEstimate(flops=flops, bytes_accessed=size, transcendentals=0)


def three_parts(x):
    a = x.astype(bf16)
    rest = x - a.astype(f32)
    b = rest.astype(bf16)
    c = (rest - b.astype(f32)).astype(bf16)
    return jnp.concatenate([a, b, c], axis=0)


def add_parts(x):
    size = x.shape[0] // 3
    return x[:size] + x[size : 2 * size] + x[2 * size :]


def in_rows(x):
    return jnp.concatenate([x[:, at : at + LANES] for at in range(0, x.shape[1], LANES)], axis=0)


def select_kernel(
    group_hbm, fill_hbm, outcome_hbm, fixed_hbm, slopes_hbm, precision_hbm, design_hbm,
    hot_ref, label_ref, valid_ref, fixed_ref, prior_ref, coef_ref, spread_ref, design_ref,
    group_ref, fill_ref, outcome_ref, own_ref, precision_ref, sems,
):
    window, blocks = hot_ref.shape
    rows = label_ref.shape[0]
    size, groups = own_ref.shape
    place, shift = place_along_cov()
    near = lax.rem(place, NEAR)
    start = pl.multiple_of(near * rows, rows)
    copies = [
        pltpu.make_async_copy(group_hbm, group_ref, sems.at[0]),
        pltpu.make_async_copy(slopes_hbm, own_ref, sems.at[1]),
        pltpu.make_async_copy(precision_hbm, precision_ref, sems.at[2]),
        pltpu.make_async_copy(outcome_hbm.at[pl.ds(start, rows)], outcome_ref, sems.at[3]),
        pltpu.make_async_copy(fill_hbm, fill_ref, sems.at[4]),
        pltpu.make_async_copy(fixed_hbm, fixed_ref, sems.at[5]),
    ]
    quarter = size // 4
    copies += [
        pltpu.make_async_copy(
            design_hbm.at[pl.ds(i * quarter, quarter)],
            design_ref.at[pl.ds(i * quarter, quarter)],
            sems.at[6 + i],
        )
        for i in range(4)
    ]
    for copy in copies[6:] + copies[:6]:
        copy.start()
    for copy in copies[:2]:
        copy.wait()
    index = group_ref[...] - (lax.axis_index("rows") - 1) * groups
    for piece in range(0, window, groups):
        ids = lax.broadcasted_iota(jnp.int32, (groups, blocks), 0) + piece
        hot_ref[piece : piece + groups, :] = (ids == index).astype(f32).astype(bf16)
    own = own_ref[...]
    coef_ref[...] = add_parts(
        jnp.dot(three_parts(own), hot_ref[groups : 2 * groups, :], preferred_element_type=f32)
    )
    for copy in copies[2:6]:
        copy.wait()
    across = lax.broadcasted_iota(jnp.int32, (size, size), 0)
    along = lax.broadcasted_iota(jnp.int32, (size, size), 1)
    fixed = jnp.where(across == along, jnp.broadcast_to(fixed_ref[...], (size, size)), 0.0)
    coef_ref[...] += jnp.sum(fixed, axis=1, keepdims=True)
    part = lax.broadcasted_iota(jnp.int32, (LANES, LANES), 0)
    for p in range(size):
        ones = (lax.rem(part, size) == p) & (part < 3 * size)
        spread_ref[:, p * LANES : (p + 1) * LANES] = ones.astype(f32).astype(bf16)
    slope_rows = in_rows(own)
    precision = precision_ref[...]
    columns = lax.rem(lax.broadcasted_iota(jnp.int32, (size, LANES), 1) // size, NEAR)
    for peer in range(NEAR):
        kept = [
            jnp.where(columns == lax.rem(peer + shift, NEAR), precision[:, at : at + LANES], 0.0)
            for at in range(0, precision.shape[1], LANES)
        ]
        prior_ref[peer, : slope_rows.shape[0], :] = slope_rows
        both = kept[0] + pltpu.roll(kept[1], size, 1)
        packed = both[: size // 2] + pltpu.roll(both[size // 2 :], 2 * size, 1)
        prior_ref[peer, slope_rows.shape[0] :, :] = packed
    fill = fill_ref[pl.ds(near, 1), :].astype(f32)
    column = jnp.broadcast_to(fill, (rows, rows)).T
    lane = lax.broadcasted_iota(jnp.int32, (rows, LANES), 1).astype(f32)
    valid_ref[...] = (lane < column).astype(f32)
    label_ref[...] = outcome_ref[...].astype(f32)
    for copy in copies[6:]:
        copy.wait()


def predict_kernel(
    even_ref, odd_ref, own_coef_ref, hot_ref, spread_ref, design_ref, prior_ref, out_ref, coef_ref
):
    size, groups = even_ref.shape
    blocks = hot_ref.shape[1]
    share = blocks // NEAR
    parity = lax.rem(lax.axis_index("rows"), 2)
    coefs = own_coef_ref[...]
    for ref, place in ((even_ref, 1 - parity), (odd_ref, parity)):
        piece = hot_ref[pl.ds(pl.multiple_of(place * 2 * groups, groups), groups), :]
        coefs += add_parts(jnp.dot(three_parts(ref[...]), piece, preferred_element_type=f32))
    parts = three_parts(coefs).astype(f32)
    padded = jnp.concatenate([parts, jnp.zeros((LANES - 3 * size, blocks), f32)], axis=0)
    coef_ref[...] = padded.T.astype(bf16)

    step = 2 * share

    def chunk(i, carry):
        start = pl.multiple_of(i * step, step)
        here = coef_ref[pl.ds(start, step), :]
        total = jnp.zeros((step, LANES), f32)
        for p in range(0, size, 2):
            wide = jnp.dot(
                here, spread_ref[:, p * LANES : (p + 2) * LANES], preferred_element_type=f32
            )
            total = total + wide[:, :LANES] * design_ref[p, pl.ds(start, step), :].astype(f32)
            total = total + wide[:, LANES:] * design_ref[p + 1, pl.ds(start, step), :].astype(f32)
        for k in range(2):
            out_ref[2 * i + k, :share, :] = total[k * share : (k + 1) * share]
            out_ref[2 * i + k, share:, :] = prior_ref[2 * i + k]
        return carry

    lax.fori_loop(0, NEAR // 2, chunk, 0)


def gather_kernel(parts_ref, keep_ref, send_ref, prior_ref):
    groups = prior_ref.shape[1]
    halves = groups // LANES
    size = 2 * (keep_ref.shape[0] - parts_ref.shape[1]) // (2 * halves - 1)
    rows = keep_ref.shape[0] - 2 * size * halves
    total = jnp.sum(parts_ref[:, :rows, :], axis=0)
    columns = [
        parts_ref[:, at : at + size, :].reshape(-1, LANES)
        for at in range(rows, rows + size * halves, size)
    ]
    packed = [parts_ref[n, rows + size * halves :, :] for n in range(parts_ref.shape[0])]
    unpacked = [x for y in packed for x in (y, pltpu.roll(y, LANES - 2 * size, 1))]
    prior_ref[...] = lax.dot_general(
        jnp.concatenate(unpacked, axis=0),
        jnp.concatenate(columns, axis=1),
        (((0,), (0,)), ((), ())),
        precision=lax.Precision.HIGHEST,
        preferred_element_type=f32,
    )
    place, shift = place_along_cov()
    near, group = lax.rem(place, NEAR), place // NEAR
    odd = lax.rem(lax.axis_index("rows"), 2)
    partner, _ = far_partners(group, odd)
    pieces = LANES // size
    for ref, target in ((keep_ref, group), (send_ref, partner)):
        _, beyond = far_partners(target, odd)
        ref[:rows, :] = total
        for at, member in ((rows, target), (rows + halves * size, beyond)):
            cov = lax.rem(member * NEAR + near + shift, lax.axis_size("cov"))
            piece = lax.rem(lax.rem(cov, pieces) + cov // pieces, pieces)
            part = prior_ref[pl.ds(pl.multiple_of(piece * size, size), size), :]
            ref[at : at + halves * size, :] = in_rows(part)


def relay_kernel(kept_ref, received_ref, keep_ref, send_ref):
    rows = 2 * keep_ref.shape[0] - kept_ref.shape[0]
    last = keep_ref.shape[0]
    total = kept_ref[...] + received_ref[...]
    keep_ref[...] = total[:last]
    send_ref[:rows, :] = total[:rows]
    send_ref[rows:, :] = total[last:]


def residual_kernel(kept_ref, received_ref, label_ref, valid_ref, out_ref, prior_ref):
    rows = label_ref.shape[0]
    total = kept_ref[...] + received_ref[...]
    residual = jnp.where(valid_ref[...] > 0.5, label_ref[...] - jax.nn.sigmoid(total[:rows]), 0.0)
    out_ref[...] = jnp.broadcast_to(residual[None], out_ref.shape)
    prior_ref[...] = total[rows:]


def gradient_kernel(design_ref, back_ref, fixed_ref, grad_ref):
    size, blocks, _ = design_ref.shape
    share = blocks // NEAR
    lane = lax.broadcasted_iota(jnp.int32, (share, LANES), 1)

    def chunk(peer, total):
        start = pl.multiple_of(peer * share, share)
        residual = back_ref[peer]
        grads = jnp.zeros((share, LANES), f32)
        for p in range(size):
            product = design_ref[p, pl.ds(start, share), :].astype(f32) * residual
            grads = jnp.where(lane == p, jnp.sum(product, axis=1, keepdims=True), grads)
        grad_ref[pl.ds(start, share), :] = grads
        return total + jnp.sum(grads, axis=0, keepdims=True)

    total = lax.fori_loop(0, NEAR, chunk, jnp.zeros((1, LANES), f32))
    fixed_ref[...] = jnp.broadcast_to(total[None], fixed_ref.shape)


def group_kernel(grad_ref, hot_ref, prior_ref, even_ref, odd_ref, own_ref):
    size, groups = own_ref.shape
    parts = three_parts(grad_ref[...].T[:size])
    sums = add_parts(
        lax.dot_general(parts, hot_ref[...], (((1,), (1,)), ((), ())), preferred_element_type=f32)
    )
    lower, upper = sums[:, :groups], sums[:, 2 * groups :]
    odd = lax.rem(lax.axis_index("rows"), 2) == 1
    even_ref[...] = jnp.where(odd, lower, upper)
    odd_ref[...] = jnp.where(odd, upper, lower)
    halves = [prior_ref[at : at + size, :] for at in range(0, prior_ref.shape[0], size)]
    own_ref[...] = sums[:, groups : 2 * groups] - jnp.concatenate(halves, axis=1)


def finish_kernel(fixed_all_ref, fixed_ref, own_ref, even_ref, odd_ref, fixed_out, slope_out):
    size = fixed_ref.shape[1]
    fixed_out[...] = jnp.sum(fixed_all_ref[...], axis=0)[:1, :size] - fixed_ref[...]
    slope_out[...] = own_ref[...] + even_ref[...] + odd_ref[...]


def shape(*dims, dtype=f32):
    return jax.ShapeDtypeStruct(dims, dtype)


def body(design, outcome, block_fill, block_group, fixed_coef, slopes, precision):
    size, group_count = slopes.shape
    blocks = block_group.shape[0]
    covs, rows = lax.axis_size("cov"), lax.axis_size("rows")
    share = blocks // NEAR
    near_groups, first_pairs, second_pairs = cov_groups()
    slope_rows = size * group_count // LANES

    from_even = swap(slopes, "rows", 0)
    from_odd = swap(slopes, "rows", 1)

    hot, label, valid, fixed_row, prior_rows, own_coefs, spread_hot, design_here = pl.pallas_call(
        select_kernel,
        out_shape=(
            shape(3 * group_count, blocks, dtype=bf16),
            shape(share, LANES),
            shape(share, LANES),
            shape(1, size),
            shape(NEAR, slope_rows + size // 2, LANES),
            shape(size, blocks),
            shape(LANES, size * LANES, dtype=bf16),
            shape(*design.shape, dtype=bf16),
        ),
        in_specs=[HBM] * 7,
        out_specs=(VMEM,) * 8,
        scratch_shapes=[
            pltpu.VMEM((1, blocks), jnp.int32),
            pltpu.VMEM((blocks // LANES, LANES), jnp.int32),
            pltpu.VMEM((share, LANES), jnp.int32),
            pltpu.VMEM((size, group_count), f32),
            pltpu.VMEM((size, covs * size), f32),
            pltpu.SemaphoreType.DMA((10,)),
        ],
        compiler_params=ROOM,
        cost_estimate=cost(10_000_000, 5_000_000),
        name="select",
    )(
        *(
            pltpu.with_memory_space_constraint(x, pltpu.HBM)
            for x in (
                block_group.reshape(1, blocks),
                block_fill.reshape(blocks // LANES, LANES),
                outcome,
                fixed_coef.reshape(1, size),
                slopes,
                precision,
                design,
            )
        ),
    )

    partial = pl.pallas_call(
        predict_kernel,
        out_shape=shape(NEAR, share + slope_rows + size // 2, LANES),
        in_specs=[VMEM] * 7,
        out_specs=VMEM,
        scratch_shapes=[pltpu.VMEM((blocks, LANES), bf16)],
        compiler_params=ROOM,
        name="predict",
    )(from_even, from_odd, own_coefs, hot, spread_hot, design_here, prior_rows)

    received = exchange(partial, ("rows", "cov"), near_groups)
    kept, sent = pl.pallas_call(
        gather_kernel,
        out_shape=(shape(share + 2 * slope_rows, LANES),) * 2,
        in_specs=[VMEM],
        out_specs=(VMEM, VMEM),
        scratch_shapes=[pltpu.VMEM((LANES, group_count), f32)],
        compiler_params=ROOM,
        name="gather",
    )(received)
    received = lax.ppermute(sent, ("rows", "cov"), first_pairs)
    kept, sent = pl.pallas_call(
        relay_kernel,
        out_shape=(shape(share + slope_rows, LANES),) * 2,
        in_specs=[VMEM] * 2,
        out_specs=(VMEM, VMEM),
        compiler_params=ROOM,
        name="relay",
    )(kept, received)
    received = lax.ppermute(sent, ("rows", "cov"), second_pairs)
    spread, prior = pl.pallas_call(
        residual_kernel,
        out_shape=(shape(NEAR, share, LANES), shape(slope_rows, LANES)),
        in_specs=[VMEM] * 4,
        out_specs=(VMEM, VMEM),
        compiler_params=ROOM,
        name="residual",
    )(kept, received, label, valid)
    back = exchange(spread, ("rows", "cov"), near_groups)

    fixed_parts, grads = pl.pallas_call(
        gradient_kernel,
        out_shape=(shape(rows, 2, LANES), shape(blocks, LANES)),
        in_specs=[VMEM] * 2,
        out_specs=(VMEM,) * 2,
        compiler_params=ROOM,
        name="gradient",
    )(design_here, back)
    fixed_all = exchange(fixed_parts, "rows")

    to_even, to_odd, own = pl.pallas_call(
        group_kernel,
        out_shape=(shape(size, group_count),) * 3,
        in_specs=[VMEM] * 3,
        out_specs=(VMEM,) * 3,
        compiler_params=ROOM,
        cost_estimate=cost(100_000_000, 5_000_000),
        name="group",
    )(grads, hot, prior)
    given_even = swap(to_even, "rows", 0)
    given_odd = swap(to_odd, "rows", 1)

    fixed_grad, slope_grad = pl.pallas_call(
        finish_kernel,
        out_shape=(shape(1, size), shape(size, group_count)),
        in_specs=[VMEM] * 5,
        out_specs=(VMEM, VMEM),
        compiler_params=ROOM,
        name="finish",
    )(fixed_all, fixed_row, own, given_even, given_odd)
    return (fixed_grad.reshape(size), slope_grad)


def solution(mesh):
    return jax.shard_map(
        body,
        mesh=mesh,
        in_specs=(
            P("cov", "rows", None),
            P("rows", None),
            P("rows"),
            P("rows"),
            P("cov"),
            P("cov", "rows"),
            P("cov", None),
        ),
        out_specs=(P("cov"), P("cov", "rows")),
        check_vma=False,
    )
```
